128 devices in a mesh: gx: 8 (over z, core), gy: 16 (over y, x).
Axes of the slice: x: 4, y: 4, z: 4, core: 2. Of those that a mesh axis runs over, the one named last changes fastest.
Arguments:
- e_fields: float32 [3, 128, 256, 128], P(None, 'gx', 'gy'), may hold values from -0.6 to 0.6
- h_fields: float32 [3, 128, 256, 128], P(None, 'gx', 'gy'), may hold values from -6 to 6
- material: int32 [128, 256, 128], P('gx', 'gy'), may hold values from 0 to 7
- permittivity: float32 [8], replicated, may hold values from 1 to 10
- conductivity: float32 [8], replicated, may hold values from 0.05 to 0.5
- electrode_cells: int32 [16384], P(('gx', 'gy')), may hold values from 0 to 255
- electrode_dest: int32 [16384, 1], P(('gx', 'gy')), may hold values from 0 to 127; in each aligned block of 128 rows (0 to 127, 128 to 255, ...) at most 2 rows name the same one
- target_cells: int32 [16384], P(('gx', 'gy')), may hold values from 0 to 255
- electrode_gain: float32 [16384], P(('gx', 'gy')), may hold values from 1 to 4
Outputs:
- e_out: float32 [3, 128, 256, 128], P(None, 'gx', 'gy')
- h_out: float32 [3, 128, 256, 128], P(None, 'gx', 'gy')
The draws below stay inside these ranges and needn't reach their ends.
Inputs may be any that keep to these rules, and one draw needn't show every extreme that they name: `electrode_dest`: no tile is named by more than 2 of the 128 rows of one device, and in every draw some device names some tile exactly 2 times. `electrode_cells`: a cell of the owning tile, numbered with x slower than y. `target_cells`: a cell of the receiving tile, numbered with x slower than y.
All inputs are finite; a program needn't handle non-finite values.
Results may differ from the reference program's by a relative error of at most 0.0003.
Values sent between devices are 32-bit elements; how exact they have to be, the bound alone decides.
No kernel may reach another device: no remote copies, remote signals or barrier semaphores. Data moves between devices by JAX's collectives and lax.ppermute only.
A program may use at most 128 MiB of HBM per device.

```python
import math
import jax
import jax.numpy as jnp
import numpy as np
from jax import lax

CX = 16
CY = 16
NZ = 128
MATS = 8
EL_DEV = 128
CAP = 2
NX = 128
NY = 256
ROWS = 16384
N_GY = 16
DEVICES = 128


def draw_material(key, part):
    block_x = max(1, min(32, NX // 4))
    block_y = max(1, min(32, NY // 4))
    block_z = max(1, min(32, NZ // 4))
    count_x = -(-NX // block_x)
    count_y = -(-NY // block_y)
    count_z = -(-NZ // block_z)
    coarse = jax.random.randint(jax.random.fold_in(key, 7), (count_x, count_y, count_z), 0, MATS, dtype=jnp.int32)
    coarse = coarse.at[0, 0, 0].set(0)
    coarse = coarse.at[count_x - 1, count_y - 1, count_z - 1].set(MATS - 1)
    filled = jnp.repeat(coarse, block_x, axis=0)
    filled = jnp.repeat(filled, block_y, axis=1)
    filled = jnp.repeat(filled, block_z, axis=2)
    return filled[:NX, :NY, :NZ].astype(jnp.int32)


def touch_ends(entries, rng, low, largest):
    index_at = [jax.random.randint(jax.random.fold_in(rng, axis), (), 0, length) for axis, length in enumerate(entries.shape)]
    longest = entries.shape.index(max(entries.shape))
    next_to = index_at[:longest] + [(index_at[longest] + 1) % entries.shape[longest]] + index_at[longest + 1:]
    return entries.at[tuple(index_at)].set(low).at[tuple(next_to)].set(largest)


def steps_of(stream_key, extent, pieces, least, largest):
    factor_of = 1.0
    for dim, parts in pieces:
        steps = jax.random.uniform(jax.random.fold_in(jax.random.fold_in(stream_key, 6), dim), (parts,), jnp.float32, least / len(pieces), largest / len(pieces))
        factor_of = factor_of * jnp.repeat(jnp.exp(steps), extent[dim] // parts).reshape((-1,) + (1,) * (len(extent) - 1 - dim))
    return factor_of


def shared_out(key, own, number, rows, number_of, top, bound, skew):
    order = jax.random.permutation(key, number_of)
    crowded, ordinary = portions_of(number_of, rows * top, bound, skew, True), portions_of(number_of, rows * top, bound, skew, False)
    places = jnp.arange(number_of)

    def named(lengths, turn):
        used = int((lengths > 0).sum())
        fixed = max(1, used // 4)
        passed = fixed + (places - fixed + turn * (used - fixed)) % max(1, number_of - fixed)
        return jnp.zeros((number_of,), jnp.int32).at[order[jnp.where(places < fixed, places, passed)]].set(jnp.asarray(lengths, jnp.int32))

    lengths = jnp.where(number % 4 == 0, named(crowded, number // 4), named(ordinary, number - number // 4 - 1))
    mixed = jax.random.permutation(jax.random.fold_in(own, 3), number_of)
    donor, taker = mixed[0:number_of // 2 * 2:2], mixed[1:number_of // 2 * 2:2]
    slack = jnp.minimum(lengths[donor] - 1, bound - lengths[taker]) // 2
    slack = jnp.where((donor == order[0]) | (taker == order[0]) | (lengths[taker] == 0), 0, jnp.maximum(slack, 0))
    passed = jax.random.randint(jax.random.fold_in(own, 4), (number_of // 2,), 0, 1 << 20) % (slack + 1)
    lengths = lengths.at[donor].add(-passed).at[taker].add(passed)
    items = jnp.searchsorted(jnp.cumsum(lengths), jnp.arange(rows * top), side="right").astype(jnp.int32)
    grid = items.reshape(top, rows).T
    grid = grid[jax.random.permutation(jax.random.fold_in(own, 1), rows)]
    turn = jax.random.randint(jax.random.fold_in(own, 2), (rows, 1), 0, top)
    return jnp.take_along_axis(grid, (jnp.arange(top)[None, :] + turn) % top, axis=1)


def portions_of(amount, total, bound, slope, full):
    loads = [(1 << 20) // math.isqrt(rank ** slope) + 1 for rank in range(1, amount + 1)]
    largest = bound if full else min(bound, max(-(-total // amount), total * loads[0] // sum(loads)))
    least = 1 if total - largest >= amount - 1 else 0
    given, spare = [largest] + [least] * (amount - 1), total - largest - least * (amount - 1)
    while spare > 0:
        candidates = [i for i in range(1, amount) if given[i] < largest] or [i for i in range(1, amount) if given[i] < bound]
        pool, left = sum([loads[i] for i in candidates]), spare
        for i in candidates:
            addition = min(bound - given[i], max(1, left * loads[i] // pool), spare)
            given[i] = given[i] + addition
            spare = spare - addition
    return np.array(given)


def gaussian(key, dims, scale, bound, shards=(), kind=jnp.bfloat16):
    result = jax.random.normal(key, dims, jnp.float32) * scale
    if len(shards) > 0:
        result = steps_of(key, dims, shards, -0.22, 0.18) * result
    return jnp.clip(result, min=-bound, max=bound).astype(kind)


def setup_inputs(seed: int = 0) -> dict:
    key_list = jax.random.split(jax.random.key(seed), 10)
    e_fields = gaussian(key_list[0], (3, NX, NY, NZ), 0.1, 0.6, ((1, 8), (2, 16)), jnp.float32)
    h_fields = gaussian(key_list[1], (3, NX, NY, NZ), 1.0, 6.0, ((1, 8), (2, 16)), jnp.float32)
    material = draw_material(jax.random.fold_in(key_list[9], 71), 0)
    permittivity = jnp.clip(jnp.exp(jax.random.uniform(key_list[3], (MATS,), jnp.float32, math.log(1.0), math.log(10.0))), 1.0, 10.0)
    conductivity = jnp.clip(jnp.exp(jax.random.uniform(key_list[4], (MATS,), jnp.float32, math.log(0.05), math.log(0.5))), 0.05, 0.5)
    electrode_cells = touch_ends(jax.random.randint(key_list[5], (ROWS,), 0, CX * CY), jax.random.fold_in(key_list[5], 1), 0, (CX * CY) - 1).astype(jnp.int32)
    electrode_dest_keys = jax.random.split(jax.random.fold_in(key_list[6], 1), ROWS // EL_DEV)
    electrode_dest_turns = jax.random.permutation(jax.random.fold_in(key_list[6], 3), ROWS // EL_DEV)
    electrode_dest = jax.vmap(lambda own, number: shared_out(jax.random.fold_in(key_list[6], 2), own, number, EL_DEV, DEVICES, 1, CAP, 2))(electrode_dest_keys, electrode_dest_turns).reshape((ROWS, 1))
    target_cells = touch_ends(jax.random.randint(key_list[7], (ROWS,), 0, CX * CY), jax.random.fold_in(key_list[7], 1), 0, (CX * CY) - 1).astype(jnp.int32)
    electrode_gain = jnp.clip(jnp.exp(math.log(4.0) - 1.3862944 * jax.random.uniform(key_list[8], (ROWS,), jnp.float32) ** steps_of(key_list[8], (ROWS,), ((0, 128),), -0.2, 0.2)), 1.0, 4.0)
    return dict(e_fields=e_fields, h_fields=h_fields, material=material, permittivity=permittivity, conductivity=conductivity, electrode_cells=electrode_cells, electrode_dest=electrode_dest, target_cells=target_cells, electrode_gain=electrode_gain)


half_step = 16.0
line_factor = 256.0

def plus_z(field):
    tail = jnp.zeros_like(field[..., :1])
    return jnp.concatenate([field[..., 1:], tail], axis=-1) - field

def minus_z(field):
    head = jnp.zeros_like(field[..., :1])
    return field - jnp.concatenate([head, field[..., :-1]], axis=-1)

def minus_x(padded):
    return padded[1:-1, 1:-1] - padded[:-2, 1:-1]

def plus_x(padded):
    return padded[2:, 1:-1] - padded[1:-1, 1:-1]

def minus_y(padded):
    return padded[1:-1, 1:-1] - padded[1:-1, :-2]

def plus_y(padded):
    return padded[1:-1, 2:] - padded[1:-1, 1:-1]

def cross_yx(padded):
    forward = padded[2:] - padded[1:-1]
    return forward[:, 1:-1] - forward[:, :-2]

def cross_xy(padded):
    forward = padded[:, 2:] - padded[:, 1:-1]
    return forward[1:-1] - forward[:-2]

def pad_plane(field):
    return jnp.pad(field, ((1, 1), (1, 1), (0, 0)))

def coefficients(material, permittivity, conductivity):
    eps_cell = jnp.zeros(material.shape, permittivity.dtype)
    sigma_cell = jnp.zeros(material.shape, permittivity.dtype)
    for index in range(permittivity.shape[0]):
        chosen = material == index
        eps_cell = eps_cell + jnp.where(chosen, permittivity[index], 0.0)
        sigma_cell = sigma_cell + jnp.where(chosen, conductivity[index], 0.0)
    loss = sigma_cell * half_step / (2.0 * eps_cell)
    keep_rate = (1.0 - loss) / (1.0 + loss)
    drive_rate = half_step / (eps_cell * (1.0 + loss))
    return (keep_rate, drive_rate, drive_rate * line_factor)

def line_solve(coupling, right_side, axis):
    moved = jnp.moveaxis(coupling, axis, -1)
    target = jnp.moveaxis(right_side, axis, -1)
    sub_diag = (-moved).at[..., 0].set(0.0)
    super_diag = (-moved).at[..., -1].set(0.0)
    main_diag = 1.0 + 2.0 * moved
    solved = lax.linalg.tridiagonal_solve(sub_diag, main_diag, super_diag, target[..., None])[..., 0]
    return jnp.moveaxis(solved, -1, axis)

def electrode_field(ez_now, electrode_cells, electrode_dest, target_cells, electrode_gain):
    row_total = electrode_cells.shape[0]
    owner_dev = jnp.arange(row_total, dtype=jnp.int32) // EL_DEV
    source_x = owner_dev // N_GY * CX + electrode_cells // CY
    source_y = owner_dev % N_GY * CY + electrode_cells % CY
    current = ez_now[source_x, source_y, :] * electrode_gain[:, None]
    target = electrode_dest[:, 0]
    dest_x = target // N_GY * CX + target_cells // CY
    dest_y = target % N_GY * CY + target_cells % CY
    return jnp.zeros_like(ez_now).at[dest_x, dest_y].add(current)

def reference(e_fields, h_fields, material, permittivity, conductivity, electrode_cells, electrode_dest, target_cells, electrode_gain):
    keep_rate, drive_rate, coupling = coefficients(material, permittivity, conductivity)
    ex_now, ey_now, ez_now = (e_fields[0], e_fields[1], e_fields[2])
    hx_now, hy_now, hz_now = (h_fields[0], h_fields[1], h_fields[2])
    injected = electrode_field(ez_now, electrode_cells, electrode_dest, target_cells, electrode_gain)
    ex_pad, ey_pad, ez_pad = (pad_plane(ex_now), pad_plane(ey_now), pad_plane(ez_now))
    hx_pad, hy_pad, hz_pad = (pad_plane(hx_now), pad_plane(hy_now), pad_plane(hz_now))
    rhs_ex = keep_rate * ex_now + drive_rate * (minus_y(hz_pad) - minus_z(hy_now) - half_step * cross_yx(ey_pad))
    rhs_ey = keep_rate * ey_now + drive_rate * (minus_z(hx_now) - minus_x(hz_pad) - half_step * minus_z(plus_y(ez_pad)))
    rhs_ez = keep_rate * ez_now + drive_rate * (minus_x(hy_pad) - minus_y(hx_pad) - half_step * minus_x(plus_z(ex_pad)) - injected)
    ex_half = line_solve(coupling, rhs_ex, 1)
    ey_half = line_solve(coupling, rhs_ey, 2)
    ez_half = line_solve(coupling, rhs_ez, 0)
    exh_pad, eyh_pad, ezh_pad = (pad_plane(ex_half), pad_plane(ey_half), pad_plane(ez_half))
    hx_half = hx_now + half_step * (plus_z(ey_half) - plus_y(ez_pad))
    hy_half = hy_now + half_step * (plus_x(ezh_pad) - plus_z(ex_now))
    hz_half = hz_now + half_step * (plus_y(exh_pad) - plus_x(ey_pad))
    hxh_pad, hyh_pad, hzh_pad = (pad_plane(hx_half), pad_plane(hy_half), pad_plane(hz_half))
    rhs_ex = keep_rate * ex_half + drive_rate * (minus_y(hzh_pad) - minus_z(hy_half) - half_step * minus_z(plus_x(ezh_pad)))
    rhs_ey = keep_rate * ey_half + drive_rate * (minus_z(hx_half) - minus_x(hzh_pad) - half_step * cross_xy(exh_pad))
    rhs_ez = keep_rate * ez_half + drive_rate * (minus_x(hyh_pad) - minus_y(hxh_pad) - half_step * minus_y(plus_z(eyh_pad)) - injected)
    ex_new = line_solve(coupling, rhs_ex, 2)
    ey_new = line_solve(coupling, rhs_ey, 0)
    ez_new = line_solve(coupling, rhs_ez, 1)
    eyn_pad, ezn_pad = (pad_plane(ey_new), pad_plane(ez_new))
    hx_new = hx_half + half_step * (plus_z(ey_half) - plus_y(ezn_pad))
    hy_new = hy_half + half_step * (plus_x(ezh_pad) - plus_z(ex_new))
    hz_new = hz_half + half_step * (plus_y(exh_pad) - plus_x(eyn_pad))
    return (jnp.stack([ex_new, ey_new, ez_new]), jnp.stack([hx_new, hy_new, hz_new]))
```

```python
import jax
import jax.numpy as jnp
from jax import lax
from jax.experimental import pallas as pl
from jax.experimental.pallas import tpu as pltpu
from jax.sharding import PartitionSpec as P

F32 = jnp.float32
BF16 = jnp.bfloat16
CX = 16
CY = 16
NZ = 128
CELLS = CX * CY
GX = 8
GY = 16
HS = 16.0
INV = 1.0 / 256.0

R1_VAL, R1_HALO, R1_G11, R1_G1N, R1_GNN, R1_CODE, R1 = 0, 32, 48, 64, 80, 96, 104
R2_VAL, R2_CODE, R2_HA, R2_HB, R2_P1, R2_P2, R2_G11, R2_G1N, R2_GNN, R2 = (
    0, 16, 24, 40, 56, 72, 88, 104, 120, 136)
R3_Z, R3_Y, R3_T, R3 = 0, 16, 32, 48
R4 = 16


def iota(shape, dim):
    return lax.broadcasted_iota(jnp.int32, shape, dim)


def z_up(f):
    return jnp.where(iota(f.shape, 1) == NZ - 1, 0.0, pltpu.roll(f, NZ - 1, 1))


def z_down(f):
    return jnp.where(iota(f.shape, 1) == 0, 0.0, pltpu.roll(f, 1, 1))


def y_up(f, last):
    return jnp.where(iota(f.shape, 0) == CY - 1, last, pltpu.roll(f, CY - 1, 0))


def y_down(f, first):
    return jnp.where(iota(f.shape, 0) == 0, first, pltpu.roll(f, 1, 0))


def rows(x):
    return pl.ds(x * CY, CY)


def strided(y):
    return pl.ds(y, CX, stride=CY)


def z_solve(w, d):
    lane = iota(w.shape, 1)
    a = jnp.where(lane == 0, 0.0, 1.0)
    c = jnp.where(lane == NZ - 1, 0.0, 1.0)
    e = w + (2.0 - a - c)
    step = 1
    while step < NZ:
        rb = 1.0 / (e + a + c)
        eb = e * rb
        db = d * rb
        e = e + a * pltpu.roll(eb, step, 1) + c * pltpu.roll(eb, NZ - step, 1)
        d = d + a * pltpu.roll(db, step, 1) + c * pltpu.roll(db, NZ - step, 1)
        if 2 * step < NZ:
            a, c = a * pltpu.roll(a * rb, step, 1), c * pltpu.roll(c * rb, NZ - step, 1)
        step *= 2
    return d / e


def pivots(ws):
    def sweep(seq):
        s, l = seq[0], None
        rf = 1.0 / (1.0 + 1.0 + s)
        out = [rf]
        l = rf
        for w in seq[1:]:
            s = w + s * rf
            rf = 1.0 / (1.0 + l + s)
            out.append(rf)
            l = l * rf
        return out, l
    fwd, link = sweep(ws)
    bwd, _ = sweep(ws[::-1])
    return fwd, bwd[::-1], link


def ends(ds, fwd, bwd):
    y = ds[0]
    b = ds[-1]
    n = len(ds)
    for k in range(1, n):
        y = ds[k] + fwd[k - 1] * y
        b = ds[n - 1 - k] + bwd[n - k] * b
    return b * bwd[0], y * fwd[n - 1]


def block_solve(ds, fwd, left, right):
    ys = [ds[0] + left]
    for k in range(1, len(ds)):
        ys.append(ds[k] + fwd[k - 1] * ys[-1])
    u = (ys[-1] + right) * fwd[-1]
    us = [u]
    for k in range(len(ds) - 2, -1, -1):
        u = (ys[k] + u) * fwd[k]
        us.append(u)
    return us[::-1]


def static_fold(n, g11, g1n, gnn, h_ref, hr_ref, be_ref, de_ref):
    zero = jnp.zeros((16, NZ), F32)
    be = zero
    de = zero
    be_ref[0] = be
    de_ref[n] = de
    for k in range(n):
        a1, a2, a3 = g11(k), g1n(k), gnn(k)
        h = a2 / (1.0 - a1 * be)
        be = a3 + a2 * h * be
        h_ref[k] = h
        be_ref[k + 1] = be
        j = n - 1 - k
        b1, b2, b3 = g11(j), g1n(j), gnn(j)
        hr = b2 / (1.0 - b3 * de)
        de = b1 + b2 * hr * de
        hr_ref[j] = hr
        de_ref[j] = de


def interface(n, me, own_m, own_n, recv, h_ref, hr_ref, be_ref, de_ref):
    al = jnp.zeros((16, NZ), F32)
    ga = jnp.zeros((16, NZ), F32)
    for k in range(n - 1):
        al = jnp.where(k < me, recv(k) + h_ref[k] * al, al)
        j = n - 1 - k
        ga = jnp.where(j > me, recv(j) + hr_ref[j] * ga, ga)
    be, be1 = be_ref[me], be_ref[me + 1]
    de, de1 = de_ref[me], de_ref[me + 1]
    own_ga = own_n + hr_ref[me] * ga
    own_al = own_m + h_ref[me] * al
    left = (al + be * own_ga) / (1.0 - be * de)
    right = (ga + de1 * own_al) / (1.0 - be1 * de1)
    return left, right


def to_messages(me, p1, p2, h_ref, hr_ref, be_ref, de_ref):
    m = p2 + h_ref[me] * be_ref[me] * p1
    n = p1 + hr_ref[me] * de_ref[me + 1] * p2
    return m, n


def split_dot(sel, values):
    hi = values.astype(BF16)
    rest = values - hi.astype(F32)
    mid = rest.astype(BF16)
    low = (rest - mid.astype(F32)).astype(BF16)
    dims = (((1,), (0,)), ((), ()))

    def part(v):
        return lax.dot_general(sel, v, dims, preferred_element_type=F32)

    return part(hi) + part(mid) + part(low)


def k1(e, h, mat, perm, cond, cells, dest, tgt, gain, msg, w_o, v_o, fx_o, bx_o):
    me = lax.axis_index("gx")
    ws = [(perm[k] + 8.0 * cond[k]) * (1.0 / 4096.0) for k in range(8)]
    vs = [(perm[k] - 8.0 * cond[k]) * (1.0 / 4096.0) for k in range(8)]

    def pick(table, bits):
        for bit in bits:
            table = [jnp.where(bit, table[2 * k + 1], table[2 * k]) for k in range(len(table) // 2)]
        return table[0]

    wx = []
    for x in range(CX):
        m = mat[rows(x), :]
        bits = [(m & 1) != 0, (m & 2) != 0, (m & 4) != 0]
        w = pick(ws, bits)
        w_o[rows(x), :] = w
        v_o[rows(x), :] = pick(vs, bits)
        wx.append(w)
    fwd, bwd, link = pivots(wx)
    for x in range(CX):
        fx_o[x] = fwd[x]
        bx_o[x] = bwd[x]
    to = dest[...]
    to_b = jnp.broadcast_to(to, (128, 128))
    same = (to_b.T == to_b) & (iota((128, 128), 0) < iota((128, 128), 1))
    rank = jnp.sum(same.astype(jnp.int32), axis=0, keepdims=True)
    lane_slot = rank * GY + (to & (GY - 1))
    dest_x = to >> 4
    hot = iota((CELLS, 128), 0) == dest_x * 32 + lane_slot
    slot_gain = jnp.sum(jnp.where(hot, gain[...], 0.0), axis=1, keepdims=True)
    from_cell = (iota((CELLS, 128), 0) == cells[...]).astype(BF16)
    nt = (((1,), (1,)), ((), ()))
    pickm = lax.dot_general(hot.astype(BF16), from_cell, nt, preferred_element_type=F32)
    vals = split_dot(pickm.astype(BF16), e[2]) * slot_gain
    code_at = jnp.where(iota((8, 128), 0) == dest_x, (tgt[...] + 1).astype(F32), 0.0).astype(BF16)
    lane_hot = (iota((128, 128), 0) == lane_slot).astype(BF16)
    code = lax.dot_general(code_at, lane_hot, nt, preferred_element_type=F32)
    hz_last = h[2, rows(CX - 1), :]
    ey_first = e[1, rows(0), :]
    for d in range(GX):
        msg[d, 0:32, :] = vals[d * 32:(d + 1) * 32]
        msg[d, R1_HALO:R1_HALO + 16, :] = jnp.where(d > me, hz_last, ey_first)
        msg[d, R1_G11:R1_G11 + 16, :] = bwd[0]
        msg[d, R1_G1N:R1_G1N + 16, :] = link
        msg[d, R1_GNN:R1_GNN + 16, :] = fwd[CX - 1]
        msg[d, R1_CODE:R1_CODE + 8, :] = jnp.broadcast_to(code[d:d + 1], (8, NZ))


def k1b(w, fy_o, by_o, g_o):
    ws = [w[strided(y), :] for y in range(CY)]
    fwd, bwd, link = pivots(ws)
    for y in range(CY):
        fy_o[y] = fwd[y]
        by_o[y] = bwd[y]
    g_o[0] = bwd[0]
    g_o[1] = link
    g_o[2] = fwd[CY - 1]


def k2(m1, e, h, w, v, fy, by, g, msg, hzp_o, dx_o, halo_o):
    gx = lax.axis_index("gx")
    me = lax.axis_index("gy")
    lo = jnp.maximum(gx - 1, 0) * R1 + R1_HALO
    hi = jnp.minimum(gx + 1, GX - 1) * R1 + R1_HALO
    hz_low = jnp.where(gx > 0, m1[pl.ds(lo, 16), :], 0.0)
    ey_high = jnp.where(gx < GX - 1, m1[pl.ds(hi, 16), :], 0.0)
    halo_o[...] = hz_low
    for x in range(CX):
        ey = e[1, rows(x), :]
        ey_next = e[1, rows(x + 1), :] if x < CX - 1 else ey_high
        hzp = h[2, rows(x), :] - HS * (ey_next - ey)
        hzp_o[rows(x), :] = hzp
        hy = h[1, rows(x), :]
        curl = (hzp - y_down(hzp, 0.0)) - (hy - z_down(hy))
        dx_o[rows(x), :] = v[rows(x), :] * e[0, rows(x), :] + INV * curl
    bwd = [by[y] for y in range(CY)]
    fwd = [fy[y] for y in range(CY)]
    p1, p2 = ends([dx_o[strided(y), :] for y in range(CY)], fwd, bwd)
    t = -INV * hzp_o[strided(CY - 1), :]
    p2 = p2 + t
    ez_first = e[2, strided(0), :]
    hx_last = h[0, strided(CY - 1), :]
    code = m1[pl.ds(R1_CODE, 8, stride=R1), :]
    for d in range(GY):
        for r in range(2):
            msg[d, r * 8:r * 8 + 8, :] = m1[pl.ds(r * GY + d, 8, stride=R1), :]
        msg[d, R2_CODE:R2_CODE + 8, :] = code
        msg[d, R2_HA:R2_HA + 16, :] = jnp.where(d > me, hx_last, ez_first)
        msg[d, R2_HB:R2_HB + 16, :] = t
        msg[d, R2_P1:R2_P1 + 16, :] = p1
        msg[d, R2_P2:R2_P2 + 16, :] = p2
        msg[d, R2_G11:R2_G11 + 16, :] = g[0]
        msg[d, R2_G1N:R2_G1N + 16, :] = g[1]
        msg[d, R2_GNN:R2_GNN + 16, :] = g[2]


def k2b(m1, h_o, hr_o, be_o, de_o):
    static_fold(
        GX,
        lambda j: m1[pl.ds(j * R1 + R1_G11, 16), :],
        lambda j: m1[pl.ds(j * R1 + R1_G1N, 16), :],
        lambda j: m1[pl.ds(j * R1 + R1_GNN, 16), :],
        h_o, hr_o, be_o, de_o)


def k3(m2, e, h, w, v, hzp, dx, hz_low, fy, fx, bx, hx_c, hrx_c, bex, dex,
       msg, hy_c, hry_c, bey, dey, ex1_o, hz1_o, hz1m_o, inj_o, hyp_o, hxpp_o, hzpp_o,
       dz_o, dy2_o, own_o, hxp_s, ey1_s, dy1_s):
    gx = lax.axis_index("gx")
    me = lax.axis_index("gy")
    static_fold(GY, lambda j: m2[j, R2_G11:R2_G11 + 16, :], lambda j: m2[j, R2_G1N:R2_G1N + 16, :],
                lambda j: m2[j, R2_GNN:R2_GNN + 16, :], hy_c, hry_c, bey, dey)
    p1 = m2[me, R2_P1:R2_P1 + 16, :]
    p2 = m2[me, R2_P2:R2_P2 + 16, :]
    own_m, own_n = to_messages(me, p1, p2, hy_c, hry_c, bey, dey)

    def recv(j):
        q1 = m2[j, R2_P1:R2_P1 + 16, :]
        q2 = m2[j, R2_P2:R2_P2 + 16, :]
        return jnp.where(j < me, q2 + hy_c[j] * bey[j] * q1, q1 + hry_c[j] * dey[j + 1] * q2)

    left, right = interface(GY, me, own_m, own_n, recv, hy_c, hry_c, bey, dey)
    us = block_solve([dx[strided(y), :] for y in range(CY)], [fy[y] for y in range(CY)], left, right)
    for y in range(CY):
        ex1_o[strided(y), :] = us[y]
    below = jnp.maximum(me - 1, 0)
    above = jnp.minimum(me + 1, GY - 1)
    t = m2[below, R2_HB:R2_HB + 16, :]
    hz1m_o[...] = jnp.where(me > 0, HS * (us[0] - left) - 240.0 * t, 0.0)
    hx_low = jnp.where(me > 0, m2[below, R2_HA:R2_HA + 16, :], 0.0)
    ez_high = jnp.where(me < GY - 1, m2[above, R2_HA:R2_HA + 16, :], 0.0)
    codes = jnp.concatenate([m2[j, R2_CODE:R2_CODE + 8, :] for j in range(GY)], axis=0).astype(BF16)
    inj = None
    for r in range(2):
        lane = (iota((8, 128), 1) == r * GY + me).astype(BF16)
        code_row = lax.dot_general(lane, codes, (((1,), (1,)), ((), ())), preferred_element_type=F32)[0:1]
        land = ((iota((CELLS, 128), 0) + 1).astype(F32) == code_row).astype(BF16)
        vals = jnp.concatenate([m2[j, r * 8:r * 8 + 8, :] for j in range(GY)], axis=0)
        part = split_dot(land, vals)
        inj = part if inj is None else inj + part
    inj_o[...] = inj
    prev_hyp = None
    for x in range(CX):
        ez = e[2, rows(x), :]
        hx = h[0, rows(x), :]
        ex = e[0, rows(x), :]
        hz = h[2, rows(x), :]
        hxp = hx - HS * (y_up(ez, ez_high[x:x + 1]) - ez)
        hxp_s[rows(x), :] = hxp
        hyp = h[1, rows(x), :] - HS * (z_up(ex) - ex)
        hyp_o[rows(x), :] = hyp
        curl = hyp - (hx - y_down(hx, hx_low[x:x + 1])) - inj_o[rows(x), :]
        if x > 0:
            curl = curl - prev_hyp
        prev_hyp = hyp
        dz_o[rows(x), :] = v[rows(x), :] * ez + INV * curl
        hz_prev = h[2, rows(x - 1), :] if x > 0 else hz_low[...]
        curl = (hxp - z_down(hxp)) - (hz - hz_prev)
        dy1_s[rows(x), :] = v[rows(x), :] * e[1, rows(x), :] + INV * curl
    for q in range(4):
        part = pl.ds(q * 64, 64)
        ey1_s[part, :] = z_solve(w[part, :], dy1_s[part, :])
    prev = None
    for x in range(CX):
        ey1 = ey1_s[rows(x), :]
        dey1 = HS * (z_up(ey1) - ey1)
        hx1 = hxp_s[rows(x), :] + dey1
        hxpp_o[rows(x), :] = hx1 + dey1
        ex1 = ex1_o[rows(x), :]
        dex1 = HS * (y_up(ex1, right[x:x + 1]) - ex1)
        hz1 = hzp[rows(x), :] + dex1
        hz1_o[rows(x), :] = hz1
        hzpp = hz1 + dex1
        hzpp_o[rows(x), :] = hzpp
        curl = (hx1 - z_down(hx1)) - hzpp
        if x > 0:
            curl = curl + prev
        prev = hzpp
        dy2_o[rows(x), :] = v[rows(x), :] * ey1 + INV * curl
    fwd = [fx[x] for x in range(CX)]
    bwd = [bx[x] for x in range(CX)]
    tz = -INV * hyp_o[rows(CX - 1), :]
    p1, p2 = ends([dz_o[rows(x), :] for x in range(CX)], fwd, bwd)
    mz, nz = to_messages(gx, p1, p2 + tz, hx_c, hrx_c, bex, dex)
    ty = INV * hzpp_o[rows(CX - 1), :]
    p1, p2 = ends([dy2_o[rows(x), :] for x in range(CX)], fwd, bwd)
    my, ny = to_messages(gx, p1, p2 + ty, hx_c, hrx_c, bex, dex)
    own_o[0], own_o[1], own_o[2], own_o[3] = mz, nz, my, ny
    for d in range(GX):
        msg[d, 0:16, :] = jnp.where(d > gx, mz, nz)
        msg[d, 16:32, :] = jnp.where(d > gx, my, ny)
        msg[d, 32:48, :] = tz


def k4(m3, own, v, w, dz, fx, fy, by, hyp, hxpp, inj, hx_c, hrx_c, bex, dex, hy_c, hry_c, bey, dey,
       msg, dz2_o, hypp_o, own_o):
    gx = lax.axis_index("gx")
    me = lax.axis_index("gy")
    left, right = interface(GX, gx, own[0], own[1], lambda j: m3[j, 0:16, :], hx_c, hrx_c, bex, dex)
    us = block_solve([dz[rows(x), :] for x in range(CX)], [fx[x] for x in range(CX)], left, right)
    t = m3[jnp.maximum(gx - 1, 0), 32:48, :]
    prev = jnp.where(gx > 0, HS * (us[0] - left) - 240.0 * t, 0.0)
    for x in range(CX):
        dez = HS * ((us[x + 1] if x < CX - 1 else right) - us[x])
        hy1 = hyp[rows(x), :] + dez
        hypp_o[rows(x), :] = hy1 + dez
        hx2 = hxpp[rows(x), :]
        curl = (hy1 - prev) - (hx2 - y_down(hx2, 0.0)) - inj[rows(x), :]
        prev = hy1
        dz2_o[rows(x), :] = v[rows(x), :] * us[x] + INV * curl
    p1, p2 = ends([dz2_o[strided(y), :] for y in range(CY)], [fy[y] for y in range(CY)], [by[y] for y in range(CY)])
    p2 = p2 + INV * hxpp[strided(CY - 1), :]
    m, n = to_messages(me, p1, p2, hy_c, hry_c, bey, dey)
    own_o[0], own_o[1] = m, n
    for d in range(GY):
        msg[d] = jnp.where(d > me, m, n)


def k4b(m3, own, v, w, fx, ex1, hz1, hz1m, hypp, hzpp, dy2, hx_c, hrx_c, bex, dex,
        ex2_o, ey2_o, hy2_o, hz2_o, dx2_s):
    gx = lax.axis_index("gx")
    left, right = interface(GX, gx, own[2], own[3], lambda j: m3[j, 16:32, :], hx_c, hrx_c, bex, dex)
    us = block_solve([dy2[rows(x), :] for x in range(CX)], [fx[x] for x in range(CX)], left, right)
    for x in range(CX):
        ey2_o[rows(x), :] = us[x]
        hz2_o[rows(x), :] = hzpp[rows(x), :] - HS * ((us[x + 1] if x < CX - 1 else right) - us[x])
        hz = hz1[rows(x), :]
        hy = hypp[rows(x), :]
        curl = (hz - y_down(hz, hz1m[x:x + 1, :])) - (hy - z_down(hy))
        dx2_s[rows(x), :] = v[rows(x), :] * ex1[rows(x), :] + INV * curl
    for q in range(4):
        part = pl.ds(q * 64, 64)
        ex2 = z_solve(w[part, :], dx2_s[part, :])
        ex2_o[part, :] = ex2
        hy2_o[part, :] = hypp[part, :] - HS * (z_up(ex2) - ex2)


def k5(m4, own, dz2, fy, hxpp, ex2, ey2, hy2, hz2, hy_c, hry_c, bey, dey, e_o, h_o):
    me = lax.axis_index("gy")
    left, right = interface(GY, me, own[0], own[1], lambda j: m4[j], hy_c, hry_c, bey, dey)
    us = block_solve([dz2[strided(y), :] for y in range(CY)], [fy[y] for y in range(CY)], left, right)
    for y in range(CY):
        e_o[2, strided(y), :] = us[y]
    e_o[0] = ex2[...]
    e_o[1] = ey2[...]
    h_o[1] = hy2[...]
    h_o[2] = hz2[...]
    for x in range(CX):
        ez2 = e_o[2, rows(x), :]
        h_o[0, rows(x), :] = hxpp[rows(x), :] - HS * (y_up(ez2, right[x:x + 1]) - ez2)


def call(kernel, shapes, args, scratch=(), smem=()):
    specs = [
        pl.BlockSpec(memory_space=pltpu.SMEM if k in smem else pltpu.VMEM) for k in range(len(args))
    ]
    return pl.pallas_call(
        kernel,
        out_shape=[jax.ShapeDtypeStruct(s, F32) for s in shapes],
        in_specs=specs,
        out_specs=[pl.BlockSpec(memory_space=pltpu.VMEM) for _ in shapes],
        scratch_shapes=[pltpu.VMEM(s, F32) for s in scratch],
        name=kernel.__name__,
    )(*args)


def exchange(message, axis):
    return lax.all_to_all(message, axis, split_axis=0, concat_axis=0, tiled=True)


FIELD = (CELLS, NZ)
FACE = (16, NZ)
LINE = (16, 16, NZ)


def body(e_fields, h_fields, material, permittivity, conductivity, electrode_cells, electrode_dest,
         target_cells, electrode_gain):
    e = e_fields.reshape(3, CELLS, NZ)
    h = h_fields.reshape(3, CELLS, NZ)
    mat = material.reshape(CELLS, NZ)
    msg1, w, v, fx, bx = call(
        k1, [(GX, R1, NZ), FIELD, FIELD, LINE, LINE],
        (e, h, mat, permittivity, conductivity, electrode_cells.reshape(1, 128),
         electrode_dest.reshape(1, 128), target_cells.reshape(1, 128), electrode_gain.reshape(1, 128)),
        smem=(3, 4))
    m1 = exchange(msg1, "gx").reshape(GX * R1, NZ)
    fy, by, g = call(k1b, [LINE, LINE, (3,) + FACE], (w,))
    msg2, hzp, dx, hz_low = call(
        k2, [(GY, R2, NZ), FIELD, FIELD, FACE], (m1, e, h, w, v, fy, by, g))
    m2 = exchange(msg2, "gy")
    xstat = call(k2b, [(GX,) + FACE, (GX,) + FACE, (GX + 1,) + FACE, (GX + 1,) + FACE], (m1,))
    (msg3, hyc, hryc, bey, dey, ex1, hz1, hz1m, inj, hyp, hxpp, hzpp, dz, dy2, own) = call(
        k3, [(GX, R3, NZ), (GY,) + FACE, (GY,) + FACE, (GY + 1,) + FACE, (GY + 1,) + FACE,
             FIELD, FIELD, FACE, FIELD, FIELD, FIELD, FIELD, FIELD, FIELD, (4,) + FACE],
        (m2, e, h, w, v, hzp, dx, hz_low, fy, fx, bx, *xstat), scratch=[FIELD, FIELD, FIELD])
    ystat = (hyc, hryc, bey, dey)
    m3 = exchange(msg3, "gx")
    msg4, dz2, hypp, own2 = call(
        k4, [(GY, R4, NZ), FIELD, FIELD, (2,) + FACE],
        (m3, own, v, w, dz, fx, fy, by, hyp, hxpp, inj, *xstat, *ystat))
    m4 = exchange(msg4, "gy")
    ex2, ey2, hy2, hz2 = call(
        k4b, [FIELD] * 4, (m3, own, v, w, fx, ex1, hz1, hz1m, hypp, hzpp, dy2, *xstat), scratch=[FIELD])
    e_out, h_out = call(
        k5, [(3,) + FIELD, (3,) + FIELD], (m4, own2, dz2, fy, hxpp, ex2, ey2, hy2, hz2, *ystat))
    return e_out.reshape(3, CX, CY, NZ), h_out.reshape(3, CX, CY, NZ)


def solution(mesh):
    in_specs = (
        P(None, "gx", "gy", None),
        P(None, "gx", "gy", None),
        P("gx", "gy", None),
        P(),
        P(),
        P(("gx", "gy")),
        P(("gx", "gy"), None),
        P(("gx", "gy")),
        P(("gx", "gy")),
    )
    out_specs = (P(None, "gx", "gy", None), P(None, "gx", "gy", None))
    return jax.shard_map(body, mesh=mesh, in_specs=in_specs, out_specs=out_specs, check_vma=False)
```

```python
import jax
import jax.numpy as jnp
from jax import lax
from jax.experimental import pallas as pl
from jax.experimental.pallas import tpu as pltpu
from jax.sharding import PartitionSpec as P

F32 = jnp.float32
BF16 = jnp.bfloat16
CX = 16
CY = 16
NZ = 128
CELLS = CX * CY
GX = 8
GY = 16
HS = 16.0
INV = 1.0 / 256.0

R1_VAL, R1_HALO, R1_G11, R1_G1N, R1_GNN, R1_CODE, R1 = 0, 32, 48, 64, 80, 96, 104
R2_VAL, R2_CODE, R2_HA, R2_HB, R2_P1, R2_P2, R2_G11, R2_G1N, R2_GNN, R2 = (
    0, 16, 24, 40, 56, 72, 88, 104, 120, 136)
R3_Z, R3_Y, R3_T, R3 = 0, 16, 32, 48
R4 = 16


def iota(shape, dim):
    return lax.broadcasted_iota(jnp.int32, shape, dim)


def z_up(f):
    return jnp.where(iota(f.shape, 1) == NZ - 1, 0.0, pltpu.roll(f, NZ - 1, 1))


def z_down(f):
    return jnp.where(iota(f.shape, 1) == 0, 0.0, pltpu.roll(f, 1, 1))


def y_up(f, last):
    return jnp.where(iota(f.shape, 0) == CY - 1, last, pltpu.roll(f, CY - 1, 0))


def y_down(f, first):
    return jnp.where(iota(f.shape, 0) == 0, first, pltpu.roll(f, 1, 0))


def rows(x):
    return pl.ds(x * CY, CY)


def strided(y):
    return pl.ds(y, CX, stride=CY)


def z_solve(w, d):
    lane = iota(w.shape, 1)
    a = jnp.where(lane == 0, 0.0, 1.0)
    c = jnp.where(lane == NZ - 1, 0.0, 1.0)
    e = w + (2.0 - a - c)
    step = 1
    while step < NZ:
        rb = 1.0 / (e + a + c)
        eb = e * rb
        db = d * rb
        e = e + a * pltpu.roll(eb, step, 1) + c * pltpu.roll(eb, NZ - step, 1)
        d = d + a * pltpu.roll(db, step, 1) + c * pltpu.roll(db, NZ - step, 1)
        if 2 * step < NZ:
            a, c = a * pltpu.roll(a * rb, step, 1), c * pltpu.roll(c * rb, NZ - step, 1)
        step *= 2
    return d / e


def z_factors(w, out):
    lane = iota(w.shape, 1)
    a = jnp.where(lane == 0, 0.0, 1.0)
    c = jnp.where(lane == NZ - 1, 0.0, 1.0)
    e = w + (2.0 - a - c)
    for k in range(7):
        step = 1 << k
        rb = 1.0 / (e + a + c)
        low = a * pltpu.roll(rb, step, 1)
        high = c * pltpu.roll(rb, NZ - step, 1)
        out[2 * k], out[2 * k + 1] = low, high
        e = e + low * pltpu.roll(e, step, 1) + high * pltpu.roll(e, NZ - step, 1)
        if k < 6:
            a, c = low * pltpu.roll(a, step, 1), high * pltpu.roll(c, NZ - step, 1)
    out[14] = 1.0 / e


def z_apply(d, f):
    for k in range(7):
        step = 1 << k
        d = d + f[2 * k] * pltpu.roll(d, step, 1) + f[2 * k + 1] * pltpu.roll(d, NZ - step, 1)
    return d * f[14]


def pivots(ws):
    def sweep(seq):
        s, l = seq[0], None
        rf = 1.0 / (1.0 + 1.0 + s)
        out = [rf]
        l = rf
        for w in seq[1:]:
            s = w + s * rf
            rf = 1.0 / (1.0 + l + s)
            out.append(rf)
            l = l * rf
        return out, l
    fwd, link = sweep(ws)
    bwd, _ = sweep(ws[::-1])
    return fwd, bwd[::-1], link


def ends(ds, fwd, bwd):
    y = ds[0]
    b = ds[-1]
    n = len(ds)
    for k in range(1, n):
        y = ds[k] + fwd[k - 1] * y
        b = ds[n - 1 - k] + bwd[n - k] * b
    return b * bwd[0], y * fwd[n - 1]


def block_solve(ds, fwd, left, right):
    ys = [ds[0] + left]
    for k in range(1, len(ds)):
        ys.append(ds[k] + fwd[k - 1] * ys[-1])
    u = (ys[-1] + right) * fwd[-1]
    us = [u]
    for k in range(len(ds) - 2, -1, -1):
        u = (ys[k] + u) * fwd[k]
        us.append(u)
    return us[::-1]


def static_fold(n, g11, g1n, gnn, h_ref, hr_ref, be_ref, de_ref):
    zero = jnp.zeros((16, NZ), F32)
    be = zero
    de = zero
    be_ref[0] = be
    de_ref[n] = de
    for k in range(n):
        a1, a2, a3 = g11(k), g1n(k), gnn(k)
        h = a2 / (1.0 - a1 * be)
        be = a3 + a2 * h * be
        h_ref[k] = h
        be_ref[k + 1] = be
        j = n - 1 - k
        b1, b2, b3 = g11(j), g1n(j), gnn(j)
        hr = b2 / (1.0 - b3 * de)
        de = b1 + b2 * hr * de
        hr_ref[j] = hr
        de_ref[j] = de


def interface(n, me, own_m, own_n, recv, h_ref, hr_ref, be_ref, de_ref):
    al = jnp.zeros((16, NZ), F32)
    ga = jnp.zeros((16, NZ), F32)
    for k in range(n - 1):
        al = jnp.where(k < me, recv(k) + h_ref[k] * al, al)
        j = n - 1 - k
        ga = jnp.where(j > me, recv(j) + hr_ref[j] * ga, ga)
    be, be1 = be_ref[me], be_ref[me + 1]
    de, de1 = de_ref[me], de_ref[me + 1]
    own_ga = own_n + hr_ref[me] * ga
    own_al = own_m + h_ref[me] * al
    left = (al + be * own_ga) / (1.0 - be * de)
    right = (ga + de1 * own_al) / (1.0 - be1 * de1)
    return left, right


def to_messages(me, p1, p2, h_ref, hr_ref, be_ref, de_ref):
    m = p2 + h_ref[me] * be_ref[me] * p1
    n = p1 + hr_ref[me] * de_ref[me + 1] * p2
    return m, n


def split_dot(sel, values):
    hi = values.astype(BF16)
    rest = values - hi.astype(F32)
    mid = rest.astype(BF16)
    low = (rest - mid.astype(F32)).astype(BF16)
    dims = (((1,), (0,)), ((), ()))

    def part(v):
        return lax.dot_general(sel, v, dims, preferred_element_type=F32)

    return part(hi) + part(mid) + part(low)


def k1(e_h, h_h, mat_h, perm_h, cond_h, cells_h, dest_h, tgt_h, gain_h, msg, w_o, v_o, fx_o, bx_o,
       ez, ey_first, hz_last, mat, perm, cond, cells, dest, tgt, gain, sem):
    copies = [
        pltpu.make_async_copy(src, dst, sem.at[k])
        for k, (src, dst) in enumerate([
            (perm_h, perm), (cond_h, cond), (mat_h, mat), (dest_h, dest), (cells_h, cells), (tgt_h, tgt),
            (gain_h, gain), (e_h.at[2], ez), (e_h.at[1, rows(0)], ey_first), (h_h.at[2, rows(CX - 1)], hz_last)])
    ]
    for copy in copies:
        copy.start()
    for copy in copies[:3]:
        copy.wait()
    me = lax.axis_index("gx")
    ws = [(perm[k] + 8.0 * cond[k]) * (1.0 / 4096.0) for k in range(8)]
    vs = [(perm[k] - 8.0 * cond[k]) * (1.0 / 4096.0) for k in range(8)]

    def pick(table, bits):
        for bit in bits:
            table = [jnp.where(bit, table[2 * k + 1], table[2 * k]) for k in range(len(table) // 2)]
        return table[0]

    wx = []
    for x in range(CX):
        m = mat[rows(x), :]
        bits = [(m & 1) != 0, (m & 2) != 0, (m & 4) != 0]
        w = pick(ws, bits)
        w_o[rows(x), :] = w
        v_o[rows(x), :] = pick(vs, bits)
        wx.append(w)
    fwd, bwd, link = pivots(wx)
    for x in range(CX):
        fx_o[x] = fwd[x]
        bx_o[x] = bwd[x]
    for copy in copies[3:]:
        copy.wait()
    to = dest[...]
    to_b = jnp.broadcast_to(to, (128, 128))
    same = (to_b.T == to_b) & (iota((128, 128), 0) < iota((128, 128), 1))
    rank = jnp.sum(same.astype(jnp.int32), axis=0, keepdims=True)
    lane_slot = rank * GY + (to & (GY - 1))
    dest_x = to >> 4
    hot = iota((CELLS, 128), 0) == dest_x * 32 + lane_slot
    slot_gain = jnp.sum(jnp.where(hot, gain[...], 0.0), axis=1, keepdims=True)
    from_cell = (iota((CELLS, 128), 0) == cells[...]).astype(BF16)
    nt = (((1,), (1,)), ((), ()))
    pickm = lax.dot_general(hot.astype(BF16), from_cell, nt, preferred_element_type=F32)
    vals = split_dot(pickm.astype(BF16), ez[...]) * slot_gain
    code_at = jnp.where(iota((8, 128), 0) == dest_x, (tgt[...] + 1).astype(F32), 0.0).astype(BF16)
    lane_hot = (iota((128, 128), 0) == lane_slot).astype(BF16)
    code = lax.dot_general(code_at, lane_hot, nt, preferred_element_type=F32)
    for d in range(GX):
        msg[d, 0:32, :] = vals[d * 32:(d + 1) * 32]
        msg[d, R1_HALO:R1_HALO + 16, :] = jnp.where(d > me, hz_last[...], ey_first[...])
        msg[d, R1_G11:R1_G11 + 16, :] = bwd[0]
        msg[d, R1_G1N:R1_G1N + 16, :] = link
        msg[d, R1_GNN:R1_GNN + 16, :] = fwd[CX - 1]
        msg[d, R1_CODE:R1_CODE + 8, :] = jnp.broadcast_to(code[d:d + 1], (8, NZ))


def k1b(e, h, w, v, fy_o, by_o, g_o, hyp_o, dz_o, hxpp_o, dy2_o, zx_o, zy_o, hxp_s, ey1_s, dy1_s):
    ws = [w[strided(y), :] for y in range(CY)]
    fwd, bwd, link = pivots(ws)
    for y in range(CY):
        fy_o[y] = fwd[y]
        by_o[y] = bwd[y]
    g_o[0] = bwd[0]
    g_o[1] = link
    g_o[2] = fwd[CY - 1]
    z_factors(w[rows(0), :], zx_o)
    z_factors(w[strided(CY - 1), :], zy_o)
    prev_hyp = None
    prev_hz = None
    for x in range(CX):
        ez = e[2, rows(x), :]
        hx = h[0, rows(x), :]
        ex = e[0, rows(x), :]
        hz = h[2, rows(x), :]
        hxp = hx - HS * (y_up(ez, 0.0) - ez)
        hxp_s[rows(x), :] = hxp
        hyp = h[1, rows(x), :] - HS * (z_up(ex) - ex)
        hyp_o[rows(x), :] = hyp
        curl_z = hyp - (hx - y_down(hx, 0.0))
        curl_y = (hxp - z_down(hxp)) - hz
        if x > 0:
            curl_z = curl_z - prev_hyp
            curl_y = curl_y + prev_hz
        prev_hyp = hyp
        prev_hz = hz
        dz_o[rows(x), :] = v[rows(x), :] * ez + INV * curl_z
        dy1_s[rows(x), :] = v[rows(x), :] * e[1, rows(x), :] + INV * curl_y
    for q in range(4):
        part = pl.ds(q * 64, 64)
        ey1_s[part, :] = z_solve(w[part, :], dy1_s[part, :])
    for x in range(CX):
        ey1 = ey1_s[rows(x), :]
        dey1 = HS * (z_up(ey1) - ey1)
        hx1 = hxp_s[rows(x), :] + dey1
        hxpp_o[rows(x), :] = hx1 + dey1
        dy2_o[rows(x), :] = v[rows(x), :] * ey1 + INV * (hx1 - z_down(hx1))


def k2(m1, e, h, v, fy, by, g, msg, hzp_o, dx_o, halo_o, h_o, hr_o, be_o, de_o):
    gx = lax.axis_index("gx")
    me = lax.axis_index("gy")
    lo = jnp.maximum(gx - 1, 0) * R1 + R1_HALO
    hi = jnp.minimum(gx + 1, GX - 1) * R1 + R1_HALO
    hz_low = jnp.where(gx > 0, m1[pl.ds(lo, 16), :], 0.0)
    ey_high = jnp.where(gx < GX - 1, m1[pl.ds(hi, 16), :], 0.0)
    halo_o[...] = hz_low
    for x in range(CX):
        ey = e[1, rows(x), :]
        ey_next = e[1, rows(x + 1), :] if x < CX - 1 else ey_high
        hzp = h[2, rows(x), :] - HS * (ey_next - ey)
        hzp_o[rows(x), :] = hzp
        hy = h[1, rows(x), :]
        curl = (hzp - y_down(hzp, 0.0)) - (hy - z_down(hy))
        dx_o[rows(x), :] = v[rows(x), :] * e[0, rows(x), :] + INV * curl
    bwd = [by[y] for y in range(CY)]
    fwd = [fy[y] for y in range(CY)]
    p1, p2 = ends([dx_o[strided(y), :] for y in range(CY)], fwd, bwd)
    t = -INV * hzp_o[strided(CY - 1), :]
    p2 = p2 + t
    ez_first = e[2, strided(0), :]
    hx_last = h[0, strided(CY - 1), :]
    code = m1[pl.ds(R1_CODE, 8, stride=R1), :]
    for d in range(GY):
        for r in range(2):
            msg[d, r * 8:r * 8 + 8, :] = m1[pl.ds(r * GY + d, 8, stride=R1), :]
        msg[d, R2_CODE:R2_CODE + 8, :] = code
        msg[d, R2_HA:R2_HA + 16, :] = jnp.where(d > me, hx_last, ez_first)
        msg[d, R2_HB:R2_HB + 16, :] = t
        msg[d, R2_P1:R2_P1 + 16, :] = p1
        msg[d, R2_P2:R2_P2 + 16, :] = p2
        msg[d, R2_G11:R2_G11 + 16, :] = g[0]
        msg[d, R2_G1N:R2_G1N + 16, :] = g[1]
        msg[d, R2_GNN:R2_GNN + 16, :] = g[2]
    static_fold(
        GX,
        lambda j: m1[pl.ds(j * R1 + R1_G11, 16), :],
        lambda j: m1[pl.ds(j * R1 + R1_G1N, 16), :],
        lambda j: m1[pl.ds(j * R1 + R1_GNN, 16), :],
        h_o, hr_o, be_o, de_o)


def k3(m2, v, hzp, dx, fy, fx, bx, hz_low, hx_c, hrx_c, bex, dex, hyp, dz0, hxpp0, dy20, zx, zy,
       msg, hy_c, hry_c, bey, dey, ex1_o, hz1_o, hz1m_o, inj_o, hxpp_o, hzpp_o, dz_o, dy2_o, own_o):
    gx = lax.axis_index("gx")
    me = lax.axis_index("gy")
    static_fold(GY, lambda j: m2[j, R2_G11:R2_G11 + 16, :], lambda j: m2[j, R2_G1N:R2_G1N + 16, :],
                lambda j: m2[j, R2_GNN:R2_GNN + 16, :], hy_c, hry_c, bey, dey)
    p1 = m2[me, R2_P1:R2_P1 + 16, :]
    p2 = m2[me, R2_P2:R2_P2 + 16, :]
    own_m, own_n = to_messages(me, p1, p2, hy_c, hry_c, bey, dey)

    def recv(j):
        q1 = m2[j, R2_P1:R2_P1 + 16, :]
        q2 = m2[j, R2_P2:R2_P2 + 16, :]
        return jnp.where(j < me, q2 + hy_c[j] * bey[j] * q1, q1 + hry_c[j] * dey[j + 1] * q2)

    left, right = interface(GY, me, own_m, own_n, recv, hy_c, hry_c, bey, dey)
    us = block_solve([dx[strided(y), :] for y in range(CY)], [fy[y] for y in range(CY)], left, right)
    for y in range(CY):
        ex1_o[strided(y), :] = us[y]
    below = jnp.maximum(me - 1, 0)
    above = jnp.minimum(me + 1, GY - 1)
    t = m2[below, R2_HB:R2_HB + 16, :]
    hz1m_o[...] = jnp.where(me > 0, HS * (us[0] - left) - 240.0 * t, 0.0)
    hx_low = jnp.where(me > 0, m2[below, R2_HA:R2_HA + 16, :], 0.0)
    ez_high = jnp.where(me < GY - 1, m2[above, R2_HA:R2_HA + 16, :], 0.0)
    codes = jnp.concatenate([m2[j, R2_CODE:R2_CODE + 8, :] for j in range(GY)], axis=0).astype(BF16)
    inj = None
    for r in range(2):
        lane = (iota((8, 128), 1) == r * GY + me).astype(BF16)
        code_row = lax.dot_general(lane, codes, (((1,), (1,)), ((), ())), preferred_element_type=F32)[0:1]
        land = ((iota((CELLS, 128), 0) + 1).astype(F32) == code_row).astype(BF16)
        vals = jnp.concatenate([m2[j, r * 8:r * 8 + 8, :] for j in range(GY)], axis=0)
        part = split_dot(land, vals)
        inj = part if inj is None else inj + part
    inj_o[...] = inj
    dz_o[...] = dz0[...] - INV * inj
    dz_o[strided(0), :] = dz_o[strided(0), :] + INV * hx_low
    c_h = -HS * ez_high
    c_e = z_apply(INV * (c_h - z_down(c_h)), zy)
    c_d = HS * (z_up(c_e) - c_e)
    c_1 = c_h + c_d
    b_e = z_apply(INV * hz_low[...], zx)
    b_d = HS * (z_up(b_e) - b_e)
    hxpp_o[...] = hxpp0[...]
    hxpp_o[rows(0), :] = hxpp_o[rows(0), :] + (b_d + b_d)
    hxpp_o[strided(CY - 1), :] = hxpp_o[strided(CY - 1), :] + (c_1 + c_d)
    prev = None
    for x in range(CX):
        ex1 = ex1_o[rows(x), :]
        dex1 = HS * (y_up(ex1, right[x:x + 1]) - ex1)
        hz1 = hzp[rows(x), :] + dex1
        hz1_o[rows(x), :] = hz1
        hzpp = hz1 + dex1
        hzpp_o[rows(x), :] = hzpp
        curl = prev - hzpp if x > 0 else -hzpp
        prev = hzpp
        dy2_o[rows(x), :] = dy20[rows(x), :] + INV * curl
    dy2_o[rows(0), :] = dy2_o[rows(0), :] + v[rows(0), :] * b_e + INV * (b_d - z_down(b_d))
    dy2_o[strided(CY - 1), :] = dy2_o[strided(CY - 1), :] + v[strided(CY - 1), :] * c_e + INV * (c_1 - z_down(c_1))
    fwd = [fx[x] for x in range(CX)]
    bwd = [bx[x] for x in range(CX)]
    tz = -INV * hyp[rows(CX - 1), :]
    p1, p2 = ends([dz_o[rows(x), :] for x in range(CX)], fwd, bwd)
    mz, nz = to_messages(gx, p1, p2 + tz, hx_c, hrx_c, bex, dex)
    ty = INV * hzpp_o[rows(CX - 1), :]
    p1, p2 = ends([dy2_o[rows(x), :] for x in range(CX)], fwd, bwd)
    my, ny = to_messages(gx, p1, p2 + ty, hx_c, hrx_c, bex, dex)
    own_o[0], own_o[1], own_o[2], own_o[3] = mz, nz, my, ny
    for d in range(GX):
        msg[d, 0:16, :] = jnp.where(d > gx, mz, nz)
        msg[d, 16:32, :] = jnp.where(d > gx, my, ny)
        msg[d, 32:48, :] = tz


def k4(m3, own, v, dz, fx, fy, by, hyp, hxpp, inj, hx_c, hrx_c, bex, dex, hy_c, hry_c, bey, dey,
       msg, dz2_o, hypp_o, own_o):
    gx = lax.axis_index("gx")
    me = lax.axis_index("gy")
    left, right = interface(GX, gx, own[0], own[1], lambda j: m3[j, 0:16, :], hx_c, hrx_c, bex, dex)
    us = block_solve([dz[rows(x), :] for x in range(CX)], [fx[x] for x in range(CX)], left, right)
    t = m3[jnp.maximum(gx - 1, 0), 32:48, :]
    prev = jnp.where(gx > 0, HS * (us[0] - left) - 240.0 * t, 0.0)
    for x in range(CX):
        dez = HS * ((us[x + 1] if x < CX - 1 else right) - us[x])
        hy1 = hyp[rows(x), :] + dez
        hypp_o[rows(x), :] = hy1 + dez
        hx2 = hxpp[rows(x), :]
        curl = (hy1 - prev) - (hx2 - y_down(hx2, 0.0)) - inj[rows(x), :]
        prev = hy1
        dz2_o[rows(x), :] = v[rows(x), :] * us[x] + INV * curl
    p1, p2 = ends([dz2_o[strided(y), :] for y in range(CY)], [fy[y] for y in range(CY)], [by[y] for y in range(CY)])
    p2 = p2 + INV * hxpp[strided(CY - 1), :]
    m, n = to_messages(me, p1, p2, hy_c, hry_c, bey, dey)
    own_o[0], own_o[1] = m, n
    for d in range(GY):
        msg[d] = jnp.where(d > me, m, n)


def k4b(m3, own, v, w, fx, ex1, hz1, hz1m, hypp, hzpp, dy2, hx_c, hrx_c, bex, dex,
        e_o, h_o, ex2_s, ey2_s, hy2_s, hz2_s, dx2_s, sem):
    gx = lax.axis_index("gx")
    left, right = interface(GX, gx, own[2], own[3], lambda j: m3[j, 16:32, :], hx_c, hrx_c, bex, dex)
    us = block_solve([dy2[rows(x), :] for x in range(CX)], [fx[x] for x in range(CX)], left, right)
    for x in range(CX):
        ey2_s[rows(x), :] = us[x]
        hz2_s[rows(x), :] = hzpp[rows(x), :] - HS * ((us[x + 1] if x < CX - 1 else right) - us[x])
        hz = hz1[rows(x), :]
        hy = hypp[rows(x), :]
        curl = (hz - y_down(hz, hz1m[x:x + 1, :])) - (hy - z_down(hy))
        dx2_s[rows(x), :] = v[rows(x), :] * ex1[rows(x), :] + INV * curl
    copies = [pltpu.make_async_copy(ey2_s, e_o.at[1], sem.at[0]), pltpu.make_async_copy(hz2_s, h_o.at[2], sem.at[1]),
              pltpu.make_async_copy(ex2_s, e_o.at[0], sem.at[2]), pltpu.make_async_copy(hy2_s, h_o.at[1], sem.at[3])]
    copies[0].start()
    copies[1].start()
    for q in range(4):
        part = pl.ds(q * 64, 64)
        ex2 = z_solve(w[part, :], dx2_s[part, :])
        ex2_s[part, :] = ex2
        hy2_s[part, :] = hypp[part, :] - HS * (z_up(ex2) - ex2)
    copies[2].start()
    copies[3].start()
    for copy in copies:
        copy.wait()


def k5(m4, own, dz2, fy, hxpp, hy_c, hry_c, bey, dey, e_in, h_in, e_o, h_o, ez2_s, hx2_s, sem):
    me = lax.axis_index("gy")
    left, right = interface(GY, me, own[0], own[1], lambda j: m4[j], hy_c, hry_c, bey, dey)
    us = block_solve([dz2[strided(y), :] for y in range(CY)], [fy[y] for y in range(CY)], left, right)
    for y in range(CY):
        ez2_s[strided(y), :] = us[y]
    first = pltpu.make_async_copy(ez2_s, e_o.at[2], sem.at[0])
    first.start()
    for x in range(CX):
        ez2 = ez2_s[rows(x), :]
        hx2_s[rows(x), :] = hxpp[rows(x), :] - HS * (y_up(ez2, right[x:x + 1]) - ez2)
    second = pltpu.make_async_copy(hx2_s, h_o.at[0], sem.at[1])
    second.start()
    first.wait()
    second.wait()


def call(kernel, shapes, args, scratch=(), hbm_in=(), hbm_out=(), alias=None):
    def spec(in_hbm):
        return pl.BlockSpec(memory_space=pltpu.HBM if in_hbm else pltpu.VMEM)
    return pl.pallas_call(
        kernel,
        out_shape=[jax.ShapeDtypeStruct(s, F32) for s in shapes],
        in_specs=[spec(k in hbm_in) for k in range(len(args))],
        out_specs=[spec(k in hbm_out) for k in range(len(shapes))],
        scratch_shapes=[pltpu.VMEM(s, F32) if isinstance(s, tuple) else s for s in scratch],
        input_output_aliases=alias or {},
        compiler_params=pltpu.CompilerParams(vmem_limit_bytes=12 << 20),
        name=kernel.__name__,
    )(*args)


def exchange(message, axis):
    return lax.all_to_all(message, axis, split_axis=0, concat_axis=0, tiled=True)


FIELD = (CELLS, NZ)
FACE = (16, NZ)
LINE = (16, 16, NZ)


def body(e_fields, h_fields, material, permittivity, conductivity, electrode_cells, electrode_dest,
         target_cells, electrode_gain):
    e = e_fields.reshape(3, CELLS, NZ)
    h = h_fields.reshape(3, CELLS, NZ)
    mat = material.reshape(CELLS, NZ)
    row = (1, 128)
    dma = pltpu.SemaphoreType.DMA
    hbm = [pltpu.with_memory_space_constraint(a, pltpu.HBM) for a in (
        e, h, mat, permittivity, conductivity, electrode_cells.reshape(row),
        electrode_dest.reshape(row), target_cells.reshape(row), electrode_gain.reshape(row))]
    msg1, w, v, fx, bx = call(
        k1, [(GX, R1, NZ), FIELD, FIELD, LINE, LINE],
        hbm,
        scratch=[FIELD, FACE, FACE, pltpu.VMEM(FIELD, jnp.int32), pltpu.SMEM((8,), F32), pltpu.SMEM((8,), F32),
                 pltpu.VMEM(row, jnp.int32), pltpu.VMEM(row, jnp.int32), pltpu.VMEM(row, jnp.int32), row, dma((10,))],
        hbm_in=range(9))
    m1 = exchange(msg1, "gx").reshape(GX * R1, NZ)
    (fy, by, g, hyp, dz0, hxpp0, dy20, zx, zy) = call(
        k1b, [LINE, LINE, (3,) + FACE, FIELD, FIELD, FIELD, FIELD, (15,) + FACE, (15,) + FACE],
        (e, h, w, v), scratch=[FIELD, FIELD, FIELD])
    (msg2, hzp, dx, hz_low, *xstat) = call(
        k2, [(GY, R2, NZ), FIELD, FIELD, FACE, (GX,) + FACE, (GX,) + FACE, (GX + 1,) + FACE, (GX + 1,) + FACE],
        (m1, e, h, v, fy, by, g))
    m2 = exchange(msg2, "gy")
    (msg3, hyc, hryc, bey, dey, ex1, hz1, hz1m, inj, hxpp, hzpp, dz, dy2, own) = call(
        k3, [(GX, R3, NZ), (GY,) + FACE, (GY,) + FACE, (GY + 1,) + FACE, (GY + 1,) + FACE,
             FIELD, FIELD, FACE, FIELD, FIELD, FIELD, FIELD, FIELD, (4,) + FACE],
        (m2, v, hzp, dx, fy, fx, bx, hz_low, *xstat, hyp, dz0, hxpp0, dy20, zx, zy))
    ystat = (hyc, hryc, bey, dey)
    m3 = exchange(msg3, "gx")
    msg4, dz2, hypp, own2 = call(
        k4, [(GY, R4, NZ), FIELD, FIELD, (2,) + FACE],
        (m3, own, v, dz, fx, fy, by, hyp, hxpp, inj, *xstat, *ystat))
    m4 = exchange(msg4, "gy")
    e_out, h_out = call(
        k4b, [(3,) + FIELD, (3,) + FIELD], (m3, own, v, w, fx, ex1, hz1, hz1m, hypp, hzpp, dy2, *xstat),
        scratch=[FIELD] * 5 + [dma((4,))], hbm_out=(0, 1))
    e_out, h_out = call(
        k5, [(3,) + FIELD, (3,) + FIELD], (m4, own2, dz2, fy, hxpp, *ystat, e_out, h_out),
        scratch=[FIELD, FIELD, dma((2,))], hbm_in=(9, 10), hbm_out=(0, 1), alias={9: 0, 10: 1})
    return e_out.reshape(3, CX, CY, NZ), h_out.reshape(3, CX, CY, NZ)


def solution(mesh):
    in_specs = (
        P(None, "gx", "gy", None),
        P(None, "gx", "gy", None),
        P("gx", "gy", None),
        P(),
        P(),
        P(("gx", "gy")),
        P(("gx", "gy"), None),
        P(("gx", "gy")),
        P(("gx", "gy")),
    )
    out_specs = (P(None, "gx", "gy", None), P(None, "gx", "gy", None))
    return jax.shard_map(body, mesh=mesh, in_specs=in_specs, out_specs=out_specs, check_vma=False)
```

```python
import jax
import jax.numpy as jnp
from jax import lax
from jax.experimental import pallas as pl
from jax.experimental.pallas import tpu as pltpu
from jax.sharding import PartitionSpec as P

F32 = jnp.float32
BF16 = jnp.bfloat16
CX = 16
CY = 16
NZ = 128
CELLS = CX * CY
GX = 8
GY = 16
HS = 16.0
INV = 1.0 / 256.0

R1_VAL, R1_HALO, R1_G11, R1_G1N, R1_GNN, R1_CODE, R1 = 0, 32, 48, 64, 80, 96, 104
X_CODE, X_BLOCK, X_HALO = 64, 72, 152
Y_CODE, Y_BLOCK, Y_HALO = 64, 96, 176
HALO = (0, 32, 0, 16)
R3_Z, R3_Y, R3_T, R3 = 0, 16, 32, 48
R4 = 16


def iota(shape, dim):
    return lax.broadcasted_iota(jnp.int32, shape, dim)


def z_up(f):
    return jnp.where(iota(f.shape, 1) == NZ - 1, 0.0, pltpu.roll(f, NZ - 1, 1))


def z_down(f):
    return jnp.where(iota(f.shape, 1) == 0, 0.0, pltpu.roll(f, 1, 1))


def y_up(f, last):
    return jnp.where(iota(f.shape, 0) == CY - 1, last, pltpu.roll(f, CY - 1, 0))


def y_down(f, first):
    return jnp.where(iota(f.shape, 0) == 0, first, pltpu.roll(f, 1, 0))


def rows(x):
    return pl.ds(x * CY, CY)


def strided(y):
    return pl.ds(y, CX, stride=CY)


def z_solve(w, d):
    lane = iota(w.shape, 1)
    a = jnp.where(lane == 0, 0.0, 1.0)
    c = jnp.where(lane == NZ - 1, 0.0, 1.0)
    e = w + (2.0 - a - c)
    step = 1
    while step < NZ:
        rb = 1.0 / (e + a + c)
        eb = e * rb
        db = d * rb
        e = e + a * pltpu.roll(eb, step, 1) + c * pltpu.roll(eb, NZ - step, 1)
        d = d + a * pltpu.roll(db, step, 1) + c * pltpu.roll(db, NZ - step, 1)
        if 2 * step < NZ:
            a, c = a * pltpu.roll(a * rb, step, 1), c * pltpu.roll(c * rb, NZ - step, 1)
        step *= 2
    return d / e


def z_factors(w, out):
    lane = iota(w.shape, 1)
    a = jnp.where(lane == 0, 0.0, 1.0)
    c = jnp.where(lane == NZ - 1, 0.0, 1.0)
    e = w + (2.0 - a - c)
    for k in range(7):
        step = 1 << k
        rb = 1.0 / (e + a + c)
        low = a * pltpu.roll(rb, step, 1)
        high = c * pltpu.roll(rb, NZ - step, 1)
        out[2 * k], out[2 * k + 1] = low, high
        e = e + low * pltpu.roll(e, step, 1) + high * pltpu.roll(e, NZ - step, 1)
        if k < 6:
            a, c = low * pltpu.roll(a, step, 1), high * pltpu.roll(c, NZ - step, 1)
    out[14] = 1.0 / e


def z_apply(d, f):
    for k in range(7):
        step = 1 << k
        d = d + f[2 * k] * pltpu.roll(d, step, 1) + f[2 * k + 1] * pltpu.roll(d, NZ - step, 1)
    return d * f[14]


def pivots(ws):
    def sweep(seq):
        s, l = seq[0], None
        rf = 1.0 / (1.0 + 1.0 + s)
        out = [rf]
        l = rf
        for w in seq[1:]:
            s = w + s * rf
            rf = 1.0 / (1.0 + l + s)
            out.append(rf)
            l = l * rf
        return out, l
    fwd, link = sweep(ws)
    bwd, _ = sweep(ws[::-1])
    return fwd, bwd[::-1], link


def ends(ds, fwd, bwd):
    y = ds[0]
    b = ds[-1]
    n = len(ds)
    for k in range(1, n):
        y = ds[k] + fwd[k - 1] * y
        b = ds[n - 1 - k] + bwd[n - k] * b
    return b * bwd[0], y * fwd[n - 1]


def block_solve(ds, fwd, left, right):
    ys = [ds[0] + left]
    for k in range(1, len(ds)):
        ys.append(ds[k] + fwd[k - 1] * ys[-1])
    u = (ys[-1] + right) * fwd[-1]
    us = [u]
    for k in range(len(ds) - 2, -1, -1):
        u = (ys[k] + u) * fwd[k]
        us.append(u)
    return us[::-1]


def static_fold(n, g11, g1n, gnn, h_ref, hr_ref, be_ref, de_ref, be=None, de=None):
    zero = jnp.zeros((16, NZ), F32)
    be = zero if be is None else be
    de = zero if de is None else de
    be_ref[0] = be
    de_ref[n] = de
    for k in range(n):
        a1, a2, a3 = g11(k), g1n(k), gnn(k)
        h = a2 / (1.0 - a1 * be)
        be = a3 + a2 * h * be
        h_ref[k] = h
        be_ref[k + 1] = be
        j = n - 1 - k
        b1, b2, b3 = g11(j), g1n(j), gnn(j)
        hr = b2 / (1.0 - b3 * de)
        de = b1 + b2 * hr * de
        hr_ref[j] = hr
        de_ref[j] = de


def incoming(n, me, recv, h_ref, hr_ref, al=None, ga=None):
    zero = jnp.zeros((16, NZ), F32)
    al = zero if al is None else al
    ga = zero if ga is None else ga
    for k in range(n - 1):
        al = jnp.where(k < me, recv(k) + h_ref[k] * al, al)
        j = n - 1 - k
        ga = jnp.where(j > me, recv(j) + hr_ref[j] * ga, ga)
    return al, ga


def interface(n, me, own_m, own_n, recv, h_ref, hr_ref, be_ref, de_ref, al=None, ga=None):
    al, ga = incoming(n, me, recv, h_ref, hr_ref, al, ga)
    be, be1 = be_ref[me], be_ref[me + 1]
    de, de1 = de_ref[me], de_ref[me + 1]
    own_ga = own_n + hr_ref[me] * ga
    own_al = own_m + h_ref[me] * al
    left = (al + be * own_ga) / (1.0 - be * de)
    right = (ga + de1 * own_al) / (1.0 - be1 * de1)
    return left, right


def pair_terms(k, q1, q2, h_ref, hr_ref, be_ref, de_ref):
    return q2 + h_ref[k] * be_ref[k] * q1, q1 + hr_ref[k] * de_ref[k + 1] * q2


def faces(ref, k):
    return [ref[k, pl.ds(16 * f, 16), :] for f in range(5)]


def place(buf, own_at, own, others):
    buf[own_at] = own
    for d, value in enumerate(others, 1):
        buf[(own_at + 4 - d) & 3] = value


def to_messages(me, p1, p2, h_ref, hr_ref, be_ref, de_ref):
    m = p2 + h_ref[me] * be_ref[me] * p1
    n = p1 + hr_ref[me] * de_ref[me + 1] * p2
    return m, n


def split_dot(sel, values):
    hi = values.astype(BF16)
    rest = values - hi.astype(F32)
    mid = rest.astype(BF16)
    low = (rest - mid.astype(F32)).astype(BF16)
    dims = (((1,), (0,)), ((), ()))

    def part(v):
        return lax.dot_general(sel, v, dims, preferred_element_type=F32)

    return part(hi) + part(mid) + part(low)


def k1(e_h, h_h, mat_h, perm_h, cond_h, cells_h, dest_h, tgt_h, gain_h, msg, w_o, v_o, fx_o, bx_o,
       ez, ey_first, hz_last, mat, perm, cond, cells, dest, tgt, gain, sem):
    copies = [
        pltpu.make_async_copy(src, dst, sem.at[k])
        for k, (src, dst) in enumerate([
            (perm_h, perm), (cond_h, cond), (mat_h, mat), (dest_h, dest), (cells_h, cells), (tgt_h, tgt),
            (gain_h, gain), (e_h.at[2], ez), (e_h.at[1, rows(0)], ey_first), (h_h.at[2, rows(CX - 1)], hz_last)])
    ]
    for copy in copies:
        copy.start()
    for copy in copies[:3]:
        copy.wait()
    me = lax.axis_index("gx")
    ws = [(perm[k] + 8.0 * cond[k]) * (1.0 / 4096.0) for k in range(8)]
    vs = [(perm[k] - 8.0 * cond[k]) * (1.0 / 4096.0) for k in range(8)]

    def pick(table, bits):
        for bit in bits:
            table = [jnp.where(bit, table[2 * k + 1], table[2 * k]) for k in range(len(table) // 2)]
        return table[0]

    wx = []
    for x in range(CX):
        m = mat[rows(x), :]
        bits = [(m & 1) != 0, (m & 2) != 0, (m & 4) != 0]
        w = pick(ws, bits)
        w_o[rows(x), :] = w
        v_o[rows(x), :] = pick(vs, bits)
        wx.append(w)
    fwd, bwd, link = pivots(wx)
    for x in range(CX):
        fx_o[x] = fwd[x]
        bx_o[x] = bwd[x]
    for copy in copies[3:]:
        copy.wait()
    to = dest[...]
    to_b = jnp.broadcast_to(to, (128, 128))
    same = (to_b.T == to_b) & (iota((128, 128), 0) < iota((128, 128), 1))
    rank = jnp.sum(same.astype(jnp.int32), axis=0, keepdims=True)
    lane_slot = rank * GY + (to & (GY - 1))
    dest_x = to >> 4
    hot = iota((CELLS, 128), 0) == dest_x * 32 + lane_slot
    slot_gain = jnp.sum(jnp.where(hot, gain[...], 0.0), axis=1, keepdims=True)
    from_cell = (iota((CELLS, 128), 0) == cells[...]).astype(BF16)
    nt = (((1,), (1,)), ((), ()))
    pickm = lax.dot_general(hot.astype(BF16), from_cell, nt, preferred_element_type=F32)
    vals = split_dot(pickm.astype(BF16), ez[...]) * slot_gain
    code_at = jnp.where(iota((8, 128), 0) == dest_x, (tgt[...] + 1).astype(F32), 0.0).astype(BF16)
    lane_hot = (iota((128, 128), 0) == lane_slot).astype(BF16)
    code = lax.dot_general(code_at, lane_hot, nt, preferred_element_type=F32)
    for d in range(GX):
        msg[d, 0:32, :] = vals[d * 32:(d + 1) * 32]
        msg[d, R1_HALO:R1_HALO + 16, :] = jnp.where(d > me, hz_last[...], ey_first[...])
        msg[d, R1_G11:R1_G11 + 16, :] = bwd[0]
        msg[d, R1_G1N:R1_G1N + 16, :] = link
        msg[d, R1_GNN:R1_GNN + 16, :] = fwd[CX - 1]
        msg[d, R1_CODE:R1_CODE + 8, :] = jnp.broadcast_to(code[d:d + 1], (8, NZ))


def k1b(e, h, w, v, fy_o, by_o, g_o, hyp_o, dz_o, hxpp_o, dy2_o, zx_o, zy_o, hxp_s, ey1_s, dy1_s):
    ws = [w[strided(y), :] for y in range(CY)]
    fwd, bwd, link = pivots(ws)
    for y in range(CY):
        fy_o[y] = fwd[y]
        by_o[y] = bwd[y]
    g_o[0] = bwd[0]
    g_o[1] = link
    g_o[2] = fwd[CY - 1]
    z_factors(w[rows(0), :], zx_o)
    z_factors(w[strided(CY - 1), :], zy_o)
    prev_hyp = None
    prev_hz = None
    for x in range(CX):
        ez = e[2, rows(x), :]
        hx = h[0, rows(x), :]
        ex = e[0, rows(x), :]
        hz = h[2, rows(x), :]
        hxp = hx - HS * (y_up(ez, 0.0) - ez)
        hxp_s[rows(x), :] = hxp
        hyp = h[1, rows(x), :] - HS * (z_up(ex) - ex)
        hyp_o[rows(x), :] = hyp
        curl_z = hyp - (hx - y_down(hx, 0.0))
        curl_y = (hxp - z_down(hxp)) - hz
        if x > 0:
            curl_z = curl_z - prev_hyp
            curl_y = curl_y + prev_hz
        prev_hyp = hyp
        prev_hz = hz
        dz_o[rows(x), :] = v[rows(x), :] * ez + INV * curl_z
        dy1_s[rows(x), :] = v[rows(x), :] * e[1, rows(x), :] + INV * curl_y
    for q in range(4):
        part = pl.ds(q * 64, 64)
        ey1_s[part, :] = z_solve(w[part, :], dy1_s[part, :])
    for x in range(CX):
        ey1 = ey1_s[rows(x), :]
        dey1 = HS * (z_up(ey1) - ey1)
        hx1 = hxp_s[rows(x), :] + dey1
        hxpp_o[rows(x), :] = hx1 + dey1
        dy2_o[rows(x), :] = v[rows(x), :] * ey1 + INV * (hx1 - z_down(hx1))


def k2(m1, e, h, v, fy, by, g, mx1, mx2, mx3, own_o, hzp_o, dx_o, halo_o, h_o, hr_o, be_o, de_o, vals_s):
    gx = lax.axis_index("gx")
    me = lax.axis_index("gy")
    lo = jnp.maximum(gx - 1, 0) * R1 + R1_HALO
    hi = jnp.minimum(gx + 1, GX - 1) * R1 + R1_HALO
    hz_low = jnp.where(gx > 0, m1[pl.ds(lo, 16), :], 0.0)
    ey_high = jnp.where(gx < GX - 1, m1[pl.ds(hi, 16), :], 0.0)
    halo_o[...] = hz_low
    for x in range(CX):
        ey = e[1, rows(x), :]
        ey_next = e[1, rows(x + 1), :] if x < CX - 1 else ey_high
        hzp = h[2, rows(x), :] - HS * (ey_next - ey)
        hzp_o[rows(x), :] = hzp
        hy = h[1, rows(x), :]
        curl = (hzp - y_down(hzp, 0.0)) - (hy - z_down(hy))
        dx_o[rows(x), :] = v[rows(x), :] * e[0, rows(x), :] + INV * curl
    bwd = [by[y] for y in range(CY)]
    fwd = [fy[y] for y in range(CY)]
    p1, p2 = ends([dx_o[strided(y), :] for y in range(CY)], fwd, bwd)
    t = -INV * hzp_o[strided(CY - 1), :]
    p2 = p2 + t
    for to in range(4):
        for r in range(2):
            for y in range(4):
                at = (r * 4 + y) * 8
                vals_s[to, at:at + 8, :] = m1[pl.ds(r * GY + 4 * y + to, 8, stride=R1), :]
    code = m1[pl.ds(R1_CODE, 8, stride=R1), :]
    for d, ref in enumerate((own_o, mx1, mx2, mx3)):
        ref[0:64, :] = vals_s[(me + d) & 3]
        ref[X_CODE:X_CODE + 8, :] = code
        for f, face in enumerate((p1, p2, g[0], g[1], g[2])):
            ref[X_BLOCK + 16 * f:X_BLOCK + 16 * f + 16, :] = face
    mx1[X_HALO:X_HALO + 16, :] = h[0, strided(CY - 1), :]
    mx1[X_HALO + 16:X_HALO + 32, :] = t
    mx3[X_HALO:X_HALO + 16, :] = e[2, strided(0), :]
    static_fold(
        GX,
        lambda j: m1[pl.ds(j * R1 + R1_G11, 16), :],
        lambda j: m1[pl.ds(j * R1 + R1_G1N, 16), :],
        lambda j: m1[pl.ds(j * R1 + R1_GNN, 16), :],
        h_o, hr_o, be_o, de_o)


def k2c(own, r1, r2, r3, my1, my2, my3, own_o, blk_o, h_o, hr_o, be_o, de_o):
    at = lax.axis_index("gy") & 3
    to = lax.axis_index("gy") >> 2
    srcs = (own, r1, r2, r3)
    place(blk_o, at, own[X_BLOCK:X_HALO, :], [r[X_BLOCK:X_HALO, :] for r in srcs[1:]])
    static_fold(4, lambda k: blk_o[k, 32:48, :], lambda k: blk_o[k, 48:64, :], lambda k: blk_o[k, 64:80, :],
                h_o, hr_o, be_o, de_o)
    terms = [pair_terms(k, blk_o[k, 0:16, :], blk_o[k, 16:32, :], h_o, hr_o, be_o, de_o) for k in range(4)]
    al, ga, link = terms[0][0], terms[3][1], h_o[0]
    for k in range(1, 4):
        al = terms[k][0] + h_o[k] * al
        ga = terms[3 - k][1] + hr_o[3 - k] * ga
        link = link * h_o[k]
    for d, ref in enumerate((own_o, my1, my2, my3)):
        y = (to + d) & 3
        for k, src in enumerate(srcs):
            for r in range(2):
                row = pl.multiple_of((r * 4 + y) * 8, 8)
                ref[(k * 2 + r) * 8:(k * 2 + r) * 8 + 8, :] = src[pl.ds(row, 8), :]
            ref[Y_CODE + k * 8:Y_CODE + k * 8 + 8, :] = src[X_CODE:X_CODE + 8, :]
        for f, face in enumerate((ga, al, de_o[0], link, be_o[4])):
            ref[Y_BLOCK + 16 * f:Y_BLOCK + 16 * f + 16, :] = face
    my1[Y_HALO:Y_HALO + 32, :] = r1[X_HALO:X_HALO + 32, :]
    my3[Y_HALO:Y_HALO + 16, :] = r3[X_HALO:X_HALO + 16, :]


def k3(own, s1, s2, s3, r1, r3, blk, h0, hr0, v, hzp, dx, fy, fx, bx, hz_low, hx_c, hrx_c, bex, dex,
       hyp, dz0, hxpp0, dy20, zx, zy,
       msg, hs_c, hrs_c, bes, des, hg_c, hrg_c, beg, deg, tr_o, ex1_o, hz1_o, hz1m_o, inj_o, hxpp_o, hzpp_o,
       dz_o, dy2_o, own_o, grp):
    gx = lax.axis_index("gx")
    gy = lax.axis_index("gy")
    at = gy & 3
    me = gy >> 2
    place(grp, me, own[Y_BLOCK:Y_HALO, :], [r[Y_BLOCK:Y_HALO, :] for r in (s1, s2, s3)])
    static_fold(4, lambda k: grp[k, 32:48, :], lambda k: grp[k, 48:64, :], lambda k: grp[k, 64:80, :],
                hs_c, hrs_c, bes, des)
    static_fold(4, lambda k: blk[k, 32:48, :], lambda k: blk[k, 48:64, :], lambda k: blk[k, 64:80, :],
                hg_c, hrg_c, beg, deg, bes[me], des[me + 1])

    def group_term(k):
        m, n = pair_terms(k, grp[k, 0:16, :], grp[k, 16:32, :], hs_c, hrs_c, bes, des)
        return jnp.where(k < me, m, n)

    def tile_term(k):
        m, n = pair_terms(k, blk[k, 0:16, :], blk[k, 16:32, :], hg_c, hrg_c, beg, deg)
        return jnp.where(k < at, m, n)

    al, ga = incoming(4, me, group_term, hs_c, hrs_c)
    own_m, own_n = pair_terms(at, blk[at, 0:16, :], blk[at, 16:32, :], hg_c, hrg_c, beg, deg)
    left, right = interface(4, at, own_m, own_n, tile_term, hg_c, hrg_c, beg, deg, al, ga)
    one = jnp.ones((16, NZ), F32)
    to_right, to_left = one, one
    for k in range(4):
        to_right = jnp.where(k > at, to_right * h0[k], to_right)
        to_left = jnp.where(k < at, to_left * hr0[k], to_left)
    tr_o[0] = to_right
    tr_o[1] = to_left
    us = block_solve([dx[strided(y), :] for y in range(CY)], [fy[y] for y in range(CY)], left, right)
    for y in range(CY):
        ex1_o[strided(y), :] = us[y]
    low = jnp.where(at > 0, r1[X_HALO:X_HALO + 32, :], s1[Y_HALO:Y_HALO + 32, :])
    high = jnp.where(at < 3, r3[X_HALO:X_HALO + 16, :], s3[Y_HALO:Y_HALO + 16, :])
    hz1m_o[...] = jnp.where(gy > 0, HS * (us[0] - left) - 240.0 * low[16:32], 0.0)
    hx_low = jnp.where(gy > 0, low[0:16], 0.0)
    ez_high = jnp.where(gy < GY - 1, high, 0.0)
    srcs = (own, s1, s2, s3)
    codes = jnp.concatenate([r[Y_CODE:Y_CODE + 32, :] for r in srcs], axis=0).astype(BF16)
    inj = None
    for r in range(2):
        lane = (iota((8, 128), 1) == r * GY + gy).astype(BF16)
        code_row = lax.dot_general(lane, codes, (((1,), (1,)), ((), ())), preferred_element_type=F32)[0:1]
        land = ((iota((CELLS, 128), 0) + 1).astype(F32) == code_row).astype(BF16)
        vals = jnp.concatenate(
            [ref[(k * 2 + r) * 8:(k * 2 + r) * 8 + 8, :] for ref in srcs for k in range(4)], axis=0)
        part = split_dot(land, vals)
        inj = part if inj is None else inj + part
    inj_o[...] = inj
    dz_o[...] = dz0[...] - INV * inj
    dz_o[strided(0), :] = dz_o[strided(0), :] + INV * hx_low
    c_h = -HS * ez_high
    c_e = z_apply(INV * (c_h - z_down(c_h)), zy)
    c_d = HS * (z_up(c_e) - c_e)
    c_1 = c_h + c_d
    b_e = z_apply(INV * hz_low[...], zx)
    b_d = HS * (z_up(b_e) - b_e)
    hxpp_o[...] = hxpp0[...]
    hxpp_o[rows(0), :] = hxpp_o[rows(0), :] + (b_d + b_d)
    hxpp_o[strided(CY - 1), :] = hxpp_o[strided(CY - 1), :] + (c_1 + c_d)
    prev = None
    for x in range(CX):
        ex1 = ex1_o[rows(x), :]
        dex1 = HS * (y_up(ex1, right[x:x + 1]) - ex1)
        hz1 = hzp[rows(x), :] + dex1
        hz1_o[rows(x), :] = hz1
        hzpp = hz1 + dex1
        hzpp_o[rows(x), :] = hzpp
        curl = prev - hzpp if x > 0 else -hzpp
        prev = hzpp
        dy2_o[rows(x), :] = dy20[rows(x), :] + INV * curl
    dy2_o[rows(0), :] = dy2_o[rows(0), :] + v[rows(0), :] * b_e + INV * (b_d - z_down(b_d))
    dy2_o[strided(CY - 1), :] = dy2_o[strided(CY - 1), :] + v[strided(CY - 1), :] * c_e + INV * (c_1 - z_down(c_1))
    fwd = [fx[x] for x in range(CX)]
    bwd = [bx[x] for x in range(CX)]
    tz = -INV * hyp[rows(CX - 1), :]
    p1, p2 = ends([dz_o[rows(x), :] for x in range(CX)], fwd, bwd)
    mz, nz = to_messages(gx, p1, p2 + tz, hx_c, hrx_c, bex, dex)
    ty = INV * hzpp_o[rows(CX - 1), :]
    p1, p2 = ends([dy2_o[rows(x), :] for x in range(CX)], fwd, bwd)
    my, ny = to_messages(gx, p1, p2 + ty, hx_c, hrx_c, bex, dex)
    own_o[0], own_o[1], own_o[2], own_o[3] = mz, nz, my, ny
    for d in range(GX):
        msg[d, 0:16, :] = jnp.where(d > gx, mz, nz)
        msg[d, 16:32, :] = jnp.where(d > gx, my, ny)
        msg[d, 32:48, :] = tz


def k4(m3, own, v, dz, fx, fy, by, hyp, hxpp, inj, hx_c, hrx_c, bex, dex,
       h0, hr0, be0, de0, hs_c, hrs_c, bes, des, hg_c, hrg_c, beg, deg, tr, msg, dz2_o, hypp_o, own_o):
    gx = lax.axis_index("gx")
    at = lax.axis_index("gy") & 3
    me = lax.axis_index("gy") >> 2
    left, right = interface(GX, gx, own[0], own[1], lambda j: m3[j, 0:16, :], hx_c, hrx_c, bex, dex)
    us = block_solve([dz[rows(x), :] for x in range(CX)], [fx[x] for x in range(CX)], left, right)
    t = m3[jnp.maximum(gx - 1, 0), 32:48, :]
    prev = jnp.where(gx > 0, HS * (us[0] - left) - 240.0 * t, 0.0)
    for x in range(CX):
        dez = HS * ((us[x + 1] if x < CX - 1 else right) - us[x])
        hy1 = hyp[rows(x), :] + dez
        hypp_o[rows(x), :] = hy1 + dez
        hx2 = hxpp[rows(x), :]
        curl = (hy1 - prev) - (hx2 - y_down(hx2, 0.0)) - inj[rows(x), :]
        prev = hy1
        dz2_o[rows(x), :] = v[rows(x), :] * us[x] + INV * curl
    p1, p2 = ends([dz2_o[strided(y), :] for y in range(CY)], [fy[y] for y in range(CY)], [by[y] for y in range(CY)])
    p2 = p2 + INV * hxpp[strided(CY - 1), :]
    m, n = pair_terms(at, p1, p2, hg_c, hrg_c, beg, deg)
    own_o[0], own_o[1] = m, n
    m0, n0 = pair_terms(at, p1, p2, h0, hr0, be0, de0)
    m0, n0 = tr[0] * m0, tr[1] * n0
    group_m, group_n = pair_terms(me, n0, m0, hs_c, hrs_c, bes, des)
    for d in range(GY):
        y, x = d // 4, d % 4
        msg[d] = jnp.where(y > me, group_m, jnp.where(y < me, group_n, jnp.where(x > at, m, n)))


def k4b(m3, own, v, w, fx, ex1, hz1, hz1m, hypp, hzpp, dy2, hx_c, hrx_c, bex, dex,
        e_o, h_o, ex2_s, ey2_s, hy2_s, hz2_s, dx2_s, sem):
    gx = lax.axis_index("gx")
    left, right = interface(GX, gx, own[2], own[3], lambda j: m3[j, 16:32, :], hx_c, hrx_c, bex, dex)
    us = block_solve([dy2[rows(x), :] for x in range(CX)], [fx[x] for x in range(CX)], left, right)
    for x in range(CX):
        ey2_s[rows(x), :] = us[x]
        hz2_s[rows(x), :] = hzpp[rows(x), :] - HS * ((us[x + 1] if x < CX - 1 else right) - us[x])
        hz = hz1[rows(x), :]
        hy = hypp[rows(x), :]
        curl = (hz - y_down(hz, hz1m[x:x + 1, :])) - (hy - z_down(hy))
        dx2_s[rows(x), :] = v[rows(x), :] * ex1[rows(x), :] + INV * curl
    copies = [pltpu.make_async_copy(ey2_s, e_o.at[1], sem.at[0]), pltpu.make_async_copy(hz2_s, h_o.at[2], sem.at[1]),
              pltpu.make_async_copy(ex2_s, e_o.at[0], sem.at[2]), pltpu.make_async_copy(hy2_s, h_o.at[1], sem.at[3])]
    copies[0].start()
    copies[1].start()
    for q in range(4):
        part = pl.ds(q * 64, 64)
        ex2 = z_solve(w[part, :], dx2_s[part, :])
        ex2_s[part, :] = ex2
        hy2_s[part, :] = hypp[part, :] - HS * (z_up(ex2) - ex2)
    copies[2].start()
    copies[3].start()
    for copy in copies:
        copy.wait()


def k5(m4, own, dz2, fy, hxpp, hs_c, hrs_c, hg_c, hrg_c, beg, deg, e_in, h_in, e_o, h_o, ez2_s, hx2_s, sem):
    at = lax.axis_index("gy") & 3
    me = lax.axis_index("gy") >> 2
    al, ga = incoming(4, me, lambda k: m4[4 * k] + m4[4 * k + 1] + m4[4 * k + 2] + m4[4 * k + 3], hs_c, hrs_c)
    left, right = interface(4, at, own[0], own[1], lambda k: m4[4 * me + k], hg_c, hrg_c, beg, deg, al, ga)
    us = block_solve([dz2[strided(y), :] for y in range(CY)], [fy[y] for y in range(CY)], left, right)
    for y in range(CY):
        ez2_s[strided(y), :] = us[y]
    first = pltpu.make_async_copy(ez2_s, e_o.at[2], sem.at[0])
    first.start()
    for x in range(CX):
        ez2 = ez2_s[rows(x), :]
        hx2_s[rows(x), :] = hxpp[rows(x), :] - HS * (y_up(ez2, right[x:x + 1]) - ez2)
    second = pltpu.make_async_copy(hx2_s, h_o.at[0], sem.at[1])
    second.start()
    first.wait()
    second.wait()


def call(kernel, shapes, args, scratch=(), hbm_in=(), hbm_out=(), alias=None):
    def spec(in_hbm):
        return pl.BlockSpec(memory_space=pltpu.HBM if in_hbm else pltpu.VMEM)
    return pl.pallas_call(
        kernel,
        out_shape=[jax.ShapeDtypeStruct(s, F32) for s in shapes],
        in_specs=[spec(k in hbm_in) for k in range(len(args))],
        out_specs=[spec(k in hbm_out) for k in range(len(shapes))],
        scratch_shapes=[pltpu.VMEM(s, F32) if isinstance(s, tuple) else s for s in scratch],
        input_output_aliases=alias or {},
        compiler_params=pltpu.CompilerParams(vmem_limit_bytes=12 << 20),
        name=kernel.__name__,
    )(*args)


def ring_x(message, d):
    pairs = [(4 * y + x, 4 * y + (x + d) % 4) for y in range(4) for x in range(4)]
    return lax.ppermute(message, "gy", pairs)


def ring_y(message, d):
    pairs = [(4 * y + x, 4 * ((y + d) % 4) + x) for y in range(4) for x in range(4)]
    return lax.ppermute(message, "gy", pairs)


def exchange(message, axis):
    return lax.all_to_all(message, axis, split_axis=0, concat_axis=0, tiled=True)


FIELD = (CELLS, NZ)
FACE = (16, NZ)
LINE = (16, 16, NZ)


def body(e_fields, h_fields, material, permittivity, conductivity, electrode_cells, electrode_dest,
         target_cells, electrode_gain):
    e = e_fields.reshape(3, CELLS, NZ)
    h = h_fields.reshape(3, CELLS, NZ)
    mat = material.reshape(CELLS, NZ)
    row = (1, 128)
    dma = pltpu.SemaphoreType.DMA
    hbm = [pltpu.with_memory_space_constraint(a, pltpu.HBM) for a in (
        e, h, mat, permittivity, conductivity, electrode_cells.reshape(row),
        electrode_dest.reshape(row), target_cells.reshape(row), electrode_gain.reshape(row))]
    msg1, w, v, fx, bx = call(
        k1, [(GX, R1, NZ), FIELD, FIELD, LINE, LINE],
        hbm,
        scratch=[FIELD, FACE, FACE, pltpu.VMEM(FIELD, jnp.int32), pltpu.SMEM((8,), F32), pltpu.SMEM((8,), F32),
                 pltpu.VMEM(row, jnp.int32), pltpu.VMEM(row, jnp.int32), pltpu.VMEM(row, jnp.int32), row, dma((10,))],
        hbm_in=range(9))
    m1 = exchange(msg1, "gx").reshape(GX * R1, NZ)
    (fy, by, g, hyp, dz0, hxpp0, dy20, zx, zy) = call(
        k1b, [LINE, LINE, (3,) + FACE, FIELD, FIELD, FIELD, FIELD, (15,) + FACE, (15,) + FACE],
        (e, h, w, v), scratch=[FIELD, FIELD, FIELD])
    chain = [(4,) + FACE, (4,) + FACE, (5,) + FACE, (5,) + FACE]
    out = call(
        k2, [(X_HALO + HALO[d], NZ) for d in (1, 2, 3)] + [
            (X_HALO, NZ), FIELD, FIELD, FACE, (GX,) + FACE, (GX,) + FACE, (GX + 1,) + FACE, (GX + 1,) + FACE],
        (m1, e, h, v, fy, by, g), scratch=[(4, 64, NZ)])
    msgx, (ownx, hzp, dx, hz_low), xstat = out[:3], out[3:7], out[7:]
    rx = [ring_x(m, d) for d, m in enumerate(msgx, 1)]
    out = call(
        k2c, [(Y_HALO + HALO[d], NZ) for d in (1, 2, 3)] + [(Y_HALO, NZ), (4, 80, NZ)] + chain, (ownx, *rx))
    msgy, owny, blk, zstat = out[:3], out[3], out[4], out[5:]
    ry = [ring_y(m, d) for d, m in enumerate(msgy, 1)]
    out = call(
        k3, [(GX, R3, NZ)] + chain + chain + [(2,) + FACE, FIELD, FIELD, FACE, FIELD, FIELD, FIELD, FIELD, FIELD,
                                              (4,) + FACE],
        (owny, *ry, rx[0], rx[2], blk, zstat[0], zstat[1], v, hzp, dx, fy, fx, bx, hz_low, *xstat,
         hyp, dz0, hxpp0, dy20, zx, zy), scratch=[(4, 80, NZ)])
    msg3, sstat, gstat, tr = out[0], out[1:5], out[5:9], out[9]
    ex1, hz1, hz1m, inj, hxpp, hzpp, dz, dy2, own = out[10:]
    m3 = exchange(msg3, "gx")
    msg4, dz2, hypp, own2 = call(
        k4, [(GY, R4, NZ), FIELD, FIELD, (2,) + FACE],
        (m3, own, v, dz, fx, fy, by, hyp, hxpp, inj, *xstat, *zstat, *sstat, *gstat, tr))
    m4 = exchange(msg4, "gy")
    e_out, h_out = call(
        k4b, [(3,) + FIELD, (3,) + FIELD], (m3, own, v, w, fx, ex1, hz1, hz1m, hypp, hzpp, dy2, *xstat),
        scratch=[FIELD] * 5 + [dma((4,))], hbm_out=(0, 1))
    e_out, h_out = call(
        k5, [(3,) + FIELD, (3,) + FIELD], (m4, own2, dz2, fy, hxpp, sstat[0], sstat[1], *gstat, e_out, h_out),
        scratch=[FIELD, FIELD, dma((2,))], hbm_in=(11, 12), hbm_out=(0, 1), alias={11: 0, 12: 1})
    return e_out.reshape(3, CX, CY, NZ), h_out.reshape(3, CX, CY, NZ)


def solution(mesh):
    in_specs = (
        P(None, "gx", "gy", None),
        P(None, "gx", "gy", None),
        P("gx", "gy", None),
        P(),
        P(),
        P(("gx", "gy")),
        P(("gx", "gy"), None),
        P(("gx", "gy")),
        P(("gx", "gy")),
    )
    out_specs = (P(None, "gx", "gy", None), P(None, "gx", "gy", None))
    return jax.shard_map(body, mesh=mesh, in_specs=in_specs, out_specs=out_specs, check_vma=False)
```

```python
import jax
import jax.numpy as jnp
from jax import lax
from jax.experimental import pallas as pl
from jax.experimental.pallas import tpu as pltpu
from jax.sharding import PartitionSpec as P

F32 = jnp.float32
BF16 = jnp.bfloat16
CX = 16
CY = 16
NZ = 128
CELLS = CX * CY
GX = 8
GY = 16
HS = 16.0
INV = 1.0 / 256.0

C_CODE, C_HALO, C_COEF, C_ALL = 256, 264, 296, 344
Z_CODE, Z_COEF, Z_HALO = 64, 72, 120
X_CODE, X_BLOCK, X_HALO = 64, 72, 152
Y_CODE, Y_BLOCK, Y_HALO = 64, 96, 176
HALO = (0, 32, 0, 16)
Z_ROWS = (0, 16, 0, 16)
R4 = 16


def iota(shape, dim):
    return lax.broadcasted_iota(jnp.int32, shape, dim)


def z_up(f):
    return jnp.where(iota(f.shape, 1) == NZ - 1, 0.0, pltpu.roll(f, NZ - 1, 1))


def z_down(f):
    return jnp.where(iota(f.shape, 1) == 0, 0.0, pltpu.roll(f, 1, 1))


def y_up(f, last):
    return jnp.where(iota(f.shape, 0) == CY - 1, last, pltpu.roll(f, CY - 1, 0))


def y_down(f, first):
    return jnp.where(iota(f.shape, 0) == 0, first, pltpu.roll(f, 1, 0))


def rows(x):
    return pl.ds(x * CY, CY)


def strided(y):
    return pl.ds(y, CX, stride=CY)


def z_solve(w, d):
    lane = iota(w.shape, 1)
    a = jnp.where(lane == 0, 0.0, 1.0)
    c = jnp.where(lane == NZ - 1, 0.0, 1.0)
    e = w + (2.0 - a - c)
    step = 1
    while step < NZ:
        rb = 1.0 / (e + a + c)
        eb = e * rb
        db = d * rb
        e = e + a * pltpu.roll(eb, step, 1) + c * pltpu.roll(eb, NZ - step, 1)
        d = d + a * pltpu.roll(db, step, 1) + c * pltpu.roll(db, NZ - step, 1)
        if 2 * step < NZ:
            a, c = a * pltpu.roll(a * rb, step, 1), c * pltpu.roll(c * rb, NZ - step, 1)
        step *= 2
    return d / e


def z_factors(w, out):
    lane = iota(w.shape, 1)
    a = jnp.where(lane == 0, 0.0, 1.0)
    c = jnp.where(lane == NZ - 1, 0.0, 1.0)
    e = w + (2.0 - a - c)
    for k in range(7):
        step = 1 << k
        rb = 1.0 / (e + a + c)
        low = a * pltpu.roll(rb, step, 1)
        high = c * pltpu.roll(rb, NZ - step, 1)
        out[2 * k], out[2 * k + 1] = low, high
        e = e + low * pltpu.roll(e, step, 1) + high * pltpu.roll(e, NZ - step, 1)
        if k < 6:
            a, c = low * pltpu.roll(a, step, 1), high * pltpu.roll(c, NZ - step, 1)
    out[14] = 1.0 / e


def z_apply(d, f):
    for k in range(7):
        step = 1 << k
        d = d + f[2 * k] * pltpu.roll(d, step, 1) + f[2 * k + 1] * pltpu.roll(d, NZ - step, 1)
    return d * f[14]


def pivots(ws):
    def sweep(seq):
        s, l = seq[0], None
        rf = 1.0 / (1.0 + 1.0 + s)
        out = [rf]
        l = rf
        for w in seq[1:]:
            s = w + s * rf
            rf = 1.0 / (1.0 + l + s)
            out.append(rf)
            l = l * rf
        return out, l
    fwd, link = sweep(ws)
    bwd, _ = sweep(ws[::-1])
    return fwd, bwd[::-1], link


def ends(ds, fwd, bwd):
    y = ds[0]
    b = ds[-1]
    n = len(ds)
    for k in range(1, n):
        y = ds[k] + fwd[k - 1] * y
        b = ds[n - 1 - k] + bwd[n - k] * b
    return b * bwd[0], y * fwd[n - 1]


def block_solve(ds, fwd, left, right):
    ys = [ds[0] + left]
    for k in range(1, len(ds)):
        ys.append(ds[k] + fwd[k - 1] * ys[-1])
    u = (ys[-1] + right) * fwd[-1]
    us = [u]
    for k in range(len(ds) - 2, -1, -1):
        u = (ys[k] + u) * fwd[k]
        us.append(u)
    return us[::-1]


def static_fold(n, g11, g1n, gnn, h_ref, hr_ref, be_ref, de_ref, be=None, de=None):
    zero = jnp.zeros((16, NZ), F32)
    be = zero if be is None else be
    de = zero if de is None else de
    be_ref[0] = be
    de_ref[n] = de
    for k in range(n):
        a1, a2, a3 = g11(k), g1n(k), gnn(k)
        h = a2 / (1.0 - a1 * be)
        be = a3 + a2 * h * be
        h_ref[k] = h
        be_ref[k + 1] = be
        j = n - 1 - k
        b1, b2, b3 = g11(j), g1n(j), gnn(j)
        hr = b2 / (1.0 - b3 * de)
        de = b1 + b2 * hr * de
        hr_ref[j] = hr
        de_ref[j] = de


def incoming(n, me, recv, h_ref, hr_ref, al=None, ga=None):
    zero = jnp.zeros((16, NZ), F32)
    al = zero if al is None else al
    ga = zero if ga is None else ga
    for k in range(n - 1):
        al = jnp.where(k < me, recv(k) + h_ref[k] * al, al)
        j = n - 1 - k
        ga = jnp.where(j > me, recv(j) + hr_ref[j] * ga, ga)
    return al, ga


def interface(n, me, own_m, own_n, recv, h_ref, hr_ref, be_ref, de_ref, al=None, ga=None):
    al, ga = incoming(n, me, recv, h_ref, hr_ref, al, ga)
    be, be1 = be_ref[me], be_ref[me + 1]
    de, de1 = de_ref[me], de_ref[me + 1]
    own_ga = own_n + hr_ref[me] * ga
    own_al = own_m + h_ref[me] * al
    left = (al + be * own_ga) / (1.0 - be * de)
    right = (ga + de1 * own_al) / (1.0 - be1 * de1)
    return left, right


def pair_terms(k, q1, q2, h_ref, hr_ref, be_ref, de_ref):
    return q2 + h_ref[k] * be_ref[k] * q1, q1 + hr_ref[k] * de_ref[k + 1] * q2


def place(buf, own_at, own, others):
    buf[own_at] = own
    for d, value in enumerate(others, 1):
        buf[(own_at + 4 - d) & 3] = value


def split_dot(sel, values):
    hi = values.astype(BF16)
    rest = values - hi.astype(F32)
    mid = rest.astype(BF16)
    low = (rest - mid.astype(F32)).astype(BF16)
    dims = (((1,), (0,)), ((), ()))

    def part(v):
        return lax.dot_general(sel, v, dims, preferred_element_type=F32)

    return part(hi) + part(mid) + part(low)


def k1(e_h, h_h, mat_h, perm_h, cond_h, cells_h, dest_h, tgt_h, gain_h, msg, w_o, v_o, fx_o, bx_o,
       ez, ey_first, hz_last, mat, perm, cond, cells, dest, tgt, gain, sem):
    copies = [
        pltpu.make_async_copy(src, dst, sem.at[k])
        for k, (src, dst) in enumerate([
            (perm_h, perm), (cond_h, cond), (mat_h, mat), (dest_h, dest), (cells_h, cells), (tgt_h, tgt),
            (gain_h, gain), (e_h.at[2], ez), (e_h.at[1, rows(0)], ey_first), (h_h.at[2, rows(CX - 1)], hz_last)])
    ]
    for copy in copies:
        copy.start()
    for copy in copies[:3]:
        copy.wait()
    ws = [(perm[k] + 8.0 * cond[k]) * (1.0 / 4096.0) for k in range(8)]
    vs = [(perm[k] - 8.0 * cond[k]) * (1.0 / 4096.0) for k in range(8)]

    def pick(table, bits):
        for bit in bits:
            table = [jnp.where(bit, table[2 * k + 1], table[2 * k]) for k in range(len(table) // 2)]
        return table[0]

    wx = []
    for x in range(CX):
        m = mat[rows(x), :]
        bits = [(m & 1) != 0, (m & 2) != 0, (m & 4) != 0]
        w = pick(ws, bits)
        w_o[rows(x), :] = w
        v_o[rows(x), :] = pick(vs, bits)
        wx.append(w)
    fwd, bwd, link = pivots(wx)
    for x in range(CX):
        fx_o[x] = fwd[x]
        bx_o[x] = bwd[x]
    for copy in copies[3:]:
        copy.wait()
    to = dest[...]
    to_b = jnp.broadcast_to(to, (128, 128))
    same = (to_b.T == to_b) & (iota((128, 128), 0) < iota((128, 128), 1))
    rank = jnp.sum(same.astype(jnp.int32), axis=0, keepdims=True)
    lane_slot = rank * GY + (to & (GY - 1))
    dest_x = to >> 4
    hot = iota((CELLS, 128), 0) == dest_x * 32 + lane_slot
    slot_gain = jnp.sum(jnp.where(hot, gain[...], 0.0), axis=1, keepdims=True)
    from_cell = (iota((CELLS, 128), 0) == cells[...]).astype(BF16)
    nt = (((1,), (1,)), ((), ()))
    pickm = lax.dot_general(hot.astype(BF16), from_cell, nt, preferred_element_type=F32)
    vals = split_dot(pickm.astype(BF16), ez[...]) * slot_gain
    code_at = jnp.where(iota((8, 128), 0) == dest_x, (tgt[...] + 1).astype(F32), 0.0).astype(BF16)
    lane_hot = (iota((128, 128), 0) == lane_slot).astype(BF16)
    code = lax.dot_general(code_at, lane_hot, nt, preferred_element_type=F32)
    msg[0:CELLS, :] = vals
    msg[C_CODE:C_CODE + 8, :] = code
    msg[C_HALO:C_HALO + 16, :] = hz_last[...]
    msg[C_HALO + 16:C_HALO + 32, :] = ey_first[...]
    for f, face in enumerate((bwd[0], link, fwd[CX - 1])):
        msg[C_COEF + 16 * f:C_COEF + 16 * f + 16, :] = face


def k1c(own, rc, mz1, mz2, mz3, own_o, blk_o, h_o, hr_o, be_o, de_o):
    gx = lax.axis_index("gx")
    c = gx & 1
    z = gx >> 1
    blk_o[c] = own[C_COEF:C_ALL, :]
    blk_o[1 - c] = rc[C_COEF:C_ALL, :]
    static_fold(2, lambda k: blk_o[k, 0:16, :], lambda k: blk_o[k, 16:32, :], lambda k: blk_o[k, 32:48, :],
                h_o, hr_o, be_o, de_o)
    for d, ref in enumerate((own_o, mz1, mz2, mz3)):
        to = ((z + d) & 3) * 2 + c
        for r, src in enumerate((own, rc)):
            ref[32 * r:32 * r + 32, :] = src[pl.ds(pl.multiple_of(to * 32, 32), 32), :]
            ref[Z_CODE + r:Z_CODE + r + 1, :] = src[pl.ds(C_CODE + to, 1), :]
        ref[Z_CODE + 2:Z_CODE + 8, :] = jnp.zeros((6, NZ), F32)
        for f, face in enumerate((de_o[0], h_o[0] * h_o[1], be_o[2])):
            ref[Z_COEF + 16 * f:Z_COEF + 16 * f + 16, :] = face
    mz1[Z_HALO:Z_HALO + 16, :] = jnp.where(c == 1, own[C_HALO:C_HALO + 16, :], rc[C_HALO:C_HALO + 16, :])
    mz3[Z_HALO:Z_HALO + 16, :] = jnp.where(c == 0, own[C_HALO + 16:C_HALO + 32, :], rc[C_HALO + 16:C_HALO + 32, :])


def k1b(e, h, w, v, fy_o, by_o, g_o, hyp_o, dz_o, hxpp_o, dy2_o, zx_o, zy_o, hxp_s, ey1_s, dy1_s):
    ws = [w[strided(y), :] for y in range(CY)]
    fwd, bwd, link = pivots(ws)
    for y in range(CY):
        fy_o[y] = fwd[y]
        by_o[y] = bwd[y]
    g_o[0] = bwd[0]
    g_o[1] = link
    g_o[2] = fwd[CY - 1]
    z_factors(w[rows(0), :], zx_o)
    z_factors(w[strided(CY - 1), :], zy_o)
    prev_hyp = None
    prev_hz = None
    for x in range(CX):
        ez = e[2, rows(x), :]
        hx = h[0, rows(x), :]
        ex = e[0, rows(x), :]
        hz = h[2, rows(x), :]
        hxp = hx - HS * (y_up(ez, 0.0) - ez)
        hxp_s[rows(x), :] = hxp
        hyp = h[1, rows(x), :] - HS * (z_up(ex) - ex)
        hyp_o[rows(x), :] = hyp
        curl_z = hyp - (hx - y_down(hx, 0.0))
        curl_y = (hxp - z_down(hxp)) - hz
        if x > 0:
            curl_z = curl_z - prev_hyp
            curl_y = curl_y + prev_hz
        prev_hyp = hyp
        prev_hz = hz
        dz_o[rows(x), :] = v[rows(x), :] * ez + INV * curl_z
        dy1_s[rows(x), :] = v[rows(x), :] * e[1, rows(x), :] + INV * curl_y
    for q in range(4):
        part = pl.ds(q * 64, 64)
        ey1_s[part, :] = z_solve(w[part, :], dy1_s[part, :])
    for x in range(CX):
        ey1 = ey1_s[rows(x), :]
        dey1 = HS * (z_up(ey1) - ey1)
        hx1 = hxp_s[rows(x), :] + dey1
        hxpp_o[rows(x), :] = hx1 + dey1
        dy2_o[rows(x), :] = v[rows(x), :] * ey1 + INV * (hx1 - z_down(hx1))


def k2(rc, ownz, z1, z2, z3, blk, e, h, v, fy, by, g, mx1, mx2, mx3, own_o, hzp_o, dx_o, halo_o,
       h_o, hr_o, be_o, de_o, hg_o, hrg_o, beg_o, deg_o, vals_s, src_s, code_s, grp):
    gx = lax.axis_index("gx")
    me = lax.axis_index("gy")
    c = gx & 1
    z = gx >> 1
    hz_low = jnp.where(c == 1, rc[C_HALO:C_HALO + 16, :], z1[Z_HALO:Z_HALO + 16, :])
    ey_high = jnp.where(c == 0, rc[C_HALO + 16:C_HALO + 32, :], z3[Z_HALO:Z_HALO + 16, :])
    hz_low = jnp.where(gx > 0, hz_low, 0.0)
    ey_high = jnp.where(gx < GX - 1, ey_high, 0.0)
    halo_o[...] = hz_low
    for x in range(CX):
        ey = e[1, rows(x), :]
        ey_next = e[1, rows(x + 1), :] if x < CX - 1 else ey_high
        hzp = h[2, rows(x), :] - HS * (ey_next - ey)
        hzp_o[rows(x), :] = hzp
        hy = h[1, rows(x), :]
        curl = (hzp - y_down(hzp, 0.0)) - (hy - z_down(hy))
        dx_o[rows(x), :] = v[rows(x), :] * e[0, rows(x), :] + INV * curl
    bwd = [by[y] for y in range(CY)]
    fwd = [fy[y] for y in range(CY)]
    p1, p2 = ends([dx_o[strided(y), :] for y in range(CY)], fwd, bwd)
    t = -INV * hzp_o[strided(CY - 1), :]
    p2 = p2 + t
    for k, ref in enumerate((ownz, z1, z2, z3)):
        src_s[64 * k:64 * k + 64, :] = ref[0:64, :]
        code_s[2 * k:2 * k + 2, :] = ref[Z_CODE:Z_CODE + 2, :]
    for to in range(4):
        for r in range(2):
            for y in range(4):
                at = (r * 4 + y) * 8
                vals_s[to, at:at + 8, :] = src_s[pl.ds(r * GY + 4 * y + to, 8, stride=32), :]
    code = code_s[...]
    for d, ref in enumerate((own_o, mx1, mx2, mx3)):
        ref[0:64, :] = vals_s[(me + d) & 3]
        ref[X_CODE:X_CODE + 8, :] = code
        for f, face in enumerate((p1, p2, g[0], g[1], g[2])):
            ref[X_BLOCK + 16 * f:X_BLOCK + 16 * f + 16, :] = face
    mx1[X_HALO:X_HALO + 16, :] = h[0, strided(CY - 1), :]
    mx1[X_HALO + 16:X_HALO + 32, :] = t
    mx3[X_HALO:X_HALO + 16, :] = e[2, strided(0), :]
    place(grp, z, ownz[Z_COEF:Z_HALO, :], [r[Z_COEF:Z_HALO, :] for r in (z1, z2, z3)])
    static_fold(4, lambda k: grp[k, 0:16, :], lambda k: grp[k, 16:32, :], lambda k: grp[k, 32:48, :],
                h_o, hr_o, be_o, de_o)
    static_fold(2, lambda k: blk[k, 0:16, :], lambda k: blk[k, 16:32, :], lambda k: blk[k, 32:48, :],
                hg_o, hrg_o, beg_o, deg_o, be_o[z], de_o[z + 1])


def k2c(own, r1, r2, r3, my1, my2, my3, own_o, blk_o, h_o, hr_o, be_o, de_o):
    at = lax.axis_index("gy") & 3
    to = lax.axis_index("gy") >> 2
    srcs = (own, r1, r2, r3)
    place(blk_o, at, own[X_BLOCK:X_HALO, :], [r[X_BLOCK:X_HALO, :] for r in srcs[1:]])
    static_fold(4, lambda k: blk_o[k, 32:48, :], lambda k: blk_o[k, 48:64, :], lambda k: blk_o[k, 64:80, :],
                h_o, hr_o, be_o, de_o)
    terms = [pair_terms(k, blk_o[k, 0:16, :], blk_o[k, 16:32, :], h_o, hr_o, be_o, de_o) for k in range(4)]
    al, ga, link = terms[0][0], terms[3][1], h_o[0]
    for k in range(1, 4):
        al = terms[k][0] + h_o[k] * al
        ga = terms[3 - k][1] + hr_o[3 - k] * ga
        link = link * h_o[k]
    for d, ref in enumerate((own_o, my1, my2, my3)):
        y = (to + d) & 3
        for k, src in enumerate(srcs):
            for r in range(2):
                row = pl.multiple_of((r * 4 + y) * 8, 8)
                ref[(k * 2 + r) * 8:(k * 2 + r) * 8 + 8, :] = src[pl.ds(row, 8), :]
            ref[Y_CODE + k * 8:Y_CODE + k * 8 + 8, :] = src[X_CODE:X_CODE + 8, :]
        for f, face in enumerate((ga, al, de_o[0], link, be_o[4])):
            ref[Y_BLOCK + 16 * f:Y_BLOCK + 16 * f + 16, :] = face
    my1[Y_HALO:Y_HALO + 32, :] = r1[X_HALO:X_HALO + 32, :]
    my3[Y_HALO:Y_HALO + 16, :] = r3[X_HALO:X_HALO + 16, :]


def k3(own, s1, s2, s3, r1, r3, blk, h0, hr0, v, hzp, dx, fy, fx, bx, hz_low,
       hyp, dz0, hxpp0, dy20, zx, zy,
       msg, hs_c, hrs_c, bes, des, hg_c, hrg_c, beg, deg, tr_o, ex1_o, hz1_o, hz1m_o, inj_o, hxpp_o, hzpp_o,
       dz_o, dy2_o, grp):
    gy = lax.axis_index("gy")
    at = gy & 3
    me = gy >> 2
    place(grp, me, own[Y_BLOCK:Y_HALO, :], [r[Y_BLOCK:Y_HALO, :] for r in (s1, s2, s3)])
    static_fold(4, lambda k: grp[k, 32:48, :], lambda k: grp[k, 48:64, :], lambda k: grp[k, 64:80, :],
                hs_c, hrs_c, bes, des)
    static_fold(4, lambda k: blk[k, 32:48, :], lambda k: blk[k, 48:64, :], lambda k: blk[k, 64:80, :],
                hg_c, hrg_c, beg, deg, bes[me], des[me + 1])

    def group_term(k):
        m, n = pair_terms(k, grp[k, 0:16, :], grp[k, 16:32, :], hs_c, hrs_c, bes, des)
        return jnp.where(k < me, m, n)

    def tile_term(k):
        m, n = pair_terms(k, blk[k, 0:16, :], blk[k, 16:32, :], hg_c, hrg_c, beg, deg)
        return jnp.where(k < at, m, n)

    al, ga = incoming(4, me, group_term, hs_c, hrs_c)
    own_m, own_n = pair_terms(at, blk[at, 0:16, :], blk[at, 16:32, :], hg_c, hrg_c, beg, deg)
    left, right = interface(4, at, own_m, own_n, tile_term, hg_c, hrg_c, beg, deg, al, ga)
    one = jnp.ones((16, NZ), F32)
    to_right, to_left = one, one
    for k in range(4):
        to_right = jnp.where(k > at, to_right * h0[k], to_right)
        to_left = jnp.where(k < at, to_left * hr0[k], to_left)
    tr_o[0] = to_right
    tr_o[1] = to_left
    us = block_solve([dx[strided(y), :] for y in range(CY)], [fy[y] for y in range(CY)], left, right)
    for y in range(CY):
        ex1_o[strided(y), :] = us[y]
    low = jnp.where(at > 0, r1[X_HALO:X_HALO + 32, :], s1[Y_HALO:Y_HALO + 32, :])
    high = jnp.where(at < 3, r3[X_HALO:X_HALO + 16, :], s3[Y_HALO:Y_HALO + 16, :])
    hz1m_o[...] = jnp.where(gy > 0, HS * (us[0] - left) - 240.0 * low[16:32], 0.0)
    hx_low = jnp.where(gy > 0, low[0:16], 0.0)
    ez_high = jnp.where(gy < GY - 1, high, 0.0)
    srcs = (own, s1, s2, s3)
    codes = jnp.concatenate([r[Y_CODE:Y_CODE + 32, :] for r in srcs], axis=0).astype(BF16)
    inj = None
    for r in range(2):
        lane = (iota((8, 128), 1) == r * GY + gy).astype(BF16)
        code_row = lax.dot_general(lane, codes, (((1,), (1,)), ((), ())), preferred_element_type=F32)[0:1]
        land = ((iota((CELLS, 128), 0) + 1).astype(F32) == code_row).astype(BF16)
        vals = jnp.concatenate(
            [ref[(k * 2 + r) * 8:(k * 2 + r) * 8 + 8, :] for ref in srcs for k in range(4)], axis=0)
        part = split_dot(land, vals)
        inj = part if inj is None else inj + part
    inj_o[...] = inj
    dz_o[...] = dz0[...] - INV * inj
    dz_o[strided(0), :] = dz_o[strided(0), :] + INV * hx_low
    c_h = -HS * ez_high
    c_e = z_apply(INV * (c_h - z_down(c_h)), zy)
    c_d = HS * (z_up(c_e) - c_e)
    c_1 = c_h + c_d
    b_e = z_apply(INV * hz_low[...], zx)
    b_d = HS * (z_up(b_e) - b_e)
    hxpp_o[...] = hxpp0[...]
    hxpp_o[rows(0), :] = hxpp_o[rows(0), :] + (b_d + b_d)
    hxpp_o[strided(CY - 1), :] = hxpp_o[strided(CY - 1), :] + (c_1 + c_d)
    prev = None
    for x in range(CX):
        ex1 = ex1_o[rows(x), :]
        dex1 = HS * (y_up(ex1, right[x:x + 1]) - ex1)
        hz1 = hzp[rows(x), :] + dex1
        hz1_o[rows(x), :] = hz1
        hzpp = hz1 + dex1
        hzpp_o[rows(x), :] = hzpp
        curl = prev - hzpp if x > 0 else -hzpp
        prev = hzpp
        dy2_o[rows(x), :] = dy20[rows(x), :] + INV * curl
    dy2_o[rows(0), :] = dy2_o[rows(0), :] + v[rows(0), :] * b_e + INV * (b_d - z_down(b_d))
    dy2_o[strided(CY - 1), :] = dy2_o[strided(CY - 1), :] + v[strided(CY - 1), :] * c_e + INV * (c_1 - z_down(c_1))
    fwd = [fx[x] for x in range(CX)]
    bwd = [bx[x] for x in range(CX)]
    tz = -INV * hyp[rows(CX - 1), :]
    p1, p2 = ends([dz_o[rows(x), :] for x in range(CX)], fwd, bwd)
    ty = INV * hzpp_o[rows(CX - 1), :]
    q1, q2 = ends([dy2_o[rows(x), :] for x in range(CX)], fwd, bwd)
    for f, face in enumerate((p1, p2 + tz, q1, q2 + ty, tz)):
        msg[16 * f:16 * f + 16, :] = face


def k3b(own, rc, h0, hr0, be0, de0, hs_c, hrs_c, bes, des, mz1, mz2, mz3):
    gx = lax.axis_index("gx")
    c = gx & 1
    z = gx >> 1
    terms = []
    for f in range(2):
        blocks = []
        for k in range(2):
            q1 = jnp.where(c == k, own[32 * f:32 * f + 16, :], rc[32 * f:32 * f + 16, :])
            q2 = jnp.where(c == k, own[32 * f + 16:32 * f + 32, :], rc[32 * f + 16:32 * f + 32, :])
            blocks.append(pair_terms(k, q1, q2, h0, hr0, be0, de0))
        last = blocks[1][0] + h0[1] * blocks[0][0]
        first = blocks[0][1] + hr0[0] * blocks[1][1]
        terms.append(pair_terms(z, first, last, hs_c, hrs_c, bes, des))
    for d, ref in enumerate((mz1, mz2, mz3), 1):
        up = ((z + d) & 3) > z
        for f in range(2):
            ref[16 * f:16 * f + 16, :] = jnp.where(up, terms[f][0], terms[f][1])
    mz1[32:48, :] = jnp.where(c == 1, own[64:80, :], rc[64:80, :])


def x_interface(f, own, rc, zs, hs_c, hrs_c, hg_c, hrg_c, beg, deg, buf):
    gx = lax.axis_index("gx")
    c = gx & 1
    z = gx >> 1
    place(buf, z, zs[0][16 * f:16 * f + 16, :], [r[16 * f:16 * f + 16, :] for r in zs])
    al, ga = incoming(4, z, lambda k: buf[k], hs_c, hrs_c)
    own_m, own_n = pair_terms(c, own[32 * f:32 * f + 16, :], own[32 * f + 16:32 * f + 32, :], hg_c, hrg_c, beg, deg)
    other = pair_terms(1 - c, rc[32 * f:32 * f + 16, :], rc[32 * f + 16:32 * f + 32, :], hg_c, hrg_c, beg, deg)
    return interface(2, c, own_m, own_n, lambda k: other[k], hg_c, hrg_c, beg, deg, al, ga)


def k4(own, rc, z1, z2, z3, hxs, hrxs, hxg, hrxg, bexg, dexg, v, dz, fx, fy, by, hyp, hxpp, inj,
       h0, hr0, be0, de0, hs_c, hrs_c, bes, des, hg_c, hrg_c, beg, deg, tr, msg, dz2_o, hypp_o, own_o, buf):
    gx = lax.axis_index("gx")
    at = lax.axis_index("gy") & 3
    me = lax.axis_index("gy") >> 2
    left, right = x_interface(0, own, rc, (z1, z2, z3), hxs, hrxs, hxg, hrxg, bexg, dexg, buf)
    us = block_solve([dz[rows(x), :] for x in range(CX)], [fx[x] for x in range(CX)], left, right)
    t = jnp.where((gx & 1) == 1, rc[64:80, :], z1[32:48, :])
    prev = jnp.where(gx > 0, HS * (us[0] - left) - 240.0 * t, 0.0)
    for x in range(CX):
        dez = HS * ((us[x + 1] if x < CX - 1 else right) - us[x])
        hy1 = hyp[rows(x), :] + dez
        hypp_o[rows(x), :] = hy1 + dez
        hx2 = hxpp[rows(x), :]
        curl = (hy1 - prev) - (hx2 - y_down(hx2, 0.0)) - inj[rows(x), :]
        prev = hy1
        dz2_o[rows(x), :] = v[rows(x), :] * us[x] + INV * curl
    p1, p2 = ends([dz2_o[strided(y), :] for y in range(CY)], [fy[y] for y in range(CY)], [by[y] for y in range(CY)])
    p2 = p2 + INV * hxpp[strided(CY - 1), :]
    m, n = pair_terms(at, p1, p2, hg_c, hrg_c, beg, deg)
    own_o[0], own_o[1] = m, n
    m0, n0 = pair_terms(at, p1, p2, h0, hr0, be0, de0)
    m0, n0 = tr[0] * m0, tr[1] * n0
    group_m, group_n = pair_terms(me, n0, m0, hs_c, hrs_c, bes, des)
    for d in range(GY):
        y, x = d // 4, d % 4
        msg[d] = jnp.where(y > me, group_m, jnp.where(y < me, group_n, jnp.where(x > at, m, n)))


def k4b(own, rc, z1, z2, z3, hxs, hrxs, hxg, hrxg, bexg, dexg, v, w, fx, ex1, hz1, hz1m, hypp, hzpp, dy2,
        e_o, h_o, ex2_s, ey2_s, hy2_s, hz2_s, dx2_s, buf, sem):
    left, right = x_interface(1, own, rc, (z1, z2, z3), hxs, hrxs, hxg, hrxg, bexg, dexg, buf)
    us = block_solve([dy2[rows(x), :] for x in range(CX)], [fx[x] for x in range(CX)], left, right)
    for x in range(CX):
        ey2_s[rows(x), :] = us[x]
        hz2_s[rows(x), :] = hzpp[rows(x), :] - HS * ((us[x + 1] if x < CX - 1 else right) - us[x])
        hz = hz1[rows(x), :]
        hy = hypp[rows(x), :]
        curl = (hz - y_down(hz, hz1m[x:x + 1, :])) - (hy - z_down(hy))
        dx2_s[rows(x), :] = v[rows(x), :] * ex1[rows(x), :] + INV * curl
    copies = [pltpu.make_async_copy(ey2_s, e_o.at[1], sem.at[0]), pltpu.make_async_copy(hz2_s, h_o.at[2], sem.at[1]),
              pltpu.make_async_copy(ex2_s, e_o.at[0], sem.at[2]), pltpu.make_async_copy(hy2_s, h_o.at[1], sem.at[3])]
    copies[0].start()
    copies[1].start()
    for q in range(4):
        part = pl.ds(q * 64, 64)
        ex2 = z_solve(w[part, :], dx2_s[part, :])
        ex2_s[part, :] = ex2
        hy2_s[part, :] = hypp[part, :] - HS * (z_up(ex2) - ex2)
    copies[2].start()
    copies[3].start()
    for copy in copies:
        copy.wait()


def k5(m4, own, dz2, fy, hxpp, hs_c, hrs_c, hg_c, hrg_c, beg, deg, e_in, h_in, e_o, h_o, ez2_s, hx2_s, sem):
    at = lax.axis_index("gy") & 3
    me = lax.axis_index("gy") >> 2
    al, ga = incoming(4, me, lambda k: m4[4 * k] + m4[4 * k + 1] + m4[4 * k + 2] + m4[4 * k + 3], hs_c, hrs_c)
    left, right = interface(4, at, own[0], own[1], lambda k: m4[4 * me + k], hg_c, hrg_c, beg, deg, al, ga)
    us = block_solve([dz2[strided(y), :] for y in range(CY)], [fy[y] for y in range(CY)], left, right)
    for y in range(CY):
        ez2_s[strided(y), :] = us[y]
    first = pltpu.make_async_copy(ez2_s, e_o.at[2], sem.at[0])
    first.start()
    for x in range(CX):
        ez2 = ez2_s[rows(x), :]
        hx2_s[rows(x), :] = hxpp[rows(x), :] - HS * (y_up(ez2, right[x:x + 1]) - ez2)
    second = pltpu.make_async_copy(hx2_s, h_o.at[0], sem.at[1])
    second.start()
    first.wait()
    second.wait()


def call(kernel, shapes, args, scratch=(), hbm_in=(), hbm_out=(), alias=None):
    def spec(in_hbm):
        return pl.BlockSpec(memory_space=pltpu.HBM if in_hbm else pltpu.VMEM)
    return pl.pallas_call(
        kernel,
        out_shape=[jax.ShapeDtypeStruct(s, F32) for s in shapes],
        in_specs=[spec(k in hbm_in) for k in range(len(args))],
        out_specs=[spec(k in hbm_out) for k in range(len(shapes))],
        scratch_shapes=[pltpu.VMEM(s, F32) if isinstance(s, tuple) else s for s in scratch],
        input_output_aliases=alias or {},
        compiler_params=pltpu.CompilerParams(vmem_limit_bytes=12 << 20),
        name=kernel.__name__,
    )(*args)


def pair(message):
    return lax.ppermute(message, "gx", [(x, x ^ 1) for x in range(GX)])


def ring_z(message, d):
    pairs = [(2 * z + c, 2 * ((z + d) % 4) + c) for z in range(4) for c in range(2)]
    return lax.ppermute(message, "gx", pairs)


def ring_x(message, d):
    pairs = [(4 * y + x, 4 * y + (x + d) % 4) for y in range(4) for x in range(4)]
    return lax.ppermute(message, "gy", pairs)


def ring_y(message, d):
    pairs = [(4 * y + x, 4 * ((y + d) % 4) + x) for y in range(4) for x in range(4)]
    return lax.ppermute(message, "gy", pairs)


def exchange(message, axis):
    return lax.all_to_all(message, axis, split_axis=0, concat_axis=0, tiled=True)


FIELD = (CELLS, NZ)
FACE = (16, NZ)
LINE = (16, 16, NZ)


def body(e_fields, h_fields, material, permittivity, conductivity, electrode_cells, electrode_dest,
         target_cells, electrode_gain):
    e = e_fields.reshape(3, CELLS, NZ)
    h = h_fields.reshape(3, CELLS, NZ)
    mat = material.reshape(CELLS, NZ)
    row = (1, 128)
    dma = pltpu.SemaphoreType.DMA
    hbm = [pltpu.with_memory_space_constraint(a, pltpu.HBM) for a in (
        e, h, mat, permittivity, conductivity, electrode_cells.reshape(row),
        electrode_dest.reshape(row), target_cells.reshape(row), electrode_gain.reshape(row))]
    msg1, w, v, fx, bx = call(
        k1, [(C_ALL, NZ), FIELD, FIELD, LINE, LINE],
        hbm,
        scratch=[FIELD, FACE, FACE, pltpu.VMEM(FIELD, jnp.int32), pltpu.SMEM((8,), F32), pltpu.SMEM((8,), F32),
                 pltpu.VMEM(row, jnp.int32), pltpu.VMEM(row, jnp.int32), pltpu.VMEM(row, jnp.int32), row, dma((10,))],
        hbm_in=range(9))
    chain2 = [(2,) + FACE, (2,) + FACE, (3,) + FACE, (3,) + FACE]
    chain = [(4,) + FACE, (4,) + FACE, (5,) + FACE, (5,) + FACE]
    rc = pair(msg1)
    out = call(k1c, [(Z_HALO + Z_ROWS[d], NZ) for d in (1, 2, 3)] + [(Z_HALO, NZ), (2, 48, NZ)] + chain2, (msg1, rc))
    msgz, ownz, blkx, pstat = out[:3], out[3], out[4], out[5:]
    msgz, w1 = lax.optimization_barrier((msgz, w))
    rz = [ring_z(m, d) for d, m in enumerate(msgz, 1)]
    (fy, by, g, hyp, dz0, hxpp0, dy20, zx, zy) = call(
        k1b, [LINE, LINE, (3,) + FACE, FIELD, FIELD, FIELD, FIELD, (15,) + FACE, (15,) + FACE],
        (e, h, w1, v), scratch=[FIELD, FIELD, FIELD])
    out = call(
        k2, [(X_HALO + HALO[d], NZ) for d in (1, 2, 3)] + [
            (X_HALO, NZ), FIELD, FIELD, FACE] + chain + chain2,
        (rc, ownz, *rz, blkx, e, h, v, fy, by, g), scratch=[(4, 64, NZ), FIELD, (8, NZ), (4, 48, NZ)])
    msgx, (ownx, hzp, dx, hz_low), xsup, xgrp = out[:3], out[3:7], out[7:11], out[11:]
    rx = [ring_x(m, d) for d, m in enumerate(msgx, 1)]
    out = call(
        k2c, [(Y_HALO + HALO[d], NZ) for d in (1, 2, 3)] + [(Y_HALO, NZ), (4, 80, NZ)] + chain, (ownx, *rx))
    msgy, owny, blk, zstat = out[:3], out[3], out[4], out[5:]
    ry = [ring_y(m, d) for d, m in enumerate(msgy, 1)]
    out = call(
        k3, [(80, NZ)] + chain + chain + [(2,) + FACE, FIELD, FIELD, FACE, FIELD, FIELD, FIELD, FIELD, FIELD],
        (owny, *ry, rx[0], rx[2], blk, zstat[0], zstat[1], v, hzp, dx, fy, fx, bx, hz_low,
         hyp, dz0, hxpp0, dy20, zx, zy), scratch=[(4, 80, NZ)])
    msg3, sstat, gstat, tr = out[0], out[1:5], out[5:9], out[9]
    ex1, hz1, hz1m, inj, hxpp, hzpp, dz, dy2 = out[10:]
    rc3 = pair(msg3)
    msgz3 = call(k3b, [(48, NZ), (32, NZ), (32, NZ)], (msg3, rc3, *pstat, *xsup))
    got3 = (msg3, rc3, *[ring_z(m, d) for d, m in enumerate(msgz3, 1)], xsup[0], xsup[1], *xgrp)
    msg4, dz2, hypp, own2 = call(
        k4, [(GY, R4, NZ), FIELD, FIELD, (2,) + FACE],
        (*got3, v, dz, fx, fy, by, hyp, hxpp, inj, *zstat, *sstat, *gstat, tr), scratch=[(4,) + FACE])
    m4 = exchange(msg4, "gy")
    e_out, h_out = call(
        k4b, [(3,) + FIELD, (3,) + FIELD], (*got3, v, w, fx, ex1, hz1, hz1m, hypp, hzpp, dy2),
        scratch=[FIELD] * 5 + [(4,) + FACE, dma((4,))], hbm_out=(0, 1))
    e_out, h_out = call(
        k5, [(3,) + FIELD, (3,) + FIELD], (m4, own2, dz2, fy, hxpp, sstat[0], sstat[1], *gstat, e_out, h_out),
        scratch=[FIELD, FIELD, dma((2,))], hbm_in=(11, 12), hbm_out=(0, 1), alias={11: 0, 12: 1})
    return e_out.reshape(3, CX, CY, NZ), h_out.reshape(3, CX, CY, NZ)


def solution(mesh):
    in_specs = (
        P(None, "gx", "gy", None),
        P(None, "gx", "gy", None),
        P("gx", "gy", None),
        P(),
        P(),
        P(("gx", "gy")),
        P(("gx", "gy"), None),
        P(("gx", "gy")),
        P(("gx", "gy")),
    )
    out_specs = (P(None, "gx", "gy", None), P(None, "gx", "gy", None))
    return jax.shard_map(body, mesh=mesh, in_specs=in_specs, out_specs=out_specs, check_vma=False)
```

```python
import jax
import jax.numpy as jnp
from jax import lax
from jax.experimental import pallas as pl
from jax.experimental.pallas import tpu as pltpu
from jax.sharding import PartitionSpec as P

F32 = jnp.float32
BF16 = jnp.bfloat16
CX = 16
CY = 16
NZ = 128
CELLS = CX * CY
GX = 8
GY = 16
HS = 16.0
INV = 1.0 / 256.0

C_CODE, C_HALO, C_COEF, C_ALL = 256, 264, 296, 344
Z_CODE, Z_COEF, Z_HALO = 64, 72, 120
X_CODE, X_BLOCK, X_HALO = 64, 72, 152
Y_CODE, Y_BLOCK, Y_HALO = 64, 96, 176
HALO = (0, 32, 0, 16)
Z_ROWS = (0, 16, 0, 16)
R4 = 16


def iota(shape, dim):
    return lax.broadcasted_iota(jnp.int32, shape, dim)


def z_up(f):
    return jnp.where(iota(f.shape, 1) == NZ - 1, 0.0, pltpu.roll(f, NZ - 1, 1))


def z_down(f):
    return jnp.where(iota(f.shape, 1) == 0, 0.0, pltpu.roll(f, 1, 1))


def y_up(f, last):
    return jnp.where(iota(f.shape, 0) == CY - 1, last, pltpu.roll(f, CY - 1, 0))


def y_down(f, first):
    return jnp.where(iota(f.shape, 0) == 0, first, pltpu.roll(f, 1, 0))


def rows(x):
    return pl.ds(x * CY, CY)


def strided(y):
    return pl.ds(y, CX, stride=CY)


def z_solve(w, d):
    lane = iota(w.shape, 1)
    a = jnp.where(lane == 0, 0.0, 1.0)
    c = jnp.where(lane == NZ - 1, 0.0, 1.0)
    e = w + (2.0 - a - c)
    step = 1
    while step < NZ:
        rb = 1.0 / (e + a + c)
        eb = e * rb
        db = d * rb
        e = e + a * pltpu.roll(eb, step, 1) + c * pltpu.roll(eb, NZ - step, 1)
        d = d + a * pltpu.roll(db, step, 1) + c * pltpu.roll(db, NZ - step, 1)
        if 2 * step < NZ:
            a, c = a * pltpu.roll(a * rb, step, 1), c * pltpu.roll(c * rb, NZ - step, 1)
        step *= 2
    return d / e


def z_factors(w_ref, out, part):
    w = w_ref[part, :]
    lane = iota(w.shape, 1)
    a = jnp.where(lane == 0, 0.0, 1.0)
    c = jnp.where(lane == NZ - 1, 0.0, 1.0)
    e = w + (2.0 - a - c)
    for k in range(7):
        step = 1 << k
        rb = 1.0 / (e + a + c)
        low = a * pltpu.roll(rb, step, 1)
        high = c * pltpu.roll(rb, NZ - step, 1)
        out[2 * k, part, :], out[2 * k + 1, part, :] = low, high
        e = e + low * pltpu.roll(e, step, 1) + high * pltpu.roll(e, NZ - step, 1)
        if k < 6:
            a, c = low * pltpu.roll(a, step, 1), high * pltpu.roll(c, NZ - step, 1)
    out[14, part, :] = 1.0 / e


def z_apply(d, f, part):
    for k in range(7):
        step = 1 << k
        d = d + f[2 * k, part, :] * pltpu.roll(d, step, 1) + f[2 * k + 1, part, :] * pltpu.roll(d, NZ - step, 1)
    return d * f[14, part, :]


def pivots(ws):
    def sweep(seq):
        s, l = seq[0], None
        rf = 1.0 / (1.0 + 1.0 + s)
        out = [rf]
        l = rf
        for w in seq[1:]:
            s = w + s * rf
            rf = 1.0 / (1.0 + l + s)
            out.append(rf)
            l = l * rf
        return out, l
    fwd, link = sweep(ws)
    bwd, _ = sweep(ws[::-1])
    return fwd, bwd[::-1], link


def ends(ds, fwd, bwd):
    y = ds[0]
    b = ds[-1]
    n = len(ds)
    for k in range(1, n):
        y = ds[k] + fwd[k - 1] * y
        b = ds[n - 1 - k] + bwd[n - k] * b
    return b * bwd[0], y * fwd[n - 1]


def block_solve(ds, fwd, left, right):
    ys = [ds[0] + left]
    for k in range(1, len(ds)):
        ys.append(ds[k] + fwd[k - 1] * ys[-1])
    u = (ys[-1] + right) * fwd[-1]
    us = [u]
    for k in range(len(ds) - 2, -1, -1):
        u = (ys[k] + u) * fwd[k]
        us.append(u)
    return us[::-1]


def static_fold(n, g11, g1n, gnn, h_ref, hr_ref, be_ref, de_ref, be=None, de=None):
    zero = jnp.zeros((16, NZ), F32)
    be = zero if be is None else be
    de = zero if de is None else de
    be_ref[0] = be
    de_ref[n] = de
    for k in range(n):
        a1, a2, a3 = g11(k), g1n(k), gnn(k)
        h = a2 / (1.0 - a1 * be)
        be = a3 + a2 * h * be
        h_ref[k] = h
        be_ref[k + 1] = be
        j = n - 1 - k
        b1, b2, b3 = g11(j), g1n(j), gnn(j)
        hr = b2 / (1.0 - b3 * de)
        de = b1 + b2 * hr * de
        hr_ref[j] = hr
        de_ref[j] = de


def incoming(n, me, recv, h_ref, hr_ref, al=None, ga=None):
    zero = jnp.zeros((16, NZ), F32)
    al = zero if al is None else al
    ga = zero if ga is None else ga
    for k in range(n - 1):
        al = jnp.where(k < me, recv(k) + h_ref[k] * al, al)
        j = n - 1 - k
        ga = jnp.where(j > me, recv(j) + hr_ref[j] * ga, ga)
    return al, ga


def interface(n, me, own_m, own_n, recv, h_ref, hr_ref, be_ref, de_ref, al=None, ga=None):
    al, ga = incoming(n, me, recv, h_ref, hr_ref, al, ga)
    be, be1 = be_ref[me], be_ref[me + 1]
    de, de1 = de_ref[me], de_ref[me + 1]
    own_ga = own_n + hr_ref[me] * ga
    own_al = own_m + h_ref[me] * al
    left = (al + be * own_ga) / (1.0 - be * de)
    right = (ga + de1 * own_al) / (1.0 - be1 * de1)
    return left, right


def pair_terms(k, q1, q2, h_ref, hr_ref, be_ref, de_ref):
    return q2 + h_ref[k] * be_ref[k] * q1, q1 + hr_ref[k] * de_ref[k + 1] * q2


def place(buf, own_at, own, others):
    buf[own_at] = own
    for d, value in enumerate(others, 1):
        buf[(own_at + 4 - d) & 3] = value


def split_dot(sel, values):
    hi = values.astype(BF16)
    rest = values - hi.astype(F32)
    mid = rest.astype(BF16)
    low = (rest - mid.astype(F32)).astype(BF16)
    dims = (((1,), (0,)), ((), ()))

    def part(v):
        return lax.dot_general(sel, v, dims, preferred_element_type=F32)

    return part(hi) + part(mid) + part(low)


def k1(e_h, h_h, mat_h, perm_h, cond_h, cells_h, dest_h, tgt_h, gain_h, msg, w_o, v_o, fx_o, bx_o,
       ez, ey_first, hz_last, mat, perm, cond, cells, dest, tgt, gain, sem):
    copies = [
        pltpu.make_async_copy(src, dst, sem.at[k])
        for k, (src, dst) in enumerate([
            (perm_h, perm), (cond_h, cond), (mat_h, mat), (dest_h, dest), (cells_h, cells), (tgt_h, tgt),
            (gain_h, gain), (e_h.at[2], ez), (e_h.at[1, rows(0)], ey_first), (h_h.at[2, rows(CX - 1)], hz_last)])
    ]
    for copy in copies:
        copy.start()
    for copy in copies:
        copy.wait()
    ws = [(perm[k] + 8.0 * cond[k]) * (1.0 / 4096.0) for k in range(8)]
    vs = [(perm[k] - 8.0 * cond[k]) * (1.0 / 4096.0) for k in range(8)]

    def pick(table, bits):
        for bit in bits:
            table = [jnp.where(bit, table[2 * k + 1], table[2 * k]) for k in range(len(table) // 2)]
        return table[0]

    wx = []
    for x in range(CX):
        m = mat[rows(x), :]
        bits = [(m & 1) != 0, (m & 2) != 0, (m & 4) != 0]
        w = pick(ws, bits)
        w_o[rows(x), :] = w
        v_o[rows(x), :] = pick(vs, bits)
        wx.append(w)
    fwd, bwd, link = pivots(wx)
    for x in range(CX):
        fx_o[x] = fwd[x]
        bx_o[x] = bwd[x]
    to = dest[...]
    to_b = jnp.broadcast_to(to, (128, 128))
    same = (to_b.T == to_b) & (iota((128, 128), 0) < iota((128, 128), 1))
    rank = jnp.sum(same.astype(jnp.int32), axis=0, keepdims=True)
    lane_slot = rank * GY + (to & (GY - 1))
    dest_x = to >> 4
    hot = iota((CELLS, 128), 0) == dest_x * 32 + lane_slot
    slot_gain = jnp.sum(jnp.where(hot, gain[...], 0.0), axis=1, keepdims=True)
    from_cell = (iota((CELLS, 128), 0) == cells[...]).astype(BF16)
    nt = (((1,), (1,)), ((), ()))
    pickm = lax.dot_general(hot.astype(BF16), from_cell, nt, preferred_element_type=F32)
    vals = split_dot(pickm.astype(BF16), ez[...]) * slot_gain
    code_at = jnp.where(iota((8, 128), 0) == dest_x, (tgt[...] + 1).astype(F32), 0.0).astype(BF16)
    lane_hot = (iota((128, 128), 0) == lane_slot).astype(BF16)
    code = lax.dot_general(code_at, lane_hot, nt, preferred_element_type=F32)
    msg[0:CELLS, :] = vals
    msg[C_CODE:C_CODE + 8, :] = code
    msg[C_HALO:C_HALO + 16, :] = hz_last[...]
    msg[C_HALO + 16:C_HALO + 32, :] = ey_first[...]
    for f, face in enumerate((bwd[0], link, fwd[CX - 1])):
        msg[C_COEF + 16 * f:C_COEF + 16 * f + 16, :] = face


def k1c(own, rc, mz1, mz2, mz3, own_o, blk_o, h_o, hr_o, be_o, de_o):
    gx = lax.axis_index("gx")
    c = gx & 1
    z = gx >> 1
    blk_o[c] = own[C_COEF:C_ALL, :]
    blk_o[1 - c] = rc[C_COEF:C_ALL, :]
    static_fold(2, lambda k: blk_o[k, 0:16, :], lambda k: blk_o[k, 16:32, :], lambda k: blk_o[k, 32:48, :],
                h_o, hr_o, be_o, de_o)
    for d, ref in enumerate((own_o, mz1, mz2, mz3)):
        to = ((z + d) & 3) * 2 + c
        for r, src in enumerate((own, rc)):
            ref[32 * r:32 * r + 32, :] = src[pl.ds(pl.multiple_of(to * 32, 32), 32), :]
            ref[Z_CODE + r:Z_CODE + r + 1, :] = src[pl.ds(C_CODE + to, 1), :]
        ref[Z_CODE + 2:Z_CODE + 8, :] = jnp.zeros((6, NZ), F32)
        for f, face in enumerate((de_o[0], h_o[0] * h_o[1], be_o[2])):
            ref[Z_COEF + 16 * f:Z_COEF + 16 * f + 16, :] = face
    mz1[Z_HALO:Z_HALO + 16, :] = jnp.where(c == 1, own[C_HALO:C_HALO + 16, :], rc[C_HALO:C_HALO + 16, :])
    mz3[Z_HALO:Z_HALO + 16, :] = jnp.where(c == 0, own[C_HALO + 16:C_HALO + 32, :], rc[C_HALO + 16:C_HALO + 32, :])


def k1b(e, h, w, fy_o, by_o, g_o):
    ws = [w[strided(y), :] for y in range(CY)]
    fwd, bwd, link = pivots(ws)
    for y in range(CY):
        fy_o[y] = fwd[y]
        by_o[y] = bwd[y]
    g_o[0] = bwd[0]
    g_o[1] = link
    g_o[2] = fwd[CY - 1]


def k2a(e, h, w, v, hyp_o, dz_o, hxp_o, dy1_o, zf_o):
    prev_hyp = None
    prev_hz = None
    for x in range(CX):
        ez = e[2, rows(x), :]
        hx = h[0, rows(x), :]
        ex = e[0, rows(x), :]
        hz = h[2, rows(x), :]
        hxp = hx - HS * (y_up(ez, 0.0) - ez)
        hxp_o[rows(x), :] = hxp
        hyp = h[1, rows(x), :] - HS * (z_up(ex) - ex)
        hyp_o[rows(x), :] = hyp
        curl_z = hyp - (hx - y_down(hx, 0.0))
        curl_y = (hxp - z_down(hxp)) - hz
        if x > 0:
            curl_z = curl_z - prev_hyp
            curl_y = curl_y + prev_hz
        prev_hyp = hyp
        prev_hz = hz
        dz_o[rows(x), :] = v[rows(x), :] * ez + INV * curl_z
        dy1_o[rows(x), :] = v[rows(x), :] * e[1, rows(x), :] + INV * curl_y
    for q in range(4):
        z_factors(w, zf_o, pl.ds(q * 64, 64))


def k2b(v, hxp, dy1, zf, hxpp_o, dy2_o, ey1_s):
    for q in range(4):
        part = pl.ds(q * 64, 64)
        ey1_s[part, :] = z_apply(dy1[part, :], zf, part)
    for x in range(CX):
        ey1 = ey1_s[rows(x), :]
        dey1 = HS * (z_up(ey1) - ey1)
        hx1 = hxp[rows(x), :] + dey1
        hxpp_o[rows(x), :] = hx1 + dey1
        dy2_o[rows(x), :] = v[rows(x), :] * ey1 + INV * (hx1 - z_down(hx1))


def k2(rc, ownz, z1, z2, z3, blk, e, h, v, fy, by, g, mx1, mx2, mx3, own_o, hzp_o, dx_o, halo_o,
       h_o, hr_o, be_o, de_o, hg_o, hrg_o, beg_o, deg_o, vals_s, src_s, code_s, grp):
    gx = lax.axis_index("gx")
    me = lax.axis_index("gy")
    c = gx & 1
    z = gx >> 1
    hz_low = jnp.where(c == 1, rc[C_HALO:C_HALO + 16, :], z1[Z_HALO:Z_HALO + 16, :])
    ey_high = jnp.where(c == 0, rc[C_HALO + 16:C_HALO + 32, :], z3[Z_HALO:Z_HALO + 16, :])
    hz_low = jnp.where(gx > 0, hz_low, 0.0)
    ey_high = jnp.where(gx < GX - 1, ey_high, 0.0)
    halo_o[...] = hz_low
    for x in range(CX):
        ey = e[1, rows(x), :]
        ey_next = e[1, rows(x + 1), :] if x < CX - 1 else ey_high
        hzp = h[2, rows(x), :] - HS * (ey_next - ey)
        hzp_o[rows(x), :] = hzp
        hy = h[1, rows(x), :]
        curl = (hzp - y_down(hzp, 0.0)) - (hy - z_down(hy))
        dx_o[rows(x), :] = v[rows(x), :] * e[0, rows(x), :] + INV * curl
    bwd = [by[y] for y in range(CY)]
    fwd = [fy[y] for y in range(CY)]
    p1, p2 = ends([dx_o[strided(y), :] for y in range(CY)], fwd, bwd)
    t = -INV * hzp_o[strided(CY - 1), :]
    p2 = p2 + t
    for k, ref in enumerate((ownz, z1, z2, z3)):
        src_s[64 * k:64 * k + 64, :] = ref[0:64, :]
        code_s[2 * k:2 * k + 2, :] = ref[Z_CODE:Z_CODE + 2, :]
    for to in range(4):
        for r in range(2):
            for y in range(4):
                at = (r * 4 + y) * 8
                vals_s[to, at:at + 8, :] = src_s[pl.ds(r * GY + 4 * y + to, 8, stride=32), :]
    code = code_s[...]
    for d, ref in enumerate((own_o, mx1, mx2, mx3)):
        ref[0:64, :] = vals_s[(me + d) & 3]
        ref[X_CODE:X_CODE + 8, :] = code
        for f, face in enumerate((p1, p2, g[0], g[1], g[2])):
            ref[X_BLOCK + 16 * f:X_BLOCK + 16 * f + 16, :] = face
    mx1[X_HALO:X_HALO + 16, :] = h[0, strided(CY - 1), :]
    mx1[X_HALO + 16:X_HALO + 32, :] = t
    mx3[X_HALO:X_HALO + 16, :] = e[2, strided(0), :]
    place(grp, z, ownz[Z_COEF:Z_HALO, :], [r[Z_COEF:Z_HALO, :] for r in (z1, z2, z3)])
    static_fold(4, lambda k: grp[k, 0:16, :], lambda k: grp[k, 16:32, :], lambda k: grp[k, 32:48, :],
                h_o, hr_o, be_o, de_o)
    static_fold(2, lambda k: blk[k, 0:16, :], lambda k: blk[k, 16:32, :], lambda k: blk[k, 32:48, :],
                hg_o, hrg_o, beg_o, deg_o, be_o[z], de_o[z + 1])


def k2c(own, r1, r2, r3, my1, my2, my3, own_o, blk_o, h_o, hr_o, be_o, de_o):
    at = lax.axis_index("gy") & 3
    to = lax.axis_index("gy") >> 2
    srcs = (own, r1, r2, r3)
    place(blk_o, at, own[X_BLOCK:X_HALO, :], [r[X_BLOCK:X_HALO, :] for r in srcs[1:]])
    static_fold(4, lambda k: blk_o[k, 32:48, :], lambda k: blk_o[k, 48:64, :], lambda k: blk_o[k, 64:80, :],
                h_o, hr_o, be_o, de_o)
    terms = [pair_terms(k, blk_o[k, 0:16, :], blk_o[k, 16:32, :], h_o, hr_o, be_o, de_o) for k in range(4)]
    al, ga, link = terms[0][0], terms[3][1], h_o[0]
    for k in range(1, 4):
        al = terms[k][0] + h_o[k] * al
        ga = terms[3 - k][1] + hr_o[3 - k] * ga
        link = link * h_o[k]
    for d, ref in enumerate((own_o, my1, my2, my3)):
        y = (to + d) & 3
        for k, src in enumerate(srcs):
            for r in range(2):
                row = pl.multiple_of((r * 4 + y) * 8, 8)
                ref[(k * 2 + r) * 8:(k * 2 + r) * 8 + 8, :] = src[pl.ds(row, 8), :]
            ref[Y_CODE + k * 8:Y_CODE + k * 8 + 8, :] = src[X_CODE:X_CODE + 8, :]
        for f, face in enumerate((ga, al, de_o[0], link, be_o[4])):
            ref[Y_BLOCK + 16 * f:Y_BLOCK + 16 * f + 16, :] = face
    my1[Y_HALO:Y_HALO + 32, :] = r1[X_HALO:X_HALO + 32, :]
    my3[Y_HALO:Y_HALO + 16, :] = r3[X_HALO:X_HALO + 16, :]


def k3(own, s1, s2, s3, r1, r3, blk, h0, hr0, v, hzp, dx, fy, fx, bx, hz_low,
       hyp, dz0, hxpp0, dy20, zf,
       msg, hs_c, hrs_c, bes, des, hg_c, hrg_c, beg, deg, tr_o, ex1_o, hz1_o, hz1m_o, inj_o, hxpp_o, hzpp_o,
       dz_o, dy2_o, grp):
    gy = lax.axis_index("gy")
    at = gy & 3
    me = gy >> 2
    place(grp, me, own[Y_BLOCK:Y_HALO, :], [r[Y_BLOCK:Y_HALO, :] for r in (s1, s2, s3)])
    static_fold(4, lambda k: grp[k, 32:48, :], lambda k: grp[k, 48:64, :], lambda k: grp[k, 64:80, :],
                hs_c, hrs_c, bes, des)
    static_fold(4, lambda k: blk[k, 32:48, :], lambda k: blk[k, 48:64, :], lambda k: blk[k, 64:80, :],
                hg_c, hrg_c, beg, deg, bes[me], des[me + 1])

    def group_term(k):
        m, n = pair_terms(k, grp[k, 0:16, :], grp[k, 16:32, :], hs_c, hrs_c, bes, des)
        return jnp.where(k < me, m, n)

    def tile_term(k):
        m, n = pair_terms(k, blk[k, 0:16, :], blk[k, 16:32, :], hg_c, hrg_c, beg, deg)
        return jnp.where(k < at, m, n)

    al, ga = incoming(4, me, group_term, hs_c, hrs_c)
    own_m, own_n = pair_terms(at, blk[at, 0:16, :], blk[at, 16:32, :], hg_c, hrg_c, beg, deg)
    left, right = interface(4, at, own_m, own_n, tile_term, hg_c, hrg_c, beg, deg, al, ga)
    one = jnp.ones((16, NZ), F32)
    to_right, to_left = one, one
    for k in range(4):
        to_right = jnp.where(k > at, to_right * h0[k], to_right)
        to_left = jnp.where(k < at, to_left * hr0[k], to_left)
    tr_o[0] = to_right
    tr_o[1] = to_left
    us = block_solve([dx[strided(y), :] for y in range(CY)], [fy[y] for y in range(CY)], left, right)
    for y in range(CY):
        ex1_o[strided(y), :] = us[y]
    low = jnp.where(at > 0, r1[X_HALO:X_HALO + 32, :], s1[Y_HALO:Y_HALO + 32, :])
    high = jnp.where(at < 3, r3[X_HALO:X_HALO + 16, :], s3[Y_HALO:Y_HALO + 16, :])
    hz1m_o[...] = jnp.where(gy > 0, HS * (us[0] - left) - 240.0 * low[16:32], 0.0)
    hx_low = jnp.where(gy > 0, low[0:16], 0.0)
    ez_high = jnp.where(gy < GY - 1, high, 0.0)
    srcs = (own, s1, s2, s3)
    codes = jnp.concatenate([r[Y_CODE:Y_CODE + 32, :] for r in srcs], axis=0).astype(BF16)
    inj = None
    for r in range(2):
        lane = (iota((8, 128), 1) == r * GY + gy).astype(BF16)
        code_row = lax.dot_general(lane, codes, (((1,), (1,)), ((), ())), preferred_element_type=F32)[0:1]
        land = ((iota((CELLS, 128), 0) + 1).astype(F32) == code_row).astype(BF16)
        vals = jnp.concatenate(
            [ref[(k * 2 + r) * 8:(k * 2 + r) * 8 + 8, :] for ref in srcs for k in range(4)], axis=0)
        part = split_dot(land, vals)
        inj = part if inj is None else inj + part
    inj_o[...] = inj
    dz_o[...] = dz0[...] - INV * inj
    dz_o[strided(0), :] = dz_o[strided(0), :] + INV * hx_low
    c_h = -HS * ez_high
    c_e = z_apply(INV * (c_h - z_down(c_h)), zf, strided(CY - 1))
    c_d = HS * (z_up(c_e) - c_e)
    c_1 = c_h + c_d
    b_e = z_apply(INV * hz_low[...], zf, rows(0))
    b_d = HS * (z_up(b_e) - b_e)
    hxpp_o[...] = hxpp0[...]
    hxpp_o[rows(0), :] = hxpp_o[rows(0), :] + (b_d + b_d)
    hxpp_o[strided(CY - 1), :] = hxpp_o[strided(CY - 1), :] + (c_1 + c_d)
    prev = None
    for x in range(CX):
        ex1 = ex1_o[rows(x), :]
        dex1 = HS * (y_up(ex1, right[x:x + 1]) - ex1)
        hz1 = hzp[rows(x), :] + dex1
        hz1_o[rows(x), :] = hz1
        hzpp = hz1 + dex1
        hzpp_o[rows(x), :] = hzpp
        curl = prev - hzpp if x > 0 else -hzpp
        prev = hzpp
        dy2_o[rows(x), :] = dy20[rows(x), :] + INV * curl
    dy2_o[rows(0), :] = dy2_o[rows(0), :] + v[rows(0), :] * b_e + INV * (b_d - z_down(b_d))
    dy2_o[strided(CY - 1), :] = dy2_o[strided(CY - 1), :] + v[strided(CY - 1), :] * c_e + INV * (c_1 - z_down(c_1))
    fwd = [fx[x] for x in range(CX)]
    bwd = [bx[x] for x in range(CX)]
    tz = -INV * hyp[rows(CX - 1), :]
    p1, p2 = ends([dz_o[rows(x), :] for x in range(CX)], fwd, bwd)
    ty = INV * hzpp_o[rows(CX - 1), :]
    q1, q2 = ends([dy2_o[rows(x), :] for x in range(CX)], fwd, bwd)
    for f, face in enumerate((p1, p2 + tz, q1, q2 + ty, tz)):
        msg[16 * f:16 * f + 16, :] = face


def k3b(own, rc, h0, hr0, be0, de0, hs_c, hrs_c, bes, des, mz1, mz2, mz3):
    gx = lax.axis_index("gx")
    c = gx & 1
    z = gx >> 1
    terms = []
    for f in range(2):
        blocks = []
        for k in range(2):
            q1 = jnp.where(c == k, own[32 * f:32 * f + 16, :], rc[32 * f:32 * f + 16, :])
            q2 = jnp.where(c == k, own[32 * f + 16:32 * f + 32, :], rc[32 * f + 16:32 * f + 32, :])
            blocks.append(pair_terms(k, q1, q2, h0, hr0, be0, de0))
        last = blocks[1][0] + h0[1] * blocks[0][0]
        first = blocks[0][1] + hr0[0] * blocks[1][1]
        terms.append(pair_terms(z, first, last, hs_c, hrs_c, bes, des))
    for d, ref in enumerate((mz1, mz2, mz3), 1):
        up = ((z + d) & 3) > z
        for f in range(2):
            ref[16 * f:16 * f + 16, :] = jnp.where(up, terms[f][0], terms[f][1])
    mz1[32:48, :] = jnp.where(c == 1, own[64:80, :], rc[64:80, :])


def x_interface(f, own, rc, zs, hs_c, hrs_c, hg_c, hrg_c, beg, deg, buf):
    gx = lax.axis_index("gx")
    c = gx & 1
    z = gx >> 1
    place(buf, z, zs[0][16 * f:16 * f + 16, :], [r[16 * f:16 * f + 16, :] for r in zs])
    al, ga = incoming(4, z, lambda k: buf[k], hs_c, hrs_c)
    own_m, own_n = pair_terms(c, own[32 * f:32 * f + 16, :], own[32 * f + 16:32 * f + 32, :], hg_c, hrg_c, beg, deg)
    other = pair_terms(1 - c, rc[32 * f:32 * f + 16, :], rc[32 * f + 16:32 * f + 32, :], hg_c, hrg_c, beg, deg)
    return interface(2, c, own_m, own_n, lambda k: other[k], hg_c, hrg_c, beg, deg, al, ga)


def k4(own, rc, z1, z2, z3, hxs, hrxs, hxg, hrxg, bexg, dexg, v, dz, fx, fy, by, hyp, hxpp, inj,
       h0, hr0, be0, de0, hs_c, hrs_c, bes, des, hg_c, hrg_c, beg, deg, tr, msg, dz2_o, hypp_o, own_o, buf):
    gx = lax.axis_index("gx")
    at = lax.axis_index("gy") & 3
    me = lax.axis_index("gy") >> 2
    left, right = x_interface(0, own, rc, (z1, z2, z3), hxs, hrxs, hxg, hrxg, bexg, dexg, buf)
    us = block_solve([dz[rows(x), :] for x in range(CX)], [fx[x] for x in range(CX)], left, right)
    t = jnp.where((gx & 1) == 1, rc[64:80, :], z1[32:48, :])
    prev = jnp.where(gx > 0, HS * (us[0] - left) - 240.0 * t, 0.0)
    for x in range(CX):
        dez = HS * ((us[x + 1] if x < CX - 1 else right) - us[x])
        hy1 = hyp[rows(x), :] + dez
        hypp_o[rows(x), :] = hy1 + dez
        hx2 = hxpp[rows(x), :]
        curl = (hy1 - prev) - (hx2 - y_down(hx2, 0.0)) - inj[rows(x), :]
        prev = hy1
        dz2_o[rows(x), :] = v[rows(x), :] * us[x] + INV * curl
    p1, p2 = ends([dz2_o[strided(y), :] for y in range(CY)], [fy[y] for y in range(CY)], [by[y] for y in range(CY)])
    p2 = p2 + INV * hxpp[strided(CY - 1), :]
    m, n = pair_terms(at, p1, p2, hg_c, hrg_c, beg, deg)
    own_o[0], own_o[1] = m, n
    m0, n0 = pair_terms(at, p1, p2, h0, hr0, be0, de0)
    m0, n0 = tr[0] * m0, tr[1] * n0
    group_m, group_n = pair_terms(me, n0, m0, hs_c, hrs_c, bes, des)
    for d in range(GY):
        y, x = d // 4, d % 4
        msg[d] = jnp.where(y > me, group_m, jnp.where(y < me, group_n, jnp.where(x > at, m, n)))


def k4b(own, rc, z1, z2, z3, hxs, hrxs, hxg, hrxg, bexg, dexg, v, w, fx, ex1, hz1, hz1m, hypp, hzpp, dy2,
        e_o, h_o, ex2_s, ey2_s, hy2_s, hz2_s, dx2_s, buf, sem):
    left, right = x_interface(1, own, rc, (z1, z2, z3), hxs, hrxs, hxg, hrxg, bexg, dexg, buf)
    us = block_solve([dy2[rows(x), :] for x in range(CX)], [fx[x] for x in range(CX)], left, right)
    for x in range(CX):
        ey2_s[rows(x), :] = us[x]
        hz2_s[rows(x), :] = hzpp[rows(x), :] - HS * ((us[x + 1] if x < CX - 1 else right) - us[x])
        hz = hz1[rows(x), :]
        hy = hypp[rows(x), :]
        curl = (hz - y_down(hz, hz1m[x:x + 1, :])) - (hy - z_down(hy))
        dx2_s[rows(x), :] = v[rows(x), :] * ex1[rows(x), :] + INV * curl
    copies = [pltpu.make_async_copy(ey2_s, e_o.at[1], sem.at[0]), pltpu.make_async_copy(hz2_s, h_o.at[2], sem.at[1]),
              pltpu.make_async_copy(ex2_s, e_o.at[0], sem.at[2]), pltpu.make_async_copy(hy2_s, h_o.at[1], sem.at[3])]
    copies[0].start()
    copies[1].start()
    for q in range(4):
        part = pl.ds(q * 64, 64)
        ex2 = z_solve(w[part, :], dx2_s[part, :])
        ex2_s[part, :] = ex2
        hy2_s[part, :] = hypp[part, :] - HS * (z_up(ex2) - ex2)
    copies[2].start()
    copies[3].start()
    for copy in copies:
        copy.wait()


def k5(m4, own, dz2, fy, hxpp, hs_c, hrs_c, hg_c, hrg_c, beg, deg, e_in, h_in, e_o, h_o, ez2_s, hx2_s, sem):
    at = lax.axis_index("gy") & 3
    me = lax.axis_index("gy") >> 2
    al, ga = incoming(4, me, lambda k: m4[4 * k] + m4[4 * k + 1] + m4[4 * k + 2] + m4[4 * k + 3], hs_c, hrs_c)
    left, right = interface(4, at, own[0], own[1], lambda k: m4[4 * me + k], hg_c, hrg_c, beg, deg, al, ga)
    us = block_solve([dz2[strided(y), :] for y in range(CY)], [fy[y] for y in range(CY)], left, right)
    for y in range(CY):
        ez2_s[strided(y), :] = us[y]
    first = pltpu.make_async_copy(ez2_s, e_o.at[2], sem.at[0])
    first.start()
    for x in range(CX):
        ez2 = ez2_s[rows(x), :]
        hx2_s[rows(x), :] = hxpp[rows(x), :] - HS * (y_up(ez2, right[x:x + 1]) - ez2)
    second = pltpu.make_async_copy(hx2_s, h_o.at[0], sem.at[1])
    second.start()
    first.wait()
    second.wait()


def call(kernel, shapes, args, scratch=(), hbm_in=(), hbm_out=(), alias=None):
    def spec(in_hbm):
        return pl.BlockSpec(memory_space=pltpu.HBM if in_hbm else pltpu.VMEM)
    return pl.pallas_call(
        kernel,
        out_shape=[jax.ShapeDtypeStruct(s, F32) for s in shapes],
        in_specs=[spec(k in hbm_in) for k in range(len(args))],
        out_specs=[spec(k in hbm_out) for k in range(len(shapes))],
        scratch_shapes=[pltpu.VMEM(s, F32) if isinstance(s, tuple) else s for s in scratch],
        input_output_aliases=alias or {},
        compiler_params=pltpu.CompilerParams(vmem_limit_bytes=12 << 20),
        name=kernel.__name__,
    )(*args)


def pair(message):
    return lax.ppermute(message, "gx", [(x, x ^ 1) for x in range(GX)])


def ring_z(message, d):
    pairs = [(2 * z + c, 2 * ((z + d) % 4) + c) for z in range(4) for c in range(2)]
    return lax.ppermute(message, "gx", pairs)


def ring_x(message, d):
    pairs = [(4 * y + x, 4 * y + (x + d) % 4) for y in range(4) for x in range(4)]
    return lax.ppermute(message, "gy", pairs)


def ring_y(message, d):
    pairs = [(4 * y + x, 4 * ((y + d) % 4) + x) for y in range(4) for x in range(4)]
    return lax.ppermute(message, "gy", pairs)


def exchange(message, axis):
    return lax.all_to_all(message, axis, split_axis=0, concat_axis=0, tiled=True)


FIELD = (CELLS, NZ)
FACE = (16, NZ)
LINE = (16, 16, NZ)


def body(e_fields, h_fields, material, permittivity, conductivity, electrode_cells, electrode_dest,
         target_cells, electrode_gain):
    e = e_fields.reshape(3, CELLS, NZ)
    h = h_fields.reshape(3, CELLS, NZ)
    mat = material.reshape(CELLS, NZ)
    row = (1, 128)
    dma = pltpu.SemaphoreType.DMA
    hbm = [pltpu.with_memory_space_constraint(a, pltpu.HBM) for a in (
        e, h, mat, permittivity, conductivity, electrode_cells.reshape(row),
        electrode_dest.reshape(row), target_cells.reshape(row), electrode_gain.reshape(row))]
    msg1, w, v, fx, bx = call(
        k1, [(C_ALL, NZ), FIELD, FIELD, LINE, LINE],
        hbm,
        scratch=[FIELD, FACE, FACE, pltpu.VMEM(FIELD, jnp.int32), pltpu.SMEM((8,), F32), pltpu.SMEM((8,), F32),
                 pltpu.VMEM(row, jnp.int32), pltpu.VMEM(row, jnp.int32), pltpu.VMEM(row, jnp.int32), row, dma((10,))],
        hbm_in=range(9))
    chain2 = [(2,) + FACE, (2,) + FACE, (3,) + FACE, (3,) + FACE]
    chain = [(4,) + FACE, (4,) + FACE, (5,) + FACE, (5,) + FACE]
    rc = pair(msg1)
    out = call(k1c, [(Z_HALO + Z_ROWS[d], NZ) for d in (1, 2, 3)] + [(Z_HALO, NZ), (2, 48, NZ)] + chain2, (msg1, rc))
    msgz, ownz, blkx, pstat = out[:3], out[3], out[4], out[5:]
    msgz, w1 = lax.optimization_barrier((msgz, w))
    rz = [ring_z(m, d) for d, m in enumerate(msgz, 1)]
    fy, by, g = call(k1b, [LINE, LINE, (3,) + FACE], (e, h, w1))
    out = call(
        k2, [(X_HALO + HALO[d], NZ) for d in (1, 2, 3)] + [
            (X_HALO, NZ), FIELD, FIELD, FACE] + chain + chain2,
        (rc, ownz, *rz, blkx, e, h, v, fy, by, g), scratch=[(4, 64, NZ), FIELD, (8, NZ), (4, 48, NZ)])
    msgx, (ownx, hzp, dx, hz_low), xsup, xgrp = out[:3], out[3:7], out[7:11], out[11:]
    msgx, w2 = lax.optimization_barrier((msgx, w))
    rx = [ring_x(m, d) for d, m in enumerate(msgx, 1)]
    hyp, dz0, hxp, dy1, zf = call(k2a, [FIELD] * 4 + [(15,) + FIELD], (e, h, w2, v))
    out = call(
        k2c, [(Y_HALO + HALO[d], NZ) for d in (1, 2, 3)] + [(Y_HALO, NZ), (4, 80, NZ)] + chain, (ownx, *rx))
    msgy, owny, blk, zstat = out[:3], out[3], out[4], out[5:]
    msgy, zf1 = lax.optimization_barrier((msgy, zf))
    ry = [ring_y(m, d) for d, m in enumerate(msgy, 1)]
    hxpp0, dy20 = call(k2b, [FIELD, FIELD], (v, hxp, dy1, zf1), scratch=[FIELD])
    out = call(
        k3, [(80, NZ)] + chain + chain + [(2,) + FACE, FIELD, FIELD, FACE, FIELD, FIELD, FIELD, FIELD, FIELD],
        (owny, *ry, rx[0], rx[2], blk, zstat[0], zstat[1], v, hzp, dx, fy, fx, bx, hz_low,
         hyp, dz0, hxpp0, dy20, zf), scratch=[(4, 80, NZ)])
    msg3, sstat, gstat, tr = out[0], out[1:5], out[5:9], out[9]
    ex1, hz1, hz1m, inj, hxpp, hzpp, dz, dy2 = out[10:]
    rc3 = pair(msg3)
    msgz3 = call(k3b, [(48, NZ), (32, NZ), (32, NZ)], (msg3, rc3, *pstat, *xsup))
    got3 = (msg3, rc3, *[ring_z(m, d) for d, m in enumerate(msgz3, 1)], xsup[0], xsup[1], *xgrp)
    msg4, dz2, hypp, own2 = call(
        k4, [(GY, R4, NZ), FIELD, FIELD, (2,) + FACE],
        (*got3, v, dz, fx, fy, by, hyp, hxpp, inj, *zstat, *sstat, *gstat, tr), scratch=[(4,) + FACE])
    m4 = exchange(msg4, "gy")
    e_out, h_out = call(
        k4b, [(3,) + FIELD, (3,) + FIELD], (*got3, v, w, fx, ex1, hz1, hz1m, hypp, hzpp, dy2),
        scratch=[FIELD] * 5 + [(4,) + FACE, dma((4,))], hbm_out=(0, 1))
    e_out, h_out = call(
        k5, [(3,) + FIELD, (3,) + FIELD], (m4, own2, dz2, fy, hxpp, sstat[0], sstat[1], *gstat, e_out, h_out),
        scratch=[FIELD, FIELD, dma((2,))], hbm_in=(11, 12), hbm_out=(0, 1), alias={11: 0, 12: 1})
    return e_out.reshape(3, CX, CY, NZ), h_out.reshape(3, CX, CY, NZ)


def solution(mesh):
    in_specs = (
        P(None, "gx", "gy", None),
        P(None, "gx", "gy", None),
        P("gx", "gy", None),
        P(),
        P(),
        P(("gx", "gy")),
        P(("gx", "gy"), None),
        P(("gx", "gy")),
        P(("gx", "gy")),
    )
    out_specs = (P(None, "gx", "gy", None), P(None, "gx", "gy", None))
    return jax.shard_map(body, mesh=mesh, in_specs=in_specs, out_specs=out_specs, check_vma=False)
```

```python
import jax
import jax.numpy as jnp
from jax import lax
from jax.experimental import pallas as pl
from jax.experimental.pallas import tpu as pltpu
from jax.sharding import PartitionSpec as P

F32 = jnp.float32
BF16 = jnp.bfloat16
CX = 16
CY = 16
NZ = 128
CELLS = CX * CY
GX = 8
GY = 16
HS = 16.0
INV = 1.0 / 256.0

C_CODE, C_HALO, C_COEF, C_ALL = 256, 264, 296, 344
Z_CODE, Z_COEF, Z_HALO = 64, 72, 120
X_CODE, X_BLOCK, X_HALO = 64, 72, 152
Y_CODE, Y_BLOCK, Y_HALO = 64, 96, 176
HALO = (0, 32, 0, 16)
Z_ROWS = (0, 16, 0, 16)
R4 = 16


def iota(shape, dim):
    return lax.broadcasted_iota(jnp.int32, shape, dim)


def z_up(f):
    return jnp.where(iota(f.shape, 1) == NZ - 1, 0.0, pltpu.roll(f, NZ - 1, 1))


def z_down(f):
    return jnp.where(iota(f.shape, 1) == 0, 0.0, pltpu.roll(f, 1, 1))


def y_up(f, last):
    return jnp.where(iota(f.shape, 0) == CY - 1, last, pltpu.roll(f, CY - 1, 0))


def y_down(f, first):
    return jnp.where(iota(f.shape, 0) == 0, first, pltpu.roll(f, 1, 0))


def rows(x):
    return pl.ds(x * CY, CY)


def strided(y):
    return pl.ds(y, CX, stride=CY)


def z_solve(w, d):
    lane = iota(w.shape, 1)
    a = jnp.where(lane == 0, 0.0, 1.0)
    c = jnp.where(lane == NZ - 1, 0.0, 1.0)
    e = w + (2.0 - a - c)
    step = 1
    while step < NZ:
        rb = 1.0 / (e + a + c)
        eb = e * rb
        db = d * rb
        e = e + a * pltpu.roll(eb, step, 1) + c * pltpu.roll(eb, NZ - step, 1)
        d = d + a * pltpu.roll(db, step, 1) + c * pltpu.roll(db, NZ - step, 1)
        if 2 * step < NZ:
            a, c = a * pltpu.roll(a * rb, step, 1), c * pltpu.roll(c * rb, NZ - step, 1)
        step *= 2
    return d / e


def z_factors(w_ref, out, part):
    w = w_ref[part, :]
    lane = iota(w.shape, 1)
    a = jnp.where(lane == 0, 0.0, 1.0)
    c = jnp.where(lane == NZ - 1, 0.0, 1.0)
    e = w + (2.0 - a - c)
    for k in range(7):
        step = 1 << k
        rb = 1.0 / (e + a + c)
        low = a * pltpu.roll(rb, step, 1)
        high = c * pltpu.roll(rb, NZ - step, 1)
        out[2 * k, part, :], out[2 * k + 1, part, :] = low, high
        e = e + low * pltpu.roll(e, step, 1) + high * pltpu.roll(e, NZ - step, 1)
        if k < 6:
            a, c = low * pltpu.roll(a, step, 1), high * pltpu.roll(c, NZ - step, 1)
    out[14, part, :] = 1.0 / e


def z_apply(d, f, part):
    for k in range(7):
        step = 1 << k
        d = d + f[2 * k, part, :] * pltpu.roll(d, step, 1) + f[2 * k + 1, part, :] * pltpu.roll(d, NZ - step, 1)
    return d * f[14, part, :]


def pivots(ws):
    def sweep(seq):
        s, l = seq[0], None
        rf = 1.0 / (1.0 + 1.0 + s)
        out = [rf]
        l = rf
        for w in seq[1:]:
            s = w + s * rf
            rf = 1.0 / (1.0 + l + s)
            out.append(rf)
            l = l * rf
        return out, l
    fwd, link = sweep(ws)
    bwd, _ = sweep(ws[::-1])
    return fwd, bwd[::-1], link


def ends(ds, fwd, bwd):
    y = ds[0]
    b = ds[-1]
    n = len(ds)
    for k in range(1, n):
        y = ds[k] + fwd[k - 1] * y
        b = ds[n - 1 - k] + bwd[n - k] * b
    return b * bwd[0], y * fwd[n - 1]


def block_solve(ds, fwd, left, right):
    ys = [ds[0] + left]
    for k in range(1, len(ds)):
        ys.append(ds[k] + fwd[k - 1] * ys[-1])
    u = (ys[-1] + right) * fwd[-1]
    us = [u]
    for k in range(len(ds) - 2, -1, -1):
        u = (ys[k] + u) * fwd[k]
        us.append(u)
    return us[::-1]


def static_fold(n, g11, g1n, gnn, h_ref, hr_ref, be_ref, de_ref, be=None, de=None):
    zero = jnp.zeros((16, NZ), F32)
    be = zero if be is None else be
    de = zero if de is None else de
    be_ref[0] = be
    de_ref[n] = de
    for k in range(n):
        a1, a2, a3 = g11(k), g1n(k), gnn(k)
        h = a2 / (1.0 - a1 * be)
        be = a3 + a2 * h * be
        h_ref[k] = h
        be_ref[k + 1] = be
        j = n - 1 - k
        b1, b2, b3 = g11(j), g1n(j), gnn(j)
        hr = b2 / (1.0 - b3 * de)
        de = b1 + b2 * hr * de
        hr_ref[j] = hr
        de_ref[j] = de


def incoming(n, me, recv, h_ref, hr_ref, al=None, ga=None):
    zero = jnp.zeros((16, NZ), F32)
    al = zero if al is None else al
    ga = zero if ga is None else ga
    for k in range(n - 1):
        al = jnp.where(k < me, recv(k) + h_ref[k] * al, al)
        j = n - 1 - k
        ga = jnp.where(j > me, recv(j) + hr_ref[j] * ga, ga)
    return al, ga


def interface(n, me, own_m, own_n, recv, h_ref, hr_ref, be_ref, de_ref, al=None, ga=None):
    al, ga = incoming(n, me, recv, h_ref, hr_ref, al, ga)
    be, be1 = be_ref[me], be_ref[me + 1]
    de, de1 = de_ref[me], de_ref[me + 1]
    own_ga = own_n + hr_ref[me] * ga
    own_al = own_m + h_ref[me] * al
    left = (al + be * own_ga) / (1.0 - be * de)
    right = (ga + de1 * own_al) / (1.0 - be1 * de1)
    return left, right


def pair_terms(k, q1, q2, h_ref, hr_ref, be_ref, de_ref):
    return q2 + h_ref[k] * be_ref[k] * q1, q1 + hr_ref[k] * de_ref[k + 1] * q2


def place(buf, own_at, own, others):
    buf[own_at] = own
    for d, value in enumerate(others, 1):
        buf[(own_at + 4 - d) & 3] = value


def split_dot(sel, values):
    hi = values.astype(BF16)
    rest = values - hi.astype(F32)
    mid = rest.astype(BF16)
    low = (rest - mid.astype(F32)).astype(BF16)
    dims = (((1,), (0,)), ((), ()))

    def part(v):
        return lax.dot_general(sel, v, dims, preferred_element_type=F32)

    return part(hi) + part(mid) + part(low)


def k1(e_h, h_h, mat_h, perm_h, cond_h, cells_h, dest_h, tgt_h, gain_h, msg, w_o, v_o, fx_o, bx_o, e_o, h_o,
       ez, ey_first, hz_last, mat, perm, cond, cells, dest, tgt, gain, sem):
    copies = [
        pltpu.make_async_copy(src, dst, sem.at[k])
        for k, (src, dst) in enumerate([
            (perm_h, perm), (cond_h, cond), (mat_h, mat), (dest_h, dest), (cells_h, cells), (tgt_h, tgt),
            (gain_h, gain), (e_h.at[2], ez), (e_h.at[1, rows(0)], ey_first), (h_h.at[2, rows(CX - 1)], hz_last)])
    ]
    whole = [pltpu.make_async_copy(e_h, e_o, sem.at[10]), pltpu.make_async_copy(h_h, h_o, sem.at[11])]
    for copy in copies + whole:
        copy.start()
    for copy in copies:
        copy.wait()
    ws = [(perm[k] + 8.0 * cond[k]) * (1.0 / 4096.0) for k in range(8)]
    vs = [(perm[k] - 8.0 * cond[k]) * (1.0 / 4096.0) for k in range(8)]

    def pick(table, bits):
        for bit in bits:
            table = [jnp.where(bit, table[2 * k + 1], table[2 * k]) for k in range(len(table) // 2)]
        return table[0]

    wx = []
    for x in range(CX):
        m = mat[rows(x), :]
        bits = [(m & 1) != 0, (m & 2) != 0, (m & 4) != 0]
        w = pick(ws, bits)
        w_o[rows(x), :] = w
        v_o[rows(x), :] = pick(vs, bits)
        wx.append(w)
    fwd, bwd, link = pivots(wx)
    for x in range(CX):
        fx_o[x] = fwd[x]
        bx_o[x] = bwd[x]
    to = dest[...]
    to_b = jnp.broadcast_to(to, (128, 128))
    same = (to_b.T == to_b) & (iota((128, 128), 0) < iota((128, 128), 1))
    rank = jnp.sum(same.astype(jnp.int32), axis=0, keepdims=True)
    lane_slot = rank * GY + (to & (GY - 1))
    dest_x = to >> 4
    hot = iota((CELLS, 128), 0) == dest_x * 32 + lane_slot
    slot_gain = jnp.sum(jnp.where(hot, gain[...], 0.0), axis=1, keepdims=True)
    from_cell = (iota((CELLS, 128), 0) == cells[...]).astype(BF16)
    nt = (((1,), (1,)), ((), ()))
    pickm = lax.dot_general(hot.astype(BF16), from_cell, nt, preferred_element_type=F32)
    vals = split_dot(pickm.astype(BF16), ez[...]) * slot_gain
    code_at = jnp.where(iota((8, 128), 0) == dest_x, (tgt[...] + 1).astype(F32), 0.0).astype(BF16)
    lane_hot = (iota((128, 128), 0) == lane_slot).astype(BF16)
    code = lax.dot_general(code_at, lane_hot, nt, preferred_element_type=F32)
    msg[0:CELLS, :] = vals
    msg[C_CODE:C_CODE + 8, :] = code
    msg[C_HALO:C_HALO + 16, :] = hz_last[...]
    msg[C_HALO + 16:C_HALO + 32, :] = ey_first[...]
    for f, face in enumerate((bwd[0], link, fwd[CX - 1])):
        msg[C_COEF + 16 * f:C_COEF + 16 * f + 16, :] = face
    for copy in whole:
        copy.wait()


def k1c(own, rc, mz1, mz2, mz3, own_o, blk_o, h_o, hr_o, be_o, de_o):
    gx = lax.axis_index("gx")
    c = gx & 1
    z = gx >> 1
    blk_o[c] = own[C_COEF:C_ALL, :]
    blk_o[1 - c] = rc[C_COEF:C_ALL, :]
    static_fold(2, lambda k: blk_o[k, 0:16, :], lambda k: blk_o[k, 16:32, :], lambda k: blk_o[k, 32:48, :],
                h_o, hr_o, be_o, de_o)
    for d, ref in enumerate((own_o, mz1, mz2, mz3)):
        to = ((z + d) & 3) * 2 + c
        for r, src in enumerate((own, rc)):
            ref[32 * r:32 * r + 32, :] = src[pl.ds(pl.multiple_of(to * 32, 32), 32), :]
            ref[Z_CODE + r:Z_CODE + r + 1, :] = src[pl.ds(C_CODE + to, 1), :]
        ref[Z_CODE + 2:Z_CODE + 8, :] = jnp.zeros((6, NZ), F32)
        for f, face in enumerate((de_o[0], h_o[0] * h_o[1], be_o[2])):
            ref[Z_COEF + 16 * f:Z_COEF + 16 * f + 16, :] = face
    mz1[Z_HALO:Z_HALO + 16, :] = jnp.where(c == 1, own[C_HALO:C_HALO + 16, :], rc[C_HALO:C_HALO + 16, :])
    mz3[Z_HALO:Z_HALO + 16, :] = jnp.where(c == 0, own[C_HALO + 16:C_HALO + 32, :], rc[C_HALO + 16:C_HALO + 32, :])


def k1b(w, fy_o, by_o, g_o):
    ws = [w[strided(y), :] for y in range(CY)]
    fwd, bwd, link = pivots(ws)
    for y in range(CY):
        fy_o[y] = fwd[y]
        by_o[y] = bwd[y]
    g_o[0] = bwd[0]
    g_o[1] = link
    g_o[2] = fwd[CY - 1]


def k2a(e, h, w, v, hyp_o, dz_o, hxp_o, dy1_o, zf_o):
    prev_hyp = None
    prev_hz = None
    for x in range(CX):
        ez = e[2, rows(x), :]
        hx = h[0, rows(x), :]
        ex = e[0, rows(x), :]
        hz = h[2, rows(x), :]
        hxp = hx - HS * (y_up(ez, 0.0) - ez)
        hxp_o[rows(x), :] = hxp
        hyp = h[1, rows(x), :] - HS * (z_up(ex) - ex)
        hyp_o[rows(x), :] = hyp
        curl_z = hyp - (hx - y_down(hx, 0.0))
        curl_y = (hxp - z_down(hxp)) - hz
        if x > 0:
            curl_z = curl_z - prev_hyp
            curl_y = curl_y + prev_hz
        prev_hyp = hyp
        prev_hz = hz
        dz_o[rows(x), :] = v[rows(x), :] * ez + INV * curl_z
        dy1_o[rows(x), :] = v[rows(x), :] * e[1, rows(x), :] + INV * curl_y
    for q in range(4):
        z_factors(w, zf_o, pl.ds(q * 64, 64))


def k2b(v, hxp, dy1, zf, hxpp_o, dy2_o, ey1_s):
    for q in range(4):
        part = pl.ds(q * 64, 64)
        ey1_s[part, :] = z_apply(dy1[part, :], zf, part)
    for x in range(CX):
        ey1 = ey1_s[rows(x), :]
        dey1 = HS * (z_up(ey1) - ey1)
        hx1 = hxp[rows(x), :] + dey1
        hxpp_o[rows(x), :] = hx1 + dey1
        dy2_o[rows(x), :] = v[rows(x), :] * ey1 + INV * (hx1 - z_down(hx1))


def k2(rc, ownz, z1, z2, z3, blk, e, h, v, fy, by, g, mx1, mx2, mx3, own_o, hzp_o, dx_o, halo_o,
       h_o, hr_o, be_o, de_o, hg_o, hrg_o, beg_o, deg_o, vals_s, src_s, code_s, grp):
    gx = lax.axis_index("gx")
    me = lax.axis_index("gy")
    c = gx & 1
    z = gx >> 1
    hz_low = jnp.where(c == 1, rc[C_HALO:C_HALO + 16, :], z1[Z_HALO:Z_HALO + 16, :])
    ey_high = jnp.where(c == 0, rc[C_HALO + 16:C_HALO + 32, :], z3[Z_HALO:Z_HALO + 16, :])
    hz_low = jnp.where(gx > 0, hz_low, 0.0)
    ey_high = jnp.where(gx < GX - 1, ey_high, 0.0)
    halo_o[...] = hz_low
    for x in range(CX):
        ey = e[1, rows(x), :]
        ey_next = e[1, rows(x + 1), :] if x < CX - 1 else ey_high
        hzp = h[2, rows(x), :] - HS * (ey_next - ey)
        hzp_o[rows(x), :] = hzp
        hy = h[1, rows(x), :]
        curl = (hzp - y_down(hzp, 0.0)) - (hy - z_down(hy))
        dx_o[rows(x), :] = v[rows(x), :] * e[0, rows(x), :] + INV * curl
    bwd = [by[y] for y in range(CY)]
    fwd = [fy[y] for y in range(CY)]
    p1, p2 = ends([dx_o[strided(y), :] for y in range(CY)], fwd, bwd)
    t = -INV * hzp_o[strided(CY - 1), :]
    p2 = p2 + t
    for k, ref in enumerate((ownz, z1, z2, z3)):
        src_s[64 * k:64 * k + 64, :] = ref[0:64, :]
        code_s[2 * k:2 * k + 2, :] = ref[Z_CODE:Z_CODE + 2, :]
    for to in range(4):
        for r in range(2):
            for y in range(4):
                at = (r * 4 + y) * 8
                vals_s[to, at:at + 8, :] = src_s[pl.ds(r * GY + 4 * y + to, 8, stride=32), :]
    code = code_s[...]
    for d, ref in enumerate((own_o, mx1, mx2, mx3)):
        ref[0:64, :] = vals_s[(me + d) & 3]
        ref[X_CODE:X_CODE + 8, :] = code
        for f, face in enumerate((p1, p2, g[0], g[1], g[2])):
            ref[X_BLOCK + 16 * f:X_BLOCK + 16 * f + 16, :] = face
    mx1[X_HALO:X_HALO + 16, :] = h[0, strided(CY - 1), :]
    mx1[X_HALO + 16:X_HALO + 32, :] = t
    mx3[X_HALO:X_HALO + 16, :] = e[2, strided(0), :]
    place(grp, z, ownz[Z_COEF:Z_HALO, :], [r[Z_COEF:Z_HALO, :] for r in (z1, z2, z3)])
    static_fold(4, lambda k: grp[k, 0:16, :], lambda k: grp[k, 16:32, :], lambda k: grp[k, 32:48, :],
                h_o, hr_o, be_o, de_o)
    static_fold(2, lambda k: blk[k, 0:16, :], lambda k: blk[k, 16:32, :], lambda k: blk[k, 32:48, :],
                hg_o, hrg_o, beg_o, deg_o, be_o[z], de_o[z + 1])


def k2c(own, r1, r2, r3, my1, my2, my3, own_o, blk_o, h_o, hr_o, be_o, de_o):
    at = lax.axis_index("gy") & 3
    to = lax.axis_index("gy") >> 2
    srcs = (own, r1, r2, r3)
    place(blk_o, at, own[X_BLOCK:X_HALO, :], [r[X_BLOCK:X_HALO, :] for r in srcs[1:]])
    static_fold(4, lambda k: blk_o[k, 32:48, :], lambda k: blk_o[k, 48:64, :], lambda k: blk_o[k, 64:80, :],
                h_o, hr_o, be_o, de_o)
    terms = [pair_terms(k, blk_o[k, 0:16, :], blk_o[k, 16:32, :], h_o, hr_o, be_o, de_o) for k in range(4)]
    al, ga, link = terms[0][0], terms[3][1], h_o[0]
    for k in range(1, 4):
        al = terms[k][0] + h_o[k] * al
        ga = terms[3 - k][1] + hr_o[3 - k] * ga
        link = link * h_o[k]
    for d, ref in enumerate((own_o, my1, my2, my3)):
        y = (to + d) & 3
        for k, src in enumerate(srcs):
            for r in range(2):
                row = pl.multiple_of((r * 4 + y) * 8, 8)
                ref[(k * 2 + r) * 8:(k * 2 + r) * 8 + 8, :] = src[pl.ds(row, 8), :]
            ref[Y_CODE + k * 8:Y_CODE + k * 8 + 8, :] = src[X_CODE:X_CODE + 8, :]
        for f, face in enumerate((ga, al, de_o[0], link, be_o[4])):
            ref[Y_BLOCK + 16 * f:Y_BLOCK + 16 * f + 16, :] = face
    my1[Y_HALO:Y_HALO + 32, :] = r1[X_HALO:X_HALO + 32, :]
    my3[Y_HALO:Y_HALO + 16, :] = r3[X_HALO:X_HALO + 16, :]


def k3(own, s1, s2, s3, r1, r3, blk, h0, hr0, v, hzp, dx, fy, fx, bx, hz_low,
       hyp, dz0, hxpp0, dy20, zf,
       msg, hs_c, hrs_c, bes, des, hg_c, hrg_c, beg, deg, tr_o, ex1_o, hz1_o, hz1m_o, inj_o, hxpp_o, hzpp_o,
       dz_o, dy2_o, grp):
    gy = lax.axis_index("gy")
    at = gy & 3
    me = gy >> 2
    place(grp, me, own[Y_BLOCK:Y_HALO, :], [r[Y_BLOCK:Y_HALO, :] for r in (s1, s2, s3)])
    static_fold(4, lambda k: grp[k, 32:48, :], lambda k: grp[k, 48:64, :], lambda k: grp[k, 64:80, :],
                hs_c, hrs_c, bes, des)
    static_fold(4, lambda k: blk[k, 32:48, :], lambda k: blk[k, 48:64, :], lambda k: blk[k, 64:80, :],
                hg_c, hrg_c, beg, deg, bes[me], des[me + 1])

    def group_term(k):
        m, n = pair_terms(k, grp[k, 0:16, :], grp[k, 16:32, :], hs_c, hrs_c, bes, des)
        return jnp.where(k < me, m, n)

    def tile_term(k):
        m, n = pair_terms(k, blk[k, 0:16, :], blk[k, 16:32, :], hg_c, hrg_c, beg, deg)
        return jnp.where(k < at, m, n)

    al, ga = incoming(4, me, group_term, hs_c, hrs_c)
    own_m, own_n = pair_terms(at, blk[at, 0:16, :], blk[at, 16:32, :], hg_c, hrg_c, beg, deg)
    left, right = interface(4, at, own_m, own_n, tile_term, hg_c, hrg_c, beg, deg, al, ga)
    one = jnp.ones((16, NZ), F32)
    to_right, to_left = one, one
    for k in range(4):
        to_right = jnp.where(k > at, to_right * h0[k], to_right)
        to_left = jnp.where(k < at, to_left * hr0[k], to_left)
    tr_o[0] = to_right
    tr_o[1] = to_left
    us = block_solve([dx[strided(y), :] for y in range(CY)], [fy[y] for y in range(CY)], left, right)
    for y in range(CY):
        ex1_o[strided(y), :] = us[y]
    low = jnp.where(at > 0, r1[X_HALO:X_HALO + 32, :], s1[Y_HALO:Y_HALO + 32, :])
    high = jnp.where(at < 3, r3[X_HALO:X_HALO + 16, :], s3[Y_HALO:Y_HALO + 16, :])
    hz1m_o[...] = jnp.where(gy > 0, HS * (us[0] - left) - 240.0 * low[16:32], 0.0)
    hx_low = jnp.where(gy > 0, low[0:16], 0.0)
    ez_high = jnp.where(gy < GY - 1, high, 0.0)
    srcs = (own, s1, s2, s3)
    codes = jnp.concatenate([r[Y_CODE:Y_CODE + 32, :] for r in srcs], axis=0).astype(BF16)
    inj = None
    for r in range(2):
        lane = (iota((8, 128), 1) == r * GY + gy).astype(BF16)
        code_row = lax.dot_general(lane, codes, (((1,), (1,)), ((), ())), preferred_element_type=F32)[0:1]
        land = ((iota((CELLS, 128), 0) + 1).astype(F32) == code_row).astype(BF16)
        vals = jnp.concatenate(
            [ref[(k * 2 + r) * 8:(k * 2 + r) * 8 + 8, :] for ref in srcs for k in range(4)], axis=0)
        part = split_dot(land, vals)
        inj = part if inj is None else inj + part
    inj_o[...] = inj
    dz_o[...] = dz0[...] - INV * inj
    dz_o[strided(0), :] = dz_o[strided(0), :] + INV * hx_low
    c_h = -HS * ez_high
    c_e = z_apply(INV * (c_h - z_down(c_h)), zf, strided(CY - 1))
    c_d = HS * (z_up(c_e) - c_e)
    c_1 = c_h + c_d
    b_e = z_apply(INV * hz_low[...], zf, rows(0))
    b_d = HS * (z_up(b_e) - b_e)
    hxpp_o[...] = hxpp0[...]
    hxpp_o[rows(0), :] = hxpp_o[rows(0), :] + (b_d + b_d)
    hxpp_o[strided(CY - 1), :] = hxpp_o[strided(CY - 1), :] + (c_1 + c_d)
    prev = None
    for x in range(CX):
        ex1 = ex1_o[rows(x), :]
        dex1 = HS * (y_up(ex1, right[x:x + 1]) - ex1)
        hz1 = hzp[rows(x), :] + dex1
        hz1_o[rows(x), :] = hz1
        hzpp = hz1 + dex1
        hzpp_o[rows(x), :] = hzpp
        curl = prev - hzpp if x > 0 else -hzpp
        prev = hzpp
        dy2_o[rows(x), :] = dy20[rows(x), :] + INV * curl
    dy2_o[rows(0), :] = dy2_o[rows(0), :] + v[rows(0), :] * b_e + INV * (b_d - z_down(b_d))
    dy2_o[strided(CY - 1), :] = dy2_o[strided(CY - 1), :] + v[strided(CY - 1), :] * c_e + INV * (c_1 - z_down(c_1))
    fwd = [fx[x] for x in range(CX)]
    bwd = [bx[x] for x in range(CX)]
    tz = -INV * hyp[rows(CX - 1), :]
    p1, p2 = ends([dz_o[rows(x), :] for x in range(CX)], fwd, bwd)
    ty = INV * hzpp_o[rows(CX - 1), :]
    q1, q2 = ends([dy2_o[rows(x), :] for x in range(CX)], fwd, bwd)
    for f, face in enumerate((p1, p2 + tz, q1, q2 + ty, tz)):
        msg[16 * f:16 * f + 16, :] = face


def k3b(own, rc, h0, hr0, be0, de0, hs_c, hrs_c, bes, des, mz1, mz2, mz3):
    gx = lax.axis_index("gx")
    c = gx & 1
    z = gx >> 1
    terms = []
    for f in range(2):
        blocks = []
        for k in range(2):
            q1 = jnp.where(c == k, own[32 * f:32 * f + 16, :], rc[32 * f:32 * f + 16, :])
            q2 = jnp.where(c == k, own[32 * f + 16:32 * f + 32, :], rc[32 * f + 16:32 * f + 32, :])
            blocks.append(pair_terms(k, q1, q2, h0, hr0, be0, de0))
        last = blocks[1][0] + h0[1] * blocks[0][0]
        first = blocks[0][1] + hr0[0] * blocks[1][1]
        terms.append(pair_terms(z, first, last, hs_c, hrs_c, bes, des))
    for d, ref in enumerate((mz1, mz2, mz3), 1):
        up = ((z + d) & 3) > z
        for f in range(2):
            ref[16 * f:16 * f + 16, :] = jnp.where(up, terms[f][0], terms[f][1])
    mz1[32:48, :] = jnp.where(c == 1, own[64:80, :], rc[64:80, :])


def x_interface(f, own, rc, zs, hs_c, hrs_c, hg_c, hrg_c, beg, deg, buf):
    gx = lax.axis_index("gx")
    c = gx & 1
    z = gx >> 1
    place(buf, z, zs[0][16 * f:16 * f + 16, :], [r[16 * f:16 * f + 16, :] for r in zs])
    al, ga = incoming(4, z, lambda k: buf[k], hs_c, hrs_c)
    own_m, own_n = pair_terms(c, own[32 * f:32 * f + 16, :], own[32 * f + 16:32 * f + 32, :], hg_c, hrg_c, beg, deg)
    other = pair_terms(1 - c, rc[32 * f:32 * f + 16, :], rc[32 * f + 16:32 * f + 32, :], hg_c, hrg_c, beg, deg)
    return interface(2, c, own_m, own_n, lambda k: other[k], hg_c, hrg_c, beg, deg, al, ga)


def k4(own, rc, z1, z2, z3, hxs, hrxs, hxg, hrxg, bexg, dexg, v, dz, fx, fy, by, hyp, hxpp, inj,
       h0, hr0, be0, de0, hs_c, hrs_c, bes, des, hg_c, hrg_c, beg, deg, tr, msg, dz2_o, hypp_o, own_o, buf):
    gx = lax.axis_index("gx")
    at = lax.axis_index("gy") & 3
    me = lax.axis_index("gy") >> 2
    left, right = x_interface(0, own, rc, (z1, z2, z3), hxs, hrxs, hxg, hrxg, bexg, dexg, buf)
    us = block_solve([dz[rows(x), :] for x in range(CX)], [fx[x] for x in range(CX)], left, right)
    t = jnp.where((gx & 1) == 1, rc[64:80, :], z1[32:48, :])
    prev = jnp.where(gx > 0, HS * (us[0] - left) - 240.0 * t, 0.0)
    for x in range(CX):
        dez = HS * ((us[x + 1] if x < CX - 1 else right) - us[x])
        hy1 = hyp[rows(x), :] + dez
        hypp_o[rows(x), :] = hy1 + dez
        hx2 = hxpp[rows(x), :]
        curl = (hy1 - prev) - (hx2 - y_down(hx2, 0.0)) - inj[rows(x), :]
        prev = hy1
        dz2_o[rows(x), :] = v[rows(x), :] * us[x] + INV * curl
    p1, p2 = ends([dz2_o[strided(y), :] for y in range(CY)], [fy[y] for y in range(CY)], [by[y] for y in range(CY)])
    p2 = p2 + INV * hxpp[strided(CY - 1), :]
    m, n = pair_terms(at, p1, p2, hg_c, hrg_c, beg, deg)
    own_o[0], own_o[1] = m, n
    m0, n0 = pair_terms(at, p1, p2, h0, hr0, be0, de0)
    m0, n0 = tr[0] * m0, tr[1] * n0
    group_m, group_n = pair_terms(me, n0, m0, hs_c, hrs_c, bes, des)
    for d in range(GY):
        y, x = d // 4, d % 4
        msg[d] = jnp.where(y > me, group_m, jnp.where(y < me, group_n, jnp.where(x > at, m, n)))


def k4b(own, rc, z1, z2, z3, hxs, hrxs, hxg, hrxg, bexg, dexg, v, w, fx, ex1, hz1, hz1m, hypp, hzpp, dy2,
        e_o, h_o, ex2_s, ey2_s, hy2_s, hz2_s, dx2_s, buf, sem):
    left, right = x_interface(1, own, rc, (z1, z2, z3), hxs, hrxs, hxg, hrxg, bexg, dexg, buf)
    us = block_solve([dy2[rows(x), :] for x in range(CX)], [fx[x] for x in range(CX)], left, right)
    for x in range(CX):
        ey2_s[rows(x), :] = us[x]
        hz2_s[rows(x), :] = hzpp[rows(x), :] - HS * ((us[x + 1] if x < CX - 1 else right) - us[x])
        hz = hz1[rows(x), :]
        hy = hypp[rows(x), :]
        curl = (hz - y_down(hz, hz1m[x:x + 1, :])) - (hy - z_down(hy))
        dx2_s[rows(x), :] = v[rows(x), :] * ex1[rows(x), :] + INV * curl
    copies = [pltpu.make_async_copy(ey2_s, e_o.at[1], sem.at[0]), pltpu.make_async_copy(hz2_s, h_o.at[2], sem.at[1]),
              pltpu.make_async_copy(ex2_s, e_o.at[0], sem.at[2]), pltpu.make_async_copy(hy2_s, h_o.at[1], sem.at[3])]
    copies[0].start()
    copies[1].start()
    for q in range(4):
        part = pl.ds(q * 64, 64)
        ex2 = z_solve(w[part, :], dx2_s[part, :])
        ex2_s[part, :] = ex2
        hy2_s[part, :] = hypp[part, :] - HS * (z_up(ex2) - ex2)
    copies[2].start()
    copies[3].start()
    for copy in copies:
        copy.wait()


def k5(m4, own, dz2, fy, hxpp, hs_c, hrs_c, hg_c, hrg_c, beg, deg, e_in, h_in, e_o, h_o, ez2_s, hx2_s, sem):
    at = lax.axis_index("gy") & 3
    me = lax.axis_index("gy") >> 2
    al, ga = incoming(4, me, lambda k: m4[4 * k] + m4[4 * k + 1] + m4[4 * k + 2] + m4[4 * k + 3], hs_c, hrs_c)
    left, right = interface(4, at, own[0], own[1], lambda k: m4[4 * me + k], hg_c, hrg_c, beg, deg, al, ga)
    us = block_solve([dz2[strided(y), :] for y in range(CY)], [fy[y] for y in range(CY)], left, right)
    for y in range(CY):
        ez2_s[strided(y), :] = us[y]
    first = pltpu.make_async_copy(ez2_s, e_o.at[2], sem.at[0])
    first.start()
    for x in range(CX):
        ez2 = ez2_s[rows(x), :]
        hx2_s[rows(x), :] = hxpp[rows(x), :] - HS * (y_up(ez2, right[x:x + 1]) - ez2)
    second = pltpu.make_async_copy(hx2_s, h_o.at[0], sem.at[1])
    second.start()
    first.wait()
    second.wait()


def call(kernel, shapes, args, scratch=(), hbm_in=(), hbm_out=(), alias=None):
    def spec(in_hbm):
        return pl.BlockSpec(memory_space=pltpu.HBM if in_hbm else pltpu.VMEM)
    return pl.pallas_call(
        kernel,
        out_shape=[jax.ShapeDtypeStruct(s, F32) for s in shapes],
        in_specs=[spec(k in hbm_in) for k in range(len(args))],
        out_specs=[spec(k in hbm_out) for k in range(len(shapes))],
        scratch_shapes=[pltpu.VMEM(s, F32) if isinstance(s, tuple) else s for s in scratch],
        input_output_aliases=alias or {},
        compiler_params=pltpu.CompilerParams(vmem_limit_bytes=12 << 20),
        name=kernel.__name__,
    )(*args)


def pair(message):
    return lax.ppermute(message, "gx", [(x, x ^ 1) for x in range(GX)])


def ring_z(message, d):
    pairs = [(2 * z + c, 2 * ((z + d) % 4) + c) for z in range(4) for c in range(2)]
    return lax.ppermute(message, "gx", pairs)


def ring_x(message, d):
    pairs = [(4 * y + x, 4 * y + (x + d) % 4) for y in range(4) for x in range(4)]
    return lax.ppermute(message, "gy", pairs)


def ring_y(message, d):
    pairs = [(4 * y + x, 4 * ((y + d) % 4) + x) for y in range(4) for x in range(4)]
    return lax.ppermute(message, "gy", pairs)


def exchange(message, axis):
    return lax.all_to_all(message, axis, split_axis=0, concat_axis=0, tiled=True)


FIELD = (CELLS, NZ)
FACE = (16, NZ)
LINE = (16, 16, NZ)


def body(e_fields, h_fields, material, permittivity, conductivity, electrode_cells, electrode_dest,
         target_cells, electrode_gain):
    e = e_fields.reshape(3, CELLS, NZ)
    h = h_fields.reshape(3, CELLS, NZ)
    mat = material.reshape(CELLS, NZ)
    row = (1, 128)
    dma = pltpu.SemaphoreType.DMA
    hbm = [pltpu.with_memory_space_constraint(a, pltpu.HBM) for a in (
        e, h, mat, permittivity, conductivity, electrode_cells.reshape(row),
        electrode_dest.reshape(row), target_cells.reshape(row), electrode_gain.reshape(row))]
    msg1, w, v, fx, bx, e, h = call(
        k1, [(C_ALL, NZ), FIELD, FIELD, LINE, LINE, (3,) + FIELD, (3,) + FIELD],
        hbm,
        scratch=[FIELD, FACE, FACE, pltpu.VMEM(FIELD, jnp.int32), pltpu.SMEM((8,), F32), pltpu.SMEM((8,), F32),
                 pltpu.VMEM(row, jnp.int32), pltpu.VMEM(row, jnp.int32), pltpu.VMEM(row, jnp.int32), row, dma((12,))],
        hbm_in=range(9))
    chain2 = [(2,) + FACE, (2,) + FACE, (3,) + FACE, (3,) + FACE]
    chain = [(4,) + FACE, (4,) + FACE, (5,) + FACE, (5,) + FACE]
    rc = pair(msg1)
    out = call(k1c, [(Z_HALO + Z_ROWS[d], NZ) for d in (1, 2, 3)] + [(Z_HALO, NZ), (2, 48, NZ)] + chain2, (msg1, rc))
    msgz, ownz, blkx, pstat = out[:3], out[3], out[4], out[5:]
    msgz, w1 = lax.optimization_barrier((msgz, w))
    rz = [ring_z(m, d) for d, m in enumerate(msgz, 1)]
    fy, by, g = call(k1b, [LINE, LINE, (3,) + FACE], (w1,))
    out = call(
        k2, [(X_HALO + HALO[d], NZ) for d in (1, 2, 3)] + [
            (X_HALO, NZ), FIELD, FIELD, FACE] + chain + chain2,
        (rc, ownz, *rz, blkx, e, h, v, fy, by, g), scratch=[(4, 64, NZ), FIELD, (8, NZ), (4, 48, NZ)])
    msgx, (ownx, hzp, dx, hz_low), xsup, xgrp = out[:3], out[3:7], out[7:11], out[11:]
    msgx, w2 = lax.optimization_barrier((msgx, w))
    rx = [ring_x(m, d) for d, m in enumerate(msgx, 1)]
    hyp, dz0, hxp, dy1, zf = call(k2a, [FIELD] * 4 + [(15,) + FIELD], (e, h, w2, v))
    out = call(
        k2c, [(Y_HALO + HALO[d], NZ) for d in (1, 2, 3)] + [(Y_HALO, NZ), (4, 80, NZ)] + chain, (ownx, *rx))
    msgy, owny, blk, zstat = out[:3], out[3], out[4], out[5:]
    msgy, zf1 = lax.optimization_barrier((msgy, zf))
    ry = [ring_y(m, d) for d, m in enumerate(msgy, 1)]
    hxpp0, dy20 = call(k2b, [FIELD, FIELD], (v, hxp, dy1, zf1), scratch=[FIELD])
    out = call(
        k3, [(80, NZ)] + chain + chain + [(2,) + FACE, FIELD, FIELD, FACE, FIELD, FIELD, FIELD, FIELD, FIELD],
        (owny, *ry, rx[0], rx[2], blk, zstat[0], zstat[1], v, hzp, dx, fy, fx, bx, hz_low,
         hyp, dz0, hxpp0, dy20, zf), scratch=[(4, 80, NZ)])
    msg3, sstat, gstat, tr = out[0], out[1:5], out[5:9], out[9]
    ex1, hz1, hz1m, inj, hxpp, hzpp, dz, dy2 = out[10:]
    rc3 = pair(msg3)
    msgz3 = call(k3b, [(48, NZ), (32, NZ), (32, NZ)], (msg3, rc3, *pstat, *xsup))
    got3 = (msg3, rc3, *[ring_z(m, d) for d, m in enumerate(msgz3, 1)], xsup[0], xsup[1], *xgrp)
    msg4, dz2, hypp, own2 = call(
        k4, [(GY, R4, NZ), FIELD, FIELD, (2,) + FACE],
        (*got3, v, dz, fx, fy, by, hyp, hxpp, inj, *zstat, *sstat, *gstat, tr), scratch=[(4,) + FACE])
    m4 = exchange(msg4, "gy")
    e_out, h_out = call(
        k4b, [(3,) + FIELD, (3,) + FIELD], (*got3, v, w, fx, ex1, hz1, hz1m, hypp, hzpp, dy2),
        scratch=[FIELD] * 5 + [(4,) + FACE, dma((4,))], hbm_out=(0, 1))
    e_out, h_out = call(
        k5, [(3,) + FIELD, (3,) + FIELD], (m4, own2, dz2, fy, hxpp, sstat[0], sstat[1], *gstat, e_out, h_out),
        scratch=[FIELD, FIELD, dma((2,))], hbm_in=(11, 12), hbm_out=(0, 1), alias={11: 0, 12: 1})
    return e_out.reshape(3, CX, CY, NZ), h_out.reshape(3, CX, CY, NZ)


def solution(mesh):
    in_specs = (
        P(None, "gx", "gy", None),
        P(None, "gx", "gy", None),
        P("gx", "gy", None),
        P(),
        P(),
        P(("gx", "gy")),
        P(("gx", "gy"), None),
        P(("gx", "gy")),
        P(("gx", "gy")),
    )
    out_specs = (P(None, "gx", "gy", None), P(None, "gx", "gy", None))
    return jax.shard_map(body, mesh=mesh, in_specs=in_specs, out_specs=out_specs, check_vma=False)
```

```python
import jax
import jax.numpy as jnp
from jax import lax
from jax.experimental import pallas as pl
from jax.experimental.pallas import tpu as pltpu
from jax.sharding import PartitionSpec as P

F32 = jnp.float32
BF16 = jnp.bfloat16
CX = 16
CY = 16
NZ = 128
CELLS = CX * CY
GX = 8
GY = 16
HS = 16.0
INV = 1.0 / 256.0

C_CODE, C_HALO, C_COEF, C_ALL = 256, 264, 296, 344
Z_CODE, Z_COEF, Z_HALO = 64, 72, 120
X_CODE, X_BLOCK, X_HALO = 64, 72, 152
Y_CODE, Y_BLOCK, Y_HALO = 64, 72, 152
HALO = (0, 32, 0, 16)
Z_ROWS = (0, 16, 0, 16)
R4 = 16


def iota(shape, dim):
    return lax.broadcasted_iota(jnp.int32, shape, dim)


def z_up(f):
    return jnp.where(iota(f.shape, 1) == NZ - 1, 0.0, pltpu.roll(f, NZ - 1, 1))


def z_down(f):
    return jnp.where(iota(f.shape, 1) == 0, 0.0, pltpu.roll(f, 1, 1))


def y_up(f, last):
    return jnp.where(iota(f.shape, 0) == CY - 1, last, pltpu.roll(f, CY - 1, 0))


def y_down(f, first):
    return jnp.where(iota(f.shape, 0) == 0, first, pltpu.roll(f, 1, 0))


def rows(x):
    return pl.ds(x * CY, CY)


def strided(y):
    return pl.ds(y, CX, stride=CY)


def z_solve(w, d):
    lane = iota(w.shape, 1)
    a = jnp.where(lane == 0, 0.0, 1.0)
    c = jnp.where(lane == NZ - 1, 0.0, 1.0)
    e = w + (2.0 - a - c)
    step = 1
    while step < NZ:
        rb = 1.0 / (e + a + c)
        eb = e * rb
        db = d * rb
        e = e + a * pltpu.roll(eb, step, 1) + c * pltpu.roll(eb, NZ - step, 1)
        d = d + a * pltpu.roll(db, step, 1) + c * pltpu.roll(db, NZ - step, 1)
        if 2 * step < NZ:
            a, c = a * pltpu.roll(a * rb, step, 1), c * pltpu.roll(c * rb, NZ - step, 1)
        step *= 2
    return d / e


def z_factors(w_ref, out, part):
    w = w_ref[part, :]
    lane = iota(w.shape, 1)
    a = jnp.where(lane == 0, 0.0, 1.0)
    c = jnp.where(lane == NZ - 1, 0.0, 1.0)
    e = w + (2.0 - a - c)
    for k in range(7):
        step = 1 << k
        rb = 1.0 / (e + a + c)
        low = a * pltpu.roll(rb, step, 1)
        high = c * pltpu.roll(rb, NZ - step, 1)
        out[2 * k, part, :], out[2 * k + 1, part, :] = low, high
        e = e + low * pltpu.roll(e, step, 1) + high * pltpu.roll(e, NZ - step, 1)
        if k < 6:
            a, c = low * pltpu.roll(a, step, 1), high * pltpu.roll(c, NZ - step, 1)
    out[14, part, :] = 1.0 / e


def z_apply(d, f, part):
    for k in range(7):
        step = 1 << k
        d = d + f[2 * k, part, :] * pltpu.roll(d, step, 1) + f[2 * k + 1, part, :] * pltpu.roll(d, NZ - step, 1)
    return d * f[14, part, :]


def pivots(ws):
    def sweep(seq):
        s, l = seq[0], None
        rf = 1.0 / (1.0 + 1.0 + s)
        out = [rf]
        l = rf
        for w in seq[1:]:
            s = w + s * rf
            rf = 1.0 / (1.0 + l + s)
            out.append(rf)
            l = l * rf
        return out, l
    fwd, link = sweep(ws)
    bwd, _ = sweep(ws[::-1])
    return fwd, bwd[::-1], link


def ends(ds, fwd, bwd):
    y = ds[0]
    b = ds[-1]
    n = len(ds)
    for k in range(1, n):
        y = ds[k] + fwd[k - 1] * y
        b = ds[n - 1 - k] + bwd[n - k] * b
    return b * bwd[0], y * fwd[n - 1]


def block_solve(ds, fwd, left, right):
    ys = [ds[0] + left]
    for k in range(1, len(ds)):
        ys.append(ds[k] + fwd[k - 1] * ys[-1])
    u = (ys[-1] + right) * fwd[-1]
    us = [u]
    for k in range(len(ds) - 2, -1, -1):
        u = (ys[k] + u) * fwd[k]
        us.append(u)
    return us[::-1]


def static_fold(n, g11, g1n, gnn, h_ref, hr_ref, be_ref, de_ref, be=None, de=None):
    zero = jnp.zeros((16, NZ), F32)
    be = zero if be is None else be
    de = zero if de is None else de
    be_ref[0] = be
    de_ref[n] = de
    for k in range(n):
        a1, a2, a3 = g11(k), g1n(k), gnn(k)
        h = a2 / (1.0 - a1 * be)
        be = a3 + a2 * h * be
        h_ref[k] = h
        be_ref[k + 1] = be
        j = n - 1 - k
        b1, b2, b3 = g11(j), g1n(j), gnn(j)
        hr = b2 / (1.0 - b3 * de)
        de = b1 + b2 * hr * de
        hr_ref[j] = hr
        de_ref[j] = de


def incoming(n, me, recv, h_ref, hr_ref, al=None, ga=None):
    zero = jnp.zeros((16, NZ), F32)
    al = zero if al is None else al
    ga = zero if ga is None else ga
    for k in range(n - 1):
        al = jnp.where(k < me, recv(k) + h_ref[k] * al, al)
        j = n - 1 - k
        ga = jnp.where(j > me, recv(j) + hr_ref[j] * ga, ga)
    return al, ga


def interface(n, me, own_m, own_n, recv, h_ref, hr_ref, be_ref, de_ref, al=None, ga=None):
    al, ga = incoming(n, me, recv, h_ref, hr_ref, al, ga)
    be, be1 = be_ref[me], be_ref[me + 1]
    de, de1 = de_ref[me], de_ref[me + 1]
    own_ga = own_n + hr_ref[me] * ga
    own_al = own_m + h_ref[me] * al
    left = (al + be * own_ga) / (1.0 - be * de)
    right = (ga + de1 * own_al) / (1.0 - be1 * de1)
    return left, right


def pair_terms(k, q1, q2, h_ref, hr_ref, be_ref, de_ref):
    return q2 + h_ref[k] * be_ref[k] * q1, q1 + hr_ref[k] * de_ref[k + 1] * q2


def place(buf, own_at, own, others):
    buf[own_at] = own
    for d, value in enumerate(others, 1):
        buf[(own_at + 4 - d) & 3] = value


def split_dot(sel, values):
    hi = values.astype(BF16)
    rest = values - hi.astype(F32)
    mid = rest.astype(BF16)
    low = (rest - mid.astype(F32)).astype(BF16)
    dims = (((1,), (0,)), ((), ()))

    def part(v):
        return lax.dot_general(sel, v, dims, preferred_element_type=F32)

    return part(hi) + part(mid) + part(low)


def k1(e_h, h_h, mat_h, perm_h, cond_h, cells_h, dest_h, tgt_h, gain_h, msg, w_o, v_o, fx_o, bx_o,
       ez, ey_first, hz_last, mat, perm, cond, cells, dest, tgt, gain, sem):
    copies = [
        pltpu.make_async_copy(src, dst, sem.at[k])
        for k, (src, dst) in enumerate([
            (perm_h, perm), (cond_h, cond), (mat_h, mat), (dest_h, dest), (cells_h, cells), (tgt_h, tgt),
            (gain_h, gain), (e_h.at[2], ez), (e_h.at[1, rows(0)], ey_first), (h_h.at[2, rows(CX - 1)], hz_last)])
    ]
    for copy in copies:
        copy.start()
    for copy in copies:
        copy.wait()
    ws = [(perm[k] + 8.0 * cond[k]) * (1.0 / 4096.0) for k in range(8)]
    vs = [(perm[k] - 8.0 * cond[k]) * (1.0 / 4096.0) for k in range(8)]

    def pick(table, bits):
        for bit in bits:
            table = [jnp.where(bit, table[2 * k + 1], table[2 * k]) for k in range(len(table) // 2)]
        return table[0]

    wx = []
    for x in range(CX):
        m = mat[rows(x), :]
        bits = [(m & 1) != 0, (m & 2) != 0, (m & 4) != 0]
        w = pick(ws, bits)
        w_o[rows(x), :] = w
        v_o[rows(x), :] = pick(vs, bits)
        wx.append(w)
    fwd, bwd, link = pivots(wx)
    for x in range(CX):
        fx_o[x] = fwd[x]
        bx_o[x] = bwd[x]
    to = dest[...]
    to_b = jnp.broadcast_to(to, (128, 128))
    same = (to_b.T == to_b) & (iota((128, 128), 0) < iota((128, 128), 1))
    rank = jnp.sum(same.astype(jnp.int32), axis=0, keepdims=True)
    lane_slot = rank * GY + (to & (GY - 1))
    dest_x = to >> 4
    hot = iota((CELLS, 128), 0) == dest_x * 32 + lane_slot
    slot_gain = jnp.sum(jnp.where(hot, gain[...], 0.0), axis=1, keepdims=True)
    from_cell = (iota((CELLS, 128), 0) == cells[...]).astype(BF16)
    nt = (((1,), (1,)), ((), ()))
    pickm = lax.dot_general(hot.astype(BF16), from_cell, nt, preferred_element_type=F32)
    vals = split_dot(pickm.astype(BF16), ez[...]) * slot_gain
    code_at = jnp.where(iota((8, 128), 0) == dest_x, (tgt[...] + 1).astype(F32), 0.0).astype(BF16)
    lane_hot = (iota((128, 128), 0) == lane_slot).astype(BF16)
    code = lax.dot_general(code_at, lane_hot, nt, preferred_element_type=F32)
    msg[0:CELLS, :] = vals
    msg[C_CODE:C_CODE + 8, :] = code
    msg[C_HALO:C_HALO + 16, :] = hz_last[...]
    msg[C_HALO + 16:C_HALO + 32, :] = ey_first[...]
    for f, face in enumerate((bwd[0], link, fwd[CX - 1])):
        msg[C_COEF + 16 * f:C_COEF + 16 * f + 16, :] = face


def k1c(own, rc, mz1, mz2, mz3, own_o, blk_o, h_o, hr_o, be_o, de_o):
    gx = lax.axis_index("gx")
    c = gx & 1
    z = gx >> 1
    blk_o[c] = own[C_COEF:C_ALL, :]
    blk_o[1 - c] = rc[C_COEF:C_ALL, :]
    static_fold(2, lambda k: blk_o[k, 0:16, :], lambda k: blk_o[k, 16:32, :], lambda k: blk_o[k, 32:48, :],
                h_o, hr_o, be_o, de_o)
    for d, ref in enumerate((own_o, mz1, mz2, mz3)):
        to = ((z + d) & 3) * 2 + c
        for r, src in enumerate((own, rc)):
            ref[32 * r:32 * r + 32, :] = src[pl.ds(pl.multiple_of(to * 32, 32), 32), :]
            ref[Z_CODE + r:Z_CODE + r + 1, :] = src[pl.ds(C_CODE + to, 1), :]
        ref[Z_CODE + 2:Z_CODE + 8, :] = jnp.zeros((6, NZ), F32)
        for f, face in enumerate((de_o[0], h_o[0] * h_o[1], be_o[2])):
            ref[Z_COEF + 16 * f:Z_COEF + 16 * f + 16, :] = face
    mz1[Z_HALO:Z_HALO + 16, :] = jnp.where(c == 1, own[C_HALO:C_HALO + 16, :], rc[C_HALO:C_HALO + 16, :])
    mz3[Z_HALO:Z_HALO + 16, :] = jnp.where(c == 0, own[C_HALO + 16:C_HALO + 32, :], rc[C_HALO + 16:C_HALO + 32, :])


def k1b(e, h, w, fy_o, by_o, g_o):
    ws = [w[strided(y), :] for y in range(CY)]
    fwd, bwd, link = pivots(ws)
    for y in range(CY):
        fy_o[y] = fwd[y]
        by_o[y] = bwd[y]
    g_o[0] = bwd[0]
    g_o[1] = link
    g_o[2] = fwd[CY - 1]


def k2a(e, h, w, v, hyp_o, dz_o, hxp_o, dy1_o, zf_o):
    prev_hyp = None
    prev_hz = None
    for x in range(CX):
        ez = e[2, rows(x), :]
        hx = h[0, rows(x), :]
        ex = e[0, rows(x), :]
        hz = h[2, rows(x), :]
        hxp = hx - HS * (y_up(ez, 0.0) - ez)
        hxp_o[rows(x), :] = hxp
        hyp = h[1, rows(x), :] - HS * (z_up(ex) - ex)
        hyp_o[rows(x), :] = hyp
        curl_z = hyp - (hx - y_down(hx, 0.0))
        curl_y = (hxp - z_down(hxp)) - hz
        if x > 0:
            curl_z = curl_z - prev_hyp
            curl_y = curl_y + prev_hz
        prev_hyp = hyp
        prev_hz = hz
        dz_o[rows(x), :] = v[rows(x), :] * ez + INV * curl_z
        dy1_o[rows(x), :] = v[rows(x), :] * e[1, rows(x), :] + INV * curl_y
    for q in range(4):
        z_factors(w, zf_o, pl.ds(q * 64, 64))


def k2b(v, hxp, dy1, zf, hxpp_o, dy2_o, ey1_s):
    for q in range(4):
        part = pl.ds(q * 64, 64)
        ey1_s[part, :] = z_apply(dy1[part, :], zf, part)
    for x in range(CX):
        ey1 = ey1_s[rows(x), :]
        dey1 = HS * (z_up(ey1) - ey1)
        hx1 = hxp[rows(x), :] + dey1
        hxpp_o[rows(x), :] = hx1 + dey1
        dy2_o[rows(x), :] = v[rows(x), :] * ey1 + INV * (hx1 - z_down(hx1))


def k2(rc, ownz, z1, z2, z3, blk, e, h, v, fy, by, g, mx1, mx2, mx3, own_o, hzp_o, dx_o, halo_o,
       h_o, hr_o, be_o, de_o, hg_o, hrg_o, beg_o, deg_o, vals_s, src_s, code_s, grp):
    gx = lax.axis_index("gx")
    me = lax.axis_index("gy")
    c = gx & 1
    z = gx >> 1
    hz_low = jnp.where(c == 1, rc[C_HALO:C_HALO + 16, :], z1[Z_HALO:Z_HALO + 16, :])
    ey_high = jnp.where(c == 0, rc[C_HALO + 16:C_HALO + 32, :], z3[Z_HALO:Z_HALO + 16, :])
    hz_low = jnp.where(gx > 0, hz_low, 0.0)
    ey_high = jnp.where(gx < GX - 1, ey_high, 0.0)
    halo_o[...] = hz_low
    for x in range(CX):
        ey = e[1, rows(x), :]
        ey_next = e[1, rows(x + 1), :] if x < CX - 1 else ey_high
        hzp = h[2, rows(x), :] - HS * (ey_next - ey)
        hzp_o[rows(x), :] = hzp
        hy = h[1, rows(x), :]
        curl = (hzp - y_down(hzp, 0.0)) - (hy - z_down(hy))
        dx_o[rows(x), :] = v[rows(x), :] * e[0, rows(x), :] + INV * curl
    bwd = [by[y] for y in range(CY)]
    fwd = [fy[y] for y in range(CY)]
    p1, p2 = ends([dx_o[strided(y), :] for y in range(CY)], fwd, bwd)
    t = -INV * hzp_o[strided(CY - 1), :]
    p2 = p2 + t
    for k, ref in enumerate((ownz, z1, z2, z3)):
        src_s[64 * k:64 * k + 64, :] = ref[0:64, :]
        code_s[2 * k:2 * k + 2, :] = ref[Z_CODE:Z_CODE + 2, :]
    for to in range(4):
        for r in range(2):
            for y in range(4):
                at = (r * 4 + y) * 8
                vals_s[to, at:at + 8, :] = src_s[pl.ds(r * GY + 4 * y + to, 8, stride=32), :]
    code = code_s[...]
    for d, ref in enumerate((own_o, mx1, mx2, mx3)):
        ref[0:64, :] = vals_s[(me + d) & 3]
        ref[X_CODE:X_CODE + 8, :] = code
        for f, face in enumerate((p1, p2, g[0], g[1], g[2])):
            ref[X_BLOCK + 16 * f:X_BLOCK + 16 * f + 16, :] = face
    mx1[X_HALO:X_HALO + 16, :] = h[0, strided(CY - 1), :]
    mx1[X_HALO + 16:X_HALO + 32, :] = t
    mx3[X_HALO:X_HALO + 16, :] = e[2, strided(0), :]
    place(grp, z, ownz[Z_COEF:Z_HALO, :], [r[Z_COEF:Z_HALO, :] for r in (z1, z2, z3)])
    static_fold(4, lambda k: grp[k, 0:16, :], lambda k: grp[k, 16:32, :], lambda k: grp[k, 32:48, :],
                h_o, hr_o, be_o, de_o)
    static_fold(2, lambda k: blk[k, 0:16, :], lambda k: blk[k, 16:32, :], lambda k: blk[k, 32:48, :],
                hg_o, hrg_o, beg_o, deg_o, be_o[z], de_o[z + 1])


def k2c(own, r1, r2, r3, my1, my2, my3, own_o, blk_o, h_o, hr_o, be_o, de_o):
    at = lax.axis_index("gy") & 3
    to = lax.axis_index("gy") >> 2
    srcs = (own, r1, r2, r3)
    place(blk_o, at, own[X_BLOCK:X_HALO, :], [r[X_BLOCK:X_HALO, :] for r in srcs[1:]])
    static_fold(4, lambda k: blk_o[k, 32:48, :], lambda k: blk_o[k, 48:64, :], lambda k: blk_o[k, 64:80, :],
                h_o, hr_o, be_o, de_o)
    terms = [pair_terms(k, blk_o[k, 0:16, :], blk_o[k, 16:32, :], h_o, hr_o, be_o, de_o) for k in range(4)]
    al, ga, link = terms[0][0], terms[3][1], h_o[0]
    for k in range(1, 4):
        al = terms[k][0] + h_o[k] * al
        ga = terms[3 - k][1] + hr_o[3 - k] * ga
        link = link * h_o[k]
    code = own[X_CODE:X_CODE + 8, :]
    for k in range(1, 4):
        code = code + pltpu.roll(srcs[k][X_CODE:X_CODE + 8, :], 32 * k, 1)
    for d, ref in enumerate((own_o, my1, my2, my3)):
        ref[Y_CODE:Y_CODE + 8, :] = code
        y = (to + d) & 3
        for k, src in enumerate(srcs):
            for r in range(2):
                row = pl.multiple_of((r * 4 + y) * 8, 8)
                ref[(k * 2 + r) * 8:(k * 2 + r) * 8 + 8, :] = src[pl.ds(row, 8), :]
        for f, face in enumerate((ga, al, de_o[0], link, be_o[4])):
            ref[Y_BLOCK + 16 * f:Y_BLOCK + 16 * f + 16, :] = face
    my1[Y_HALO:Y_HALO + 32, :] = r1[X_HALO:X_HALO + 32, :]
    my3[Y_HALO:Y_HALO + 16, :] = r3[X_HALO:X_HALO + 16, :]


def k3(own, s1, s2, s3, r1, r3, blk, h0, hr0, v, hzp, dx, fy, fx, bx, hz_low,
       hyp, dz0, hxpp0, dy20, zf,
       msg, hs_c, hrs_c, bes, des, hg_c, hrg_c, beg, deg, tr_o, ex1_o, hz1_o, hz1m_o, inj_o, hxpp_o, hzpp_o,
       dz_o, dy2_o, grp):
    gy = lax.axis_index("gy")
    at = gy & 3
    me = gy >> 2
    place(grp, me, own[Y_BLOCK:Y_HALO, :], [r[Y_BLOCK:Y_HALO, :] for r in (s1, s2, s3)])
    static_fold(4, lambda k: grp[k, 32:48, :], lambda k: grp[k, 48:64, :], lambda k: grp[k, 64:80, :],
                hs_c, hrs_c, bes, des)
    static_fold(4, lambda k: blk[k, 32:48, :], lambda k: blk[k, 48:64, :], lambda k: blk[k, 64:80, :],
                hg_c, hrg_c, beg, deg, bes[me], des[me + 1])

    def group_term(k):
        m, n = pair_terms(k, grp[k, 0:16, :], grp[k, 16:32, :], hs_c, hrs_c, bes, des)
        return jnp.where(k < me, m, n)

    def tile_term(k):
        m, n = pair_terms(k, blk[k, 0:16, :], blk[k, 16:32, :], hg_c, hrg_c, beg, deg)
        return jnp.where(k < at, m, n)

    al, ga = incoming(4, me, group_term, hs_c, hrs_c)
    own_m, own_n = pair_terms(at, blk[at, 0:16, :], blk[at, 16:32, :], hg_c, hrg_c, beg, deg)
    left, right = interface(4, at, own_m, own_n, tile_term, hg_c, hrg_c, beg, deg, al, ga)
    one = jnp.ones((16, NZ), F32)
    to_right, to_left = one, one
    for k in range(4):
        to_right = jnp.where(k > at, to_right * h0[k], to_right)
        to_left = jnp.where(k < at, to_left * hr0[k], to_left)
    tr_o[0] = to_right
    tr_o[1] = to_left
    us = block_solve([dx[strided(y), :] for y in range(CY)], [fy[y] for y in range(CY)], left, right)
    for y in range(CY):
        ex1_o[strided(y), :] = us[y]
    low = jnp.where(at > 0, r1[X_HALO:X_HALO + 32, :], s1[Y_HALO:Y_HALO + 32, :])
    high = jnp.where(at < 3, r3[X_HALO:X_HALO + 16, :], s3[Y_HALO:Y_HALO + 16, :])
    hz1m_o[...] = jnp.where(gy > 0, HS * (us[0] - left) - 240.0 * low[16:32], 0.0)
    hx_low = jnp.where(gy > 0, low[0:16], 0.0)
    ez_high = jnp.where(gy < GY - 1, high, 0.0)
    srcs = (own, s1, s2, s3)
    tile = iota((8, NZ), 1) >> 5
    codes = jnp.concatenate(
        [jnp.where(tile == k, ref[Y_CODE:Y_CODE + 8, :], 0.0) for k in range(4) for ref in srcs], axis=0).astype(BF16)
    inj = None
    for r in range(2):
        lane = ((iota((8, 128), 1) & 31) == r * GY + gy).astype(BF16)
        code_row = lax.dot_general(lane, codes, (((1,), (1,)), ((), ())), preferred_element_type=F32)[0:1]
        land = ((iota((CELLS, 128), 0) + 1).astype(F32) == code_row).astype(BF16)
        vals = jnp.concatenate(
            [ref[(k * 2 + r) * 8:(k * 2 + r) * 8 + 8, :] for k in range(4) for ref in srcs], axis=0)
        part = split_dot(land, vals)
        inj = part if inj is None else inj + part
    inj_o[...] = inj
    dz_o[...] = dz0[...] - INV * inj
    dz_o[strided(0), :] = dz_o[strided(0), :] + INV * hx_low
    c_h = -HS * ez_high
    c_e = z_apply(INV * (c_h - z_down(c_h)), zf, strided(CY - 1))
    c_d = HS * (z_up(c_e) - c_e)
    c_1 = c_h + c_d
    b_e = z_apply(INV * hz_low[...], zf, rows(0))
    b_d = HS * (z_up(b_e) - b_e)
    hxpp_o[...] = hxpp0[...]
    hxpp_o[rows(0), :] = hxpp_o[rows(0), :] + (b_d + b_d)
    hxpp_o[strided(CY - 1), :] = hxpp_o[strided(CY - 1), :] + (c_1 + c_d)
    prev = None
    for x in range(CX):
        ex1 = ex1_o[rows(x), :]
        dex1 = HS * (y_up(ex1, right[x:x + 1]) - ex1)
        hz1 = hzp[rows(x), :] + dex1
        hz1_o[rows(x), :] = hz1
        hzpp = hz1 + dex1
        hzpp_o[rows(x), :] = hzpp
        curl = prev - hzpp if x > 0 else -hzpp
        prev = hzpp
        dy2_o[rows(x), :] = dy20[rows(x), :] + INV * curl
    dy2_o[rows(0), :] = dy2_o[rows(0), :] + v[rows(0), :] * b_e + INV * (b_d - z_down(b_d))
    dy2_o[strided(CY - 1), :] = dy2_o[strided(CY - 1), :] + v[strided(CY - 1), :] * c_e + INV * (c_1 - z_down(c_1))
    fwd = [fx[x] for x in range(CX)]
    bwd = [bx[x] for x in range(CX)]
    tz = -INV * hyp[rows(CX - 1), :]
    p1, p2 = ends([dz_o[rows(x), :] for x in range(CX)], fwd, bwd)
    ty = INV * hzpp_o[rows(CX - 1), :]
    q1, q2 = ends([dy2_o[rows(x), :] for x in range(CX)], fwd, bwd)
    for f, face in enumerate((p1, p2 + tz, q1, q2 + ty, tz)):
        msg[16 * f:16 * f + 16, :] = face


def k3b(own, rc, h0, hr0, be0, de0, hs_c, hrs_c, bes, des, mz1, mz2, mz3):
    gx = lax.axis_index("gx")
    c = gx & 1
    z = gx >> 1
    terms = []
    for f in range(2):
        blocks = []
        for k in range(2):
            q1 = jnp.where(c == k, own[32 * f:32 * f + 16, :], rc[32 * f:32 * f + 16, :])
            q2 = jnp.where(c == k, own[32 * f + 16:32 * f + 32, :], rc[32 * f + 16:32 * f + 32, :])
            blocks.append(pair_terms(k, q1, q2, h0, hr0, be0, de0))
        last = blocks[1][0] + h0[1] * blocks[0][0]
        first = blocks[0][1] + hr0[0] * blocks[1][1]
        terms.append(pair_terms(z, first, last, hs_c, hrs_c, bes, des))
    for d, ref in enumerate((mz1, mz2, mz3), 1):
        up = ((z + d) & 3) > z
        for f in range(2):
            ref[16 * f:16 * f + 16, :] = jnp.where(up, terms[f][0], terms[f][1])
    mz1[32:48, :] = jnp.where(c == 1, own[64:80, :], rc[64:80, :])


def x_interface(f, own, rc, zs, hs_c, hrs_c, hg_c, hrg_c, beg, deg, buf):
    gx = lax.axis_index("gx")
    c = gx & 1
    z = gx >> 1
    place(buf, z, zs[0][16 * f:16 * f + 16, :], [r[16 * f:16 * f + 16, :] for r in zs])
    al, ga = incoming(4, z, lambda k: buf[k], hs_c, hrs_c)
    own_m, own_n = pair_terms(c, own[32 * f:32 * f + 16, :], own[32 * f + 16:32 * f + 32, :], hg_c, hrg_c, beg, deg)
    other = pair_terms(1 - c, rc[32 * f:32 * f + 16, :], rc[32 * f + 16:32 * f + 32, :], hg_c, hrg_c, beg, deg)
    return interface(2, c, own_m, own_n, lambda k: other[k], hg_c, hrg_c, beg, deg, al, ga)


def k4(own, rc, z1, z2, z3, hxs, hrxs, hxg, hrxg, bexg, dexg, v, dz, fx, fy, by, hyp, hxpp, inj,
       h0, hr0, be0, de0, hs_c, hrs_c, bes, des, hg_c, hrg_c, beg, deg, tr, msg, dz2_o, hypp_o, own_o, buf):
    gx = lax.axis_index("gx")
    at = lax.axis_index("gy") & 3
    me = lax.axis_index("gy") >> 2
    left, right = x_interface(0, own, rc, (z1, z2, z3), hxs, hrxs, hxg, hrxg, bexg, dexg, buf)
    us = block_solve([dz[rows(x), :] for x in range(CX)], [fx[x] for x in range(CX)], left, right)
    t = jnp.where((gx & 1) == 1, rc[64:80, :], z1[32:48, :])
    prev = jnp.where(gx > 0, HS * (us[0] - left) - 240.0 * t, 0.0)
    for x in range(CX):
        dez = HS * ((us[x + 1] if x < CX - 1 else right) - us[x])
        hy1 = hyp[rows(x), :] + dez
        hypp_o[rows(x), :] = hy1 + dez
        hx2 = hxpp[rows(x), :]
        curl = (hy1 - prev) - (hx2 - y_down(hx2, 0.0)) - inj[rows(x), :]
        prev = hy1
        dz2_o[rows(x), :] = v[rows(x), :] * us[x] + INV * curl
    p1, p2 = ends([dz2_o[strided(y), :] for y in range(CY)], [fy[y] for y in range(CY)], [by[y] for y in range(CY)])
    p2 = p2 + INV * hxpp[strided(CY - 1), :]
    m, n = pair_terms(at, p1, p2, hg_c, hrg_c, beg, deg)
    own_o[0], own_o[1] = m, n
    m0, n0 = pair_terms(at, p1, p2, h0, hr0, be0, de0)
    m0, n0 = tr[0] * m0, tr[1] * n0
    group_m, group_n = pair_terms(me, n0, m0, hs_c, hrs_c, bes, des)
    for d in range(GY):
        y, x = d // 4, d % 4
        msg[d] = jnp.where(y > me, group_m, jnp.where(y < me, group_n, jnp.where(x > at, m, n)))


def k4b(own, rc, z1, z2, z3, hxs, hrxs, hxg, hrxg, bexg, dexg, v, w, fx, ex1, hz1, hz1m, hypp, hzpp, dy2,
        e_o, h_o, ex2_s, ey2_s, hy2_s, hz2_s, dx2_s, buf, sem):
    left, right = x_interface(1, own, rc, (z1, z2, z3), hxs, hrxs, hxg, hrxg, bexg, dexg, buf)
    us = block_solve([dy2[rows(x), :] for x in range(CX)], [fx[x] for x in range(CX)], left, right)
    for x in range(CX):
        ey2_s[rows(x), :] = us[x]
        hz2_s[rows(x), :] = hzpp[rows(x), :] - HS * ((us[x + 1] if x < CX - 1 else right) - us[x])
        hz = hz1[rows(x), :]
        hy = hypp[rows(x), :]
        curl = (hz - y_down(hz, hz1m[x:x + 1, :])) - (hy - z_down(hy))
        dx2_s[rows(x), :] = v[rows(x), :] * ex1[rows(x), :] + INV * curl
    copies = [pltpu.make_async_copy(ey2_s, e_o.at[1], sem.at[0]), pltpu.make_async_copy(hz2_s, h_o.at[2], sem.at[1]),
              pltpu.make_async_copy(ex2_s, e_o.at[0], sem.at[2]), pltpu.make_async_copy(hy2_s, h_o.at[1], sem.at[3])]
    copies[0].start()
    copies[1].start()
    for q in range(4):
        part = pl.ds(q * 64, 64)
        ex2 = z_solve(w[part, :], dx2_s[part, :])
        ex2_s[part, :] = ex2
        hy2_s[part, :] = hypp[part, :] - HS * (z_up(ex2) - ex2)
    copies[2].start()
    copies[3].start()
    for copy in copies:
        copy.wait()


def k5(m4, own, dz2, fy, hxpp, hs_c, hrs_c, hg_c, hrg_c, beg, deg, e_in, h_in, e_o, h_o, ez2_s, hx2_s, sem):
    at = lax.axis_index("gy") & 3
    me = lax.axis_index("gy") >> 2
    al, ga = incoming(4, me, lambda k: m4[4 * k] + m4[4 * k + 1] + m4[4 * k + 2] + m4[4 * k + 3], hs_c, hrs_c)
    left, right = interface(4, at, own[0], own[1], lambda k: m4[4 * me + k], hg_c, hrg_c, beg, deg, al, ga)
    us = block_solve([dz2[strided(y), :] for y in range(CY)], [fy[y] for y in range(CY)], left, right)
    for y in range(CY):
        ez2_s[strided(y), :] = us[y]
    first = pltpu.make_async_copy(ez2_s, e_o.at[2], sem.at[0])
    first.start()
    for x in range(CX):
        ez2 = ez2_s[rows(x), :]
        hx2_s[rows(x), :] = hxpp[rows(x), :] - HS * (y_up(ez2, right[x:x + 1]) - ez2)
    second = pltpu.make_async_copy(hx2_s, h_o.at[0], sem.at[1])
    second.start()
    first.wait()
    second.wait()


def call(kernel, shapes, args, scratch=(), hbm_in=(), hbm_out=(), alias=None):
    def spec(in_hbm):
        return pl.BlockSpec(memory_space=pltpu.HBM if in_hbm else pltpu.VMEM)
    return pl.pallas_call(
        kernel,
        out_shape=[jax.ShapeDtypeStruct(s, F32) for s in shapes],
        in_specs=[spec(k in hbm_in) for k in range(len(args))],
        out_specs=[spec(k in hbm_out) for k in range(len(shapes))],
        scratch_shapes=[pltpu.VMEM(s, F32) if isinstance(s, tuple) else s for s in scratch],
        input_output_aliases=alias or {},
        compiler_params=pltpu.CompilerParams(vmem_limit_bytes=12 << 20),
        name=kernel.__name__,
    )(*args)


def pair(message):
    return lax.ppermute(message, "gx", [(x, x ^ 1) for x in range(GX)])


def ring_z(message, d):
    pairs = [(2 * z + c, 2 * ((z + d) % 4) + c) for z in range(4) for c in range(2)]
    return lax.ppermute(message, "gx", pairs)


def ring_x(message, d):
    pairs = [(4 * y + x, 4 * y + (x + d) % 4) for y in range(4) for x in range(4)]
    return lax.ppermute(message, "gy", pairs)


def ring_y(message, d):
    pairs = [(4 * y + x, 4 * ((y + d) % 4) + x) for y in range(4) for x in range(4)]
    return lax.ppermute(message, "gy", pairs)


def exchange(message, axis):
    return lax.all_to_all(message, axis, split_axis=0, concat_axis=0, tiled=True)


FIELD = (CELLS, NZ)
FACE = (16, NZ)
LINE = (16, 16, NZ)


def body(e_fields, h_fields, material, permittivity, conductivity, electrode_cells, electrode_dest,
         target_cells, electrode_gain):
    e = e_fields.reshape(3, CELLS, NZ)
    h = h_fields.reshape(3, CELLS, NZ)
    mat = material.reshape(CELLS, NZ)
    row = (1, 128)
    dma = pltpu.SemaphoreType.DMA
    hbm = [pltpu.with_memory_space_constraint(a, pltpu.HBM) for a in (
        e, h, mat, permittivity, conductivity, electrode_cells.reshape(row),
        electrode_dest.reshape(row), target_cells.reshape(row), electrode_gain.reshape(row))]
    msg1, w, v, fx, bx = call(
        k1, [(C_ALL, NZ), FIELD, FIELD, LINE, LINE],
        hbm,
        scratch=[FIELD, FACE, FACE, pltpu.VMEM(FIELD, jnp.int32), pltpu.SMEM((8,), F32), pltpu.SMEM((8,), F32),
                 pltpu.VMEM(row, jnp.int32), pltpu.VMEM(row, jnp.int32), pltpu.VMEM(row, jnp.int32), row, dma((10,))],
        hbm_in=range(9))
    chain2 = [(2,) + FACE, (2,) + FACE, (3,) + FACE, (3,) + FACE]
    chain = [(4,) + FACE, (4,) + FACE, (5,) + FACE, (5,) + FACE]
    rc = pair(msg1)
    out = call(k1c, [(Z_HALO + Z_ROWS[d], NZ) for d in (1, 2, 3)] + [(Z_HALO, NZ), (2, 48, NZ)] + chain2, (msg1, rc))
    msgz, ownz, blkx, pstat = out[:3], out[3], out[4], out[5:]
    msgz, w1 = lax.optimization_barrier((msgz, w))
    rz = [ring_z(m, d) for d, m in enumerate(msgz, 1)]
    fy, by, g = call(k1b, [LINE, LINE, (3,) + FACE], (e, h, w1))
    out = call(
        k2, [(X_HALO + HALO[d], NZ) for d in (1, 2, 3)] + [
            (X_HALO, NZ), FIELD, FIELD, FACE] + chain + chain2,
        (rc, ownz, *rz, blkx, e, h, v, fy, by, g), scratch=[(4, 64, NZ), FIELD, (8, NZ), (4, 48, NZ)])
    msgx, (ownx, hzp, dx, hz_low), xsup, xgrp = out[:3], out[3:7], out[7:11], out[11:]
    msgx, w2 = lax.optimization_barrier((msgx, w))
    rx = [ring_x(m, d) for d, m in enumerate(msgx, 1)]
    hyp, dz0, hxp, dy1, zf = call(k2a, [FIELD] * 4 + [(15,) + FIELD], (e, h, w2, v))
    out = call(
        k2c, [(Y_HALO + HALO[d], NZ) for d in (1, 2, 3)] + [(Y_HALO, NZ), (4, 80, NZ)] + chain, (ownx, *rx))
    msgy, owny, blk, zstat = out[:3], out[3], out[4], out[5:]
    msgy, zf1 = lax.optimization_barrier((msgy, zf))
    ry = [ring_y(m, d) for d, m in enumerate(msgy, 1)]
    hxpp0, dy20 = call(k2b, [FIELD, FIELD], (v, hxp, dy1, zf1), scratch=[FIELD])
    out = call(
        k3, [(80, NZ)] + chain + chain + [(2,) + FACE, FIELD, FIELD, FACE, FIELD, FIELD, FIELD, FIELD, FIELD],
        (owny, *ry, rx[0], rx[2], blk, zstat[0], zstat[1], v, hzp, dx, fy, fx, bx, hz_low,
         hyp, dz0, hxpp0, dy20, zf), scratch=[(4, 80, NZ)])
    msg3, sstat, gstat, tr = out[0], out[1:5], out[5:9], out[9]
    ex1, hz1, hz1m, inj, hxpp, hzpp, dz, dy2 = out[10:]
    rc3 = pair(msg3)
    msgz3 = call(k3b, [(48, NZ), (32, NZ), (32, NZ)], (msg3, rc3, *pstat, *xsup))
    got3 = (msg3, rc3, *[ring_z(m, d) for d, m in enumerate(msgz3, 1)], xsup[0], xsup[1], *xgrp)
    msg4, dz2, hypp, own2 = call(
        k4, [(GY, R4, NZ), FIELD, FIELD, (2,) + FACE],
        (*got3, v, dz, fx, fy, by, hyp, hxpp, inj, *zstat, *sstat, *gstat, tr), scratch=[(4,) + FACE])
    m4 = exchange(msg4, "gy")
    e_out, h_out = call(
        k4b, [(3,) + FIELD, (3,) + FIELD], (*got3, v, w, fx, ex1, hz1, hz1m, hypp, hzpp, dy2),
        scratch=[FIELD] * 5 + [(4,) + FACE, dma((4,))], hbm_out=(0, 1))
    e_out, h_out = call(
        k5, [(3,) + FIELD, (3,) + FIELD], (m4, own2, dz2, fy, hxpp, sstat[0], sstat[1], *gstat, e_out, h_out),
        scratch=[FIELD, FIELD, dma((2,))], hbm_in=(11, 12), hbm_out=(0, 1), alias={11: 0, 12: 1})
    return e_out.reshape(3, CX, CY, NZ), h_out.reshape(3, CX, CY, NZ)


def solution(mesh):
    in_specs = (
        P(None, "gx", "gy", None),
        P(None, "gx", "gy", None),
        P("gx", "gy", None),
        P(),
        P(),
        P(("gx", "gy")),
        P(("gx", "gy"), None),
        P(("gx", "gy")),
        P(("gx", "gy")),
    )
    out_specs = (P(None, "gx", "gy", None), P(None, "gx", "gy", None))
    return jax.shard_map(body, mesh=mesh, in_specs=in_specs, out_specs=out_specs, check_vma=False)
```

```python
import jax
import jax.numpy as jnp
from jax import lax
from jax.experimental import pallas as pl
from jax.experimental.pallas import tpu as pltpu
from jax.sharding import PartitionSpec as P

F32 = jnp.float32
BF16 = jnp.bfloat16
CX = 16
CY = 16
NZ = 128
CELLS = CX * CY
GX = 8
GY = 16
HS = 16.0
INV = 1.0 / 256.0

C_CODE, C_HALO, C_COEF, C_ALL = 256, 264, 296, 344
Z_CODE, Z_COEF, Z_HALO = 64, 72, 120
X_CODE, X_BLOCK, X_HALO = 64, 72, 152
Y_CODE, Y_BLOCK, Y_HALO = 64, 72, 152
HALO = (0, 32, 0, 16)
Z_ROWS = (0, 16, 0, 16)
R4 = 16


def iota(shape, dim):
    return lax.broadcasted_iota(jnp.int32, shape, dim)


def z_up(f):
    return jnp.where(iota(f.shape, 1) == NZ - 1, 0.0, pltpu.roll(f, NZ - 1, 1))


def z_down(f):
    return jnp.where(iota(f.shape, 1) == 0, 0.0, pltpu.roll(f, 1, 1))


def y_up(f, last):
    return jnp.where(iota(f.shape, 0) == CY - 1, last, pltpu.roll(f, CY - 1, 0))


def y_down(f, first):
    return jnp.where(iota(f.shape, 0) == 0, first, pltpu.roll(f, 1, 0))


def rows(x):
    return pl.ds(x * CY, CY)


def strided(y):
    return pl.ds(y, CX, stride=CY)


def z_solve(w, d):
    lane = iota(w.shape, 1)
    a = jnp.where(lane == 0, 0.0, 1.0)
    c = jnp.where(lane == NZ - 1, 0.0, 1.0)
    e = w + (2.0 - a - c)
    step = 1
    while step < NZ:
        rb = 1.0 / (e + a + c)
        eb = e * rb
        db = d * rb
        e = e + a * pltpu.roll(eb, step, 1) + c * pltpu.roll(eb, NZ - step, 1)
        d = d + a * pltpu.roll(db, step, 1) + c * pltpu.roll(db, NZ - step, 1)
        if 2 * step < NZ:
            a, c = a * pltpu.roll(a * rb, step, 1), c * pltpu.roll(c * rb, NZ - step, 1)
        step *= 2
    return d / e


def z_factors(w_ref, out, part):
    w = w_ref[part, :]
    lane = iota(w.shape, 1)
    a = jnp.where(lane == 0, 0.0, 1.0)
    c = jnp.where(lane == NZ - 1, 0.0, 1.0)
    e = w + (2.0 - a - c)
    for k in range(7):
        step = 1 << k
        rb = 1.0 / (e + a + c)
        low = a * pltpu.roll(rb, step, 1)
        high = c * pltpu.roll(rb, NZ - step, 1)
        out[2 * k, part, :], out[2 * k + 1, part, :] = low, high
        e = e + low * pltpu.roll(e, step, 1) + high * pltpu.roll(e, NZ - step, 1)
        if k < 6:
            a, c = low * pltpu.roll(a, step, 1), high * pltpu.roll(c, NZ - step, 1)
    out[14, part, :] = 1.0 / e


def z_apply(d, f, part):
    for k in range(7):
        step = 1 << k
        d = d + f[2 * k, part, :] * pltpu.roll(d, step, 1) + f[2 * k + 1, part, :] * pltpu.roll(d, NZ - step, 1)
    return d * f[14, part, :]


def pivots(ws):
    def sweep(seq):
        s, l = seq[0], None
        rf = 1.0 / (1.0 + 1.0 + s)
        out = [rf]
        l = rf
        for w in seq[1:]:
            s = w + s * rf
            rf = 1.0 / (1.0 + l + s)
            out.append(rf)
            l = l * rf
        return out, l
    fwd, link = sweep(ws)
    bwd, _ = sweep(ws[::-1])
    return fwd, bwd[::-1], link


def ends(ds, fwd, bwd):
    y = ds[0]
    b = ds[-1]
    n = len(ds)
    for k in range(1, n):
        y = ds[k] + fwd[k - 1] * y
        b = ds[n - 1 - k] + bwd[n - k] * b
    return b * bwd[0], y * fwd[n - 1]


def block_solve(ds, fwd, left, right):
    ys = [ds[0] + left]
    for k in range(1, len(ds)):
        ys.append(ds[k] + fwd[k - 1] * ys[-1])
    u = (ys[-1] + right) * fwd[-1]
    us = [u]
    for k in range(len(ds) - 2, -1, -1):
        u = (ys[k] + u) * fwd[k]
        us.append(u)
    return us[::-1]


def static_fold(n, g11, g1n, gnn, h_ref, hr_ref, be_ref, de_ref, be=None, de=None):
    zero = jnp.zeros((16, NZ), F32)
    be = zero if be is None else be
    de = zero if de is None else de
    be_ref[0] = be
    de_ref[n] = de
    for k in range(n):
        a1, a2, a3 = g11(k), g1n(k), gnn(k)
        h = a2 / (1.0 - a1 * be)
        be = a3 + a2 * h * be
        h_ref[k] = h
        be_ref[k + 1] = be
        j = n - 1 - k
        b1, b2, b3 = g11(j), g1n(j), gnn(j)
        hr = b2 / (1.0 - b3 * de)
        de = b1 + b2 * hr * de
        hr_ref[j] = hr
        de_ref[j] = de


def incoming(n, me, recv, h_ref, hr_ref, al=None, ga=None):
    zero = jnp.zeros((16, NZ), F32)
    al = zero if al is None else al
    ga = zero if ga is None else ga
    for k in range(n - 1):
        al = jnp.where(k < me, recv(k) + h_ref[k] * al, al)
        j = n - 1 - k
        ga = jnp.where(j > me, recv(j) + hr_ref[j] * ga, ga)
    return al, ga


def interface(n, me, own_m, own_n, recv, h_ref, hr_ref, be_ref, de_ref, al=None, ga=None):
    al, ga = incoming(n, me, recv, h_ref, hr_ref, al, ga)
    be, be1 = be_ref[me], be_ref[me + 1]
    de, de1 = de_ref[me], de_ref[me + 1]
    own_ga = own_n + hr_ref[me] * ga
    own_al = own_m + h_ref[me] * al
    left = (al + be * own_ga) / (1.0 - be * de)
    right = (ga + de1 * own_al) / (1.0 - be1 * de1)
    return left, right


def pair_terms(k, q1, q2, h_ref, hr_ref, be_ref, de_ref):
    return q2 + h_ref[k] * be_ref[k] * q1, q1 + hr_ref[k] * de_ref[k + 1] * q2


def place(buf, own_at, own, others):
    buf[own_at] = own
    for d, value in enumerate(others, 1):
        buf[(own_at + 4 - d) & 3] = value


def split_dot(sel, values):
    hi = values.astype(BF16)
    rest = values - hi.astype(F32)
    mid = rest.astype(BF16)
    low = (rest - mid.astype(F32)).astype(BF16)
    dims = (((1,), (0,)), ((), ()))

    def part(v):
        return lax.dot_general(sel, v, dims, preferred_element_type=F32)

    return part(hi) + part(mid) + part(low)


def k1(e_h, h_h, mat_h, perm_h, cond_h, cells_h, dest_h, tgt_h, gain_h, msg, w_o, v_o, fx_o, bx_o, e_o, h_o,
       ez, ey_first, hz_last, mat, perm, cond, cells, dest, tgt, gain, sem):
    copies = [
        pltpu.make_async_copy(src, dst, sem.at[k])
        for k, (src, dst) in enumerate([
            (perm_h, perm), (cond_h, cond), (mat_h, mat), (dest_h, dest), (cells_h, cells), (tgt_h, tgt),
            (gain_h, gain), (e_h.at[2], ez), (e_h.at[1, rows(0)], ey_first), (h_h.at[2, rows(CX - 1)], hz_last)])
    ]
    whole = [pltpu.make_async_copy(e_h, e_o, sem.at[10]), pltpu.make_async_copy(h_h, h_o, sem.at[11])]
    for copy in copies + whole:
        copy.start()
    for copy in copies:
        copy.wait()
    ws = [(perm[k] + 8.0 * cond[k]) * (1.0 / 4096.0) for k in range(8)]
    vs = [(perm[k] - 8.0 * cond[k]) * (1.0 / 4096.0) for k in range(8)]

    def pick(table, bits):
        for bit in bits:
            table = [jnp.where(bit, table[2 * k + 1], table[2 * k]) for k in range(len(table) // 2)]
        return table[0]

    wx = []
    for x in range(CX):
        m = mat[rows(x), :]
        bits = [(m & 1) != 0, (m & 2) != 0, (m & 4) != 0]
        w = pick(ws, bits)
        w_o[rows(x), :] = w
        v_o[rows(x), :] = pick(vs, bits)
        wx.append(w)
    fwd, bwd, link = pivots(wx)
    for x in range(CX):
        fx_o[x] = fwd[x]
        bx_o[x] = bwd[x]
    to = dest[...]
    to_b = jnp.broadcast_to(to, (128, 128))
    same = (to_b.T == to_b) & (iota((128, 128), 0) < iota((128, 128), 1))
    rank = jnp.sum(same.astype(jnp.int32), axis=0, keepdims=True)
    lane_slot = rank * GY + (to & (GY - 1))
    dest_x = to >> 4
    hot = iota((CELLS, 128), 0) == dest_x * 32 + lane_slot
    slot_gain = jnp.sum(jnp.where(hot, gain[...], 0.0), axis=1, keepdims=True)
    from_cell = (iota((CELLS, 128), 0) == cells[...]).astype(BF16)
    nt = (((1,), (1,)), ((), ()))
    pickm = lax.dot_general(hot.astype(BF16), from_cell, nt, preferred_element_type=F32)
    vals = split_dot(pickm.astype(BF16), ez[...]) * slot_gain
    code_at = jnp.where(iota((8, 128), 0) == dest_x, (tgt[...] + 1).astype(F32), 0.0).astype(BF16)
    lane_hot = (iota((128, 128), 0) == lane_slot).astype(BF16)
    code = lax.dot_general(code_at, lane_hot, nt, preferred_element_type=F32)
    msg[0:CELLS, :] = vals
    msg[C_CODE:C_CODE + 8, :] = code
    msg[C_HALO:C_HALO + 16, :] = hz_last[...]
    msg[C_HALO + 16:C_HALO + 32, :] = ey_first[...]
    for f, face in enumerate((bwd[0], link, fwd[CX - 1])):
        msg[C_COEF + 16 * f:C_COEF + 16 * f + 16, :] = face
    for copy in whole:
        copy.wait()


def k1c(own, rc, mz1, mz2, mz3, own_o, blk_o, h_o, hr_o, be_o, de_o):
    gx = lax.axis_index("gx")
    c = gx & 1
    z = gx >> 1
    blk_o[c] = own[C_COEF:C_ALL, :]
    blk_o[1 - c] = rc[C_COEF:C_ALL, :]
    static_fold(2, lambda k: blk_o[k, 0:16, :], lambda k: blk_o[k, 16:32, :], lambda k: blk_o[k, 32:48, :],
                h_o, hr_o, be_o, de_o)
    for d, ref in enumerate((own_o, mz1, mz2, mz3)):
        to = ((z + d) & 3) * 2 + c
        for r, src in enumerate((own, rc)):
            ref[32 * r:32 * r + 32, :] = src[pl.ds(pl.multiple_of(to * 32, 32), 32), :]
            ref[Z_CODE + r:Z_CODE + r + 1, :] = src[pl.ds(C_CODE + to, 1), :]
        ref[Z_CODE + 2:Z_CODE + 8, :] = jnp.zeros((6, NZ), F32)
        for f, face in enumerate((de_o[0], h_o[0] * h_o[1], be_o[2])):
            ref[Z_COEF + 16 * f:Z_COEF + 16 * f + 16, :] = face
    mz1[Z_HALO:Z_HALO + 16, :] = jnp.where(c == 1, own[C_HALO:C_HALO + 16, :], rc[C_HALO:C_HALO + 16, :])
    mz3[Z_HALO:Z_HALO + 16, :] = jnp.where(c == 0, own[C_HALO + 16:C_HALO + 32, :], rc[C_HALO + 16:C_HALO + 32, :])


def k1b(w, fy_o, by_o, g_o):
    ws = [w[strided(y), :] for y in range(CY)]
    fwd, bwd, link = pivots(ws)
    for y in range(CY):
        fy_o[y] = fwd[y]
        by_o[y] = bwd[y]
    g_o[0] = bwd[0]
    g_o[1] = link
    g_o[2] = fwd[CY - 1]


def k2a(e, h, w, v, hyp_o, dz_o, hxp_o, dy1_o, zf_o):
    prev_hyp = None
    prev_hz = None
    for x in range(CX):
        ez = e[2, rows(x), :]
        hx = h[0, rows(x), :]
        ex = e[0, rows(x), :]
        hz = h[2, rows(x), :]
        hxp = hx - HS * (y_up(ez, 0.0) - ez)
        hxp_o[rows(x), :] = hxp
        hyp = h[1, rows(x), :] - HS * (z_up(ex) - ex)
        hyp_o[rows(x), :] = hyp
        curl_z = hyp - (hx - y_down(hx, 0.0))
        curl_y = (hxp - z_down(hxp)) - hz
        if x > 0:
            curl_z = curl_z - prev_hyp
            curl_y = curl_y + prev_hz
        prev_hyp = hyp
        prev_hz = hz
        dz_o[rows(x), :] = v[rows(x), :] * ez + INV * curl_z
        dy1_o[rows(x), :] = v[rows(x), :] * e[1, rows(x), :] + INV * curl_y
    for q in range(4):
        z_factors(w, zf_o, pl.ds(q * 64, 64))


def k2b(v, hxp, dy1, zf, hxpp_o, dy2_o, ey1_s):
    for q in range(4):
        part = pl.ds(q * 64, 64)
        ey1_s[part, :] = z_apply(dy1[part, :], zf, part)
    for x in range(CX):
        ey1 = ey1_s[rows(x), :]
        dey1 = HS * (z_up(ey1) - ey1)
        hx1 = hxp[rows(x), :] + dey1
        hxpp_o[rows(x), :] = hx1 + dey1
        dy2_o[rows(x), :] = v[rows(x), :] * ey1 + INV * (hx1 - z_down(hx1))


def k2(rc, ownz, z1, z2, z3, blk, e, h, v, fy, by, g, mx1, mx2, mx3, own_o, hzp_o, dx_o, halo_o,
       h_o, hr_o, be_o, de_o, hg_o, hrg_o, beg_o, deg_o, vals_s, src_s, code_s, grp):
    gx = lax.axis_index("gx")
    me = lax.axis_index("gy")
    c = gx & 1
    z = gx >> 1
    hz_low = jnp.where(c == 1, rc[C_HALO:C_HALO + 16, :], z1[Z_HALO:Z_HALO + 16, :])
    ey_high = jnp.where(c == 0, rc[C_HALO + 16:C_HALO + 32, :], z3[Z_HALO:Z_HALO + 16, :])
    hz_low = jnp.where(gx > 0, hz_low, 0.0)
    ey_high = jnp.where(gx < GX - 1, ey_high, 0.0)
    halo_o[...] = hz_low
    for x in range(CX):
        ey = e[1, rows(x), :]
        ey_next = e[1, rows(x + 1), :] if x < CX - 1 else ey_high
        hzp = h[2, rows(x), :] - HS * (ey_next - ey)
        hzp_o[rows(x), :] = hzp
        hy = h[1, rows(x), :]
        curl = (hzp - y_down(hzp, 0.0)) - (hy - z_down(hy))
        dx_o[rows(x), :] = v[rows(x), :] * e[0, rows(x), :] + INV * curl
    bwd = [by[y] for y in range(CY)]
    fwd = [fy[y] for y in range(CY)]
    p1, p2 = ends([dx_o[strided(y), :] for y in range(CY)], fwd, bwd)
    t = -INV * hzp_o[strided(CY - 1), :]
    p2 = p2 + t
    for k, ref in enumerate((ownz, z1, z2, z3)):
        src_s[64 * k:64 * k + 64, :] = ref[0:64, :]
        code_s[2 * k:2 * k + 2, :] = ref[Z_CODE:Z_CODE + 2, :]
    for to in range(4):
        for r in range(2):
            for y in range(4):
                at = (r * 4 + y) * 8
                vals_s[to, at:at + 8, :] = src_s[pl.ds(r * GY + 4 * y + to, 8, stride=32), :]
    code = code_s[...]
    for d, ref in enumerate((own_o, mx1, mx2, mx3)):
        ref[0:64, :] = vals_s[(me + d) & 3]
        ref[X_CODE:X_CODE + 8, :] = code
        for f, face in enumerate((p1, p2, g[0], g[1], g[2])):
            ref[X_BLOCK + 16 * f:X_BLOCK + 16 * f + 16, :] = face
    mx1[X_HALO:X_HALO + 16, :] = h[0, strided(CY - 1), :]
    mx1[X_HALO + 16:X_HALO + 32, :] = t
    mx3[X_HALO:X_HALO + 16, :] = e[2, strided(0), :]
    place(grp, z, ownz[Z_COEF:Z_HALO, :], [r[Z_COEF:Z_HALO, :] for r in (z1, z2, z3)])
    static_fold(4, lambda k: grp[k, 0:16, :], lambda k: grp[k, 16:32, :], lambda k: grp[k, 32:48, :],
                h_o, hr_o, be_o, de_o)
    static_fold(2, lambda k: blk[k, 0:16, :], lambda k: blk[k, 16:32, :], lambda k: blk[k, 32:48, :],
                hg_o, hrg_o, beg_o, deg_o, be_o[z], de_o[z + 1])


def k2c(own, r1, r2, r3, my1, my2, my3, own_o, blk_o, h_o, hr_o, be_o, de_o):
    at = lax.axis_index("gy") & 3
    to = lax.axis_index("gy") >> 2
    srcs = (own, r1, r2, r3)
    place(blk_o, at, own[X_BLOCK:X_HALO, :], [r[X_BLOCK:X_HALO, :] for r in srcs[1:]])
    static_fold(4, lambda k: blk_o[k, 32:48, :], lambda k: blk_o[k, 48:64, :], lambda k: blk_o[k, 64:80, :],
                h_o, hr_o, be_o, de_o)
    terms = [pair_terms(k, blk_o[k, 0:16, :], blk_o[k, 16:32, :], h_o, hr_o, be_o, de_o) for k in range(4)]
    al, ga, link = terms[0][0], terms[3][1], h_o[0]
    for k in range(1, 4):
        al = terms[k][0] + h_o[k] * al
        ga = terms[3 - k][1] + hr_o[3 - k] * ga
        link = link * h_o[k]
    code = own[X_CODE:X_CODE + 8, :]
    for k in range(1, 4):
        code = code + pltpu.roll(srcs[k][X_CODE:X_CODE + 8, :], 32 * k, 1)
    for d, ref in enumerate((own_o, my1, my2, my3)):
        ref[Y_CODE:Y_CODE + 8, :] = code
        y = (to + d) & 3
        for k, src in enumerate(srcs):
            for r in range(2):
                row = pl.multiple_of((r * 4 + y) * 8, 8)
                ref[(k * 2 + r) * 8:(k * 2 + r) * 8 + 8, :] = src[pl.ds(row, 8), :]
        for f, face in enumerate((ga, al, de_o[0], link, be_o[4])):
            ref[Y_BLOCK + 16 * f:Y_BLOCK + 16 * f + 16, :] = face
    my1[Y_HALO:Y_HALO + 32, :] = r1[X_HALO:X_HALO + 32, :]
    my3[Y_HALO:Y_HALO + 16, :] = r3[X_HALO:X_HALO + 16, :]


def k3(own, s1, s2, s3, r1, r3, blk, h0, hr0, v, hzp, dx, fy, fx, bx, hz_low,
       hyp, dz0, hxpp0, dy20, zf,
       msg, hs_c, hrs_c, bes, des, hg_c, hrg_c, beg, deg, tr_o, ex1_o, hz1_o, hz1m_o, inj_o, hxpp_o, hzpp_o,
       dz_o, dy2_o, grp):
    gy = lax.axis_index("gy")
    at = gy & 3
    me = gy >> 2
    place(grp, me, own[Y_BLOCK:Y_HALO, :], [r[Y_BLOCK:Y_HALO, :] for r in (s1, s2, s3)])
    static_fold(4, lambda k: grp[k, 32:48, :], lambda k: grp[k, 48:64, :], lambda k: grp[k, 64:80, :],
                hs_c, hrs_c, bes, des)
    static_fold(4, lambda k: blk[k, 32:48, :], lambda k: blk[k, 48:64, :], lambda k: blk[k, 64:80, :],
                hg_c, hrg_c, beg, deg, bes[me], des[me + 1])

    def group_term(k):
        m, n = pair_terms(k, grp[k, 0:16, :], grp[k, 16:32, :], hs_c, hrs_c, bes, des)
        return jnp.where(k < me, m, n)

    def tile_term(k):
        m, n = pair_terms(k, blk[k, 0:16, :], blk[k, 16:32, :], hg_c, hrg_c, beg, deg)
        return jnp.where(k < at, m, n)

    al, ga = incoming(4, me, group_term, hs_c, hrs_c)
    own_m, own_n = pair_terms(at, blk[at, 0:16, :], blk[at, 16:32, :], hg_c, hrg_c, beg, deg)
    left, right = interface(4, at, own_m, own_n, tile_term, hg_c, hrg_c, beg, deg, al, ga)
    one = jnp.ones((16, NZ), F32)
    to_right, to_left = one, one
    for k in range(4):
        to_right = jnp.where(k > at, to_right * h0[k], to_right)
        to_left = jnp.where(k < at, to_left * hr0[k], to_left)
    tr_o[0] = to_right
    tr_o[1] = to_left
    us = block_solve([dx[strided(y), :] for y in range(CY)], [fy[y] for y in range(CY)], left, right)
    for y in range(CY):
        ex1_o[strided(y), :] = us[y]
    low = jnp.where(at > 0, r1[X_HALO:X_HALO + 32, :], s1[Y_HALO:Y_HALO + 32, :])
    high = jnp.where(at < 3, r3[X_HALO:X_HALO + 16, :], s3[Y_HALO:Y_HALO + 16, :])
    hz1m_o[...] = jnp.where(gy > 0, HS * (us[0] - left) - 240.0 * low[16:32], 0.0)
    hx_low = jnp.where(gy > 0, low[0:16], 0.0)
    ez_high = jnp.where(gy < GY - 1, high, 0.0)
    srcs = (own, s1, s2, s3)
    tile = iota((8, NZ), 1) >> 5
    codes = jnp.concatenate(
        [jnp.where(tile == k, ref[Y_CODE:Y_CODE + 8, :], 0.0) for k in range(4) for ref in srcs], axis=0).astype(BF16)
    inj = None
    for r in range(2):
        lane = ((iota((8, 128), 1) & 31) == r * GY + gy).astype(BF16)
        code_row = lax.dot_general(lane, codes, (((1,), (1,)), ((), ())), preferred_element_type=F32)[0:1]
        land = ((iota((CELLS, 128), 0) + 1).astype(F32) == code_row).astype(BF16)
        vals = jnp.concatenate(
            [ref[(k * 2 + r) * 8:(k * 2 + r) * 8 + 8, :] for k in range(4) for ref in srcs], axis=0)
        part = split_dot(land, vals)
        inj = part if inj is None else inj + part
    inj_o[...] = inj
    dz_o[...] = dz0[...] - INV * inj
    dz_o[strided(0), :] = dz_o[strided(0), :] + INV * hx_low
    c_h = -HS * ez_high
    c_e = z_apply(INV * (c_h - z_down(c_h)), zf, strided(CY - 1))
    c_d = HS * (z_up(c_e) - c_e)
    c_1 = c_h + c_d
    b_e = z_apply(INV * hz_low[...], zf, rows(0))
    b_d = HS * (z_up(b_e) - b_e)
    hxpp_o[...] = hxpp0[...]
    hxpp_o[rows(0), :] = hxpp_o[rows(0), :] + (b_d + b_d)
    hxpp_o[strided(CY - 1), :] = hxpp_o[strided(CY - 1), :] + (c_1 + c_d)
    prev = None
    for x in range(CX):
        ex1 = ex1_o[rows(x), :]
        dex1 = HS * (y_up(ex1, right[x:x + 1]) - ex1)
        hz1 = hzp[rows(x), :] + dex1
        hz1_o[rows(x), :] = hz1
        hzpp = hz1 + dex1
        hzpp_o[rows(x), :] = hzpp
        curl = prev - hzpp if x > 0 else -hzpp
        prev = hzpp
        dy2_o[rows(x), :] = dy20[rows(x), :] + INV * curl
    dy2_o[rows(0), :] = dy2_o[rows(0), :] + v[rows(0), :] * b_e + INV * (b_d - z_down(b_d))
    dy2_o[strided(CY - 1), :] = dy2_o[strided(CY - 1), :] + v[strided(CY - 1), :] * c_e + INV * (c_1 - z_down(c_1))
    fwd = [fx[x] for x in range(CX)]
    bwd = [bx[x] for x in range(CX)]
    tz = -INV * hyp[rows(CX - 1), :]
    p1, p2 = ends([dz_o[rows(x), :] for x in range(CX)], fwd, bwd)
    ty = INV * hzpp_o[rows(CX - 1), :]
    q1, q2 = ends([dy2_o[rows(x), :] for x in range(CX)], fwd, bwd)
    for f, face in enumerate((p1, p2 + tz, q1, q2 + ty, tz)):
        msg[16 * f:16 * f + 16, :] = face


def k3b(own, rc, h0, hr0, be0, de0, hs_c, hrs_c, bes, des, mz1, mz2, mz3):
    gx = lax.axis_index("gx")
    c = gx & 1
    z = gx >> 1
    terms = []
    for f in range(2):
        blocks = []
        for k in range(2):
            q1 = jnp.where(c == k, own[32 * f:32 * f + 16, :], rc[32 * f:32 * f + 16, :])
            q2 = jnp.where(c == k, own[32 * f + 16:32 * f + 32, :], rc[32 * f + 16:32 * f + 32, :])
            blocks.append(pair_terms(k, q1, q2, h0, hr0, be0, de0))
        last = blocks[1][0] + h0[1] * blocks[0][0]
        first = blocks[0][1] + hr0[0] * blocks[1][1]
        terms.append(pair_terms(z, first, last, hs_c, hrs_c, bes, des))
    for d, ref in enumerate((mz1, mz2, mz3), 1):
        up = ((z + d) & 3) > z
        for f in range(2):
            ref[16 * f:16 * f + 16, :] = jnp.where(up, terms[f][0], terms[f][1])
    mz1[32:48, :] = jnp.where(c == 1, own[64:80, :], rc[64:80, :])


def x_interface(f, own, rc, zs, hs_c, hrs_c, hg_c, hrg_c, beg, deg, buf):
    gx = lax.axis_index("gx")
    c = gx & 1
    z = gx >> 1
    place(buf, z, zs[0][16 * f:16 * f + 16, :], [r[16 * f:16 * f + 16, :] for r in zs])
    al, ga = incoming(4, z, lambda k: buf[k], hs_c, hrs_c)
    own_m, own_n = pair_terms(c, own[32 * f:32 * f + 16, :], own[32 * f + 16:32 * f + 32, :], hg_c, hrg_c, beg, deg)
    other = pair_terms(1 - c, rc[32 * f:32 * f + 16, :], rc[32 * f + 16:32 * f + 32, :], hg_c, hrg_c, beg, deg)
    return interface(2, c, own_m, own_n, lambda k: other[k], hg_c, hrg_c, beg, deg, al, ga)


def k4(own, rc, z1, z2, z3, hxs, hrxs, hxg, hrxg, bexg, dexg, v, dz, fx, fy, by, hyp, hxpp, inj,
       h0, hr0, be0, de0, hs_c, hrs_c, bes, des, hg_c, hrg_c, beg, deg, tr, msg, dz2_o, hypp_o, own_o, buf):
    gx = lax.axis_index("gx")
    at = lax.axis_index("gy") & 3
    me = lax.axis_index("gy") >> 2
    left, right = x_interface(0, own, rc, (z1, z2, z3), hxs, hrxs, hxg, hrxg, bexg, dexg, buf)
    us = block_solve([dz[rows(x), :] for x in range(CX)], [fx[x] for x in range(CX)], left, right)
    t = jnp.where((gx & 1) == 1, rc[64:80, :], z1[32:48, :])
    prev = jnp.where(gx > 0, HS * (us[0] - left) - 240.0 * t, 0.0)
    for x in range(CX):
        dez = HS * ((us[x + 1] if x < CX - 1 else right) - us[x])
        hy1 = hyp[rows(x), :] + dez
        hypp_o[rows(x), :] = hy1 + dez
        hx2 = hxpp[rows(x), :]
        curl = (hy1 - prev) - (hx2 - y_down(hx2, 0.0)) - inj[rows(x), :]
        prev = hy1
        dz2_o[rows(x), :] = v[rows(x), :] * us[x] + INV * curl
    p1, p2 = ends([dz2_o[strided(y), :] for y in range(CY)], [fy[y] for y in range(CY)], [by[y] for y in range(CY)])
    p2 = p2 + INV * hxpp[strided(CY - 1), :]
    m, n = pair_terms(at, p1, p2, hg_c, hrg_c, beg, deg)
    own_o[0], own_o[1] = m, n
    m0, n0 = pair_terms(at, p1, p2, h0, hr0, be0, de0)
    m0, n0 = tr[0] * m0, tr[1] * n0
    group_m, group_n = pair_terms(me, n0, m0, hs_c, hrs_c, bes, des)
    for d in range(GY):
        y, x = d // 4, d % 4
        msg[d] = jnp.where(y > me, group_m, jnp.where(y < me, group_n, jnp.where(x > at, m, n)))


def k4b(own, rc, z1, z2, z3, hxs, hrxs, hxg, hrxg, bexg, dexg, v, w, fx, ex1, hz1, hz1m, hypp, hzpp, dy2,
        e_o, h_o, ex2_s, ey2_s, hy2_s, hz2_s, dx2_s, buf, sem):
    left, right = x_interface(1, own, rc, (z1, z2, z3), hxs, hrxs, hxg, hrxg, bexg, dexg, buf)
    us = block_solve([dy2[rows(x), :] for x in range(CX)], [fx[x] for x in range(CX)], left, right)
    for x in range(CX):
        ey2_s[rows(x), :] = us[x]
        hz2_s[rows(x), :] = hzpp[rows(x), :] - HS * ((us[x + 1] if x < CX - 1 else right) - us[x])
        hz = hz1[rows(x), :]
        hy = hypp[rows(x), :]
        curl = (hz - y_down(hz, hz1m[x:x + 1, :])) - (hy - z_down(hy))
        dx2_s[rows(x), :] = v[rows(x), :] * ex1[rows(x), :] + INV * curl
    copies = [pltpu.make_async_copy(ey2_s, e_o.at[1], sem.at[0]), pltpu.make_async_copy(hz2_s, h_o.at[2], sem.at[1]),
              pltpu.make_async_copy(ex2_s, e_o.at[0], sem.at[2]), pltpu.make_async_copy(hy2_s, h_o.at[1], sem.at[3])]
    copies[0].start()
    copies[1].start()
    for q in range(4):
        part = pl.ds(q * 64, 64)
        ex2 = z_solve(w[part, :], dx2_s[part, :])
        ex2_s[part, :] = ex2
        hy2_s[part, :] = hypp[part, :] - HS * (z_up(ex2) - ex2)
    copies[2].start()
    copies[3].start()
    for copy in copies:
        copy.wait()


def k5(m4, own, dz2, fy, hxpp, hs_c, hrs_c, hg_c, hrg_c, beg, deg, e_in, h_in, e_o, h_o, ez2_s, hx2_s, sem):
    at = lax.axis_index("gy") & 3
    me = lax.axis_index("gy") >> 2
    al, ga = incoming(4, me, lambda k: m4[4 * k] + m4[4 * k + 1] + m4[4 * k + 2] + m4[4 * k + 3], hs_c, hrs_c)
    left, right = interface(4, at, own[0], own[1], lambda k: m4[4 * me + k], hg_c, hrg_c, beg, deg, al, ga)
    us = block_solve([dz2[strided(y), :] for y in range(CY)], [fy[y] for y in range(CY)], left, right)
    for y in range(CY):
        ez2_s[strided(y), :] = us[y]
    first = pltpu.make_async_copy(ez2_s, e_o.at[2], sem.at[0])
    first.start()
    for x in range(CX):
        ez2 = ez2_s[rows(x), :]
        hx2_s[rows(x), :] = hxpp[rows(x), :] - HS * (y_up(ez2, right[x:x + 1]) - ez2)
    second = pltpu.make_async_copy(hx2_s, h_o.at[0], sem.at[1])
    second.start()
    first.wait()
    second.wait()


def call(kernel, shapes, args, scratch=(), hbm_in=(), hbm_out=(), alias=None):
    def spec(in_hbm):
        return pl.BlockSpec(memory_space=pltpu.HBM if in_hbm else pltpu.VMEM)
    return pl.pallas_call(
        kernel,
        out_shape=[jax.ShapeDtypeStruct(s, F32) for s in shapes],
        in_specs=[spec(k in hbm_in) for k in range(len(args))],
        out_specs=[spec(k in hbm_out) for k in range(len(shapes))],
        scratch_shapes=[pltpu.VMEM(s, F32) if isinstance(s, tuple) else s for s in scratch],
        input_output_aliases=alias or {},
        compiler_params=pltpu.CompilerParams(vmem_limit_bytes=12 << 20),
        name=kernel.__name__,
    )(*args)


def pair(message):
    return lax.ppermute(message, "gx", [(x, x ^ 1) for x in range(GX)])


def ring_z(message, d):
    pairs = [(2 * z + c, 2 * ((z + d) % 4) + c) for z in range(4) for c in range(2)]
    return lax.ppermute(message, "gx", pairs)


def ring_x(message, d):
    pairs = [(4 * y + x, 4 * y + (x + d) % 4) for y in range(4) for x in range(4)]
    return lax.ppermute(message, "gy", pairs)


def ring_y(message, d):
    pairs = [(4 * y + x, 4 * ((y + d) % 4) + x) for y in range(4) for x in range(4)]
    return lax.ppermute(message, "gy", pairs)


def exchange(message, axis):
    return lax.all_to_all(message, axis, split_axis=0, concat_axis=0, tiled=True)


FIELD = (CELLS, NZ)
FACE = (16, NZ)
LINE = (16, 16, NZ)


def body(e_fields, h_fields, material, permittivity, conductivity, electrode_cells, electrode_dest,
         target_cells, electrode_gain):
    e = e_fields.reshape(3, CELLS, NZ)
    h = h_fields.reshape(3, CELLS, NZ)
    mat = material.reshape(CELLS, NZ)
    row = (1, 128)
    dma = pltpu.SemaphoreType.DMA
    hbm = [pltpu.with_memory_space_constraint(a, pltpu.HBM) for a in (
        e, h, mat, permittivity, conductivity, electrode_cells.reshape(row),
        electrode_dest.reshape(row), target_cells.reshape(row), electrode_gain.reshape(row))]
    msg1, w, v, fx, bx, e, h = call(
        k1, [(C_ALL, NZ), FIELD, FIELD, LINE, LINE, (3,) + FIELD, (3,) + FIELD],
        hbm,
        scratch=[FIELD, FACE, FACE, pltpu.VMEM(FIELD, jnp.int32), pltpu.SMEM((8,), F32), pltpu.SMEM((8,), F32),
                 pltpu.VMEM(row, jnp.int32), pltpu.VMEM(row, jnp.int32), pltpu.VMEM(row, jnp.int32), row, dma((12,))],
        hbm_in=range(9))
    chain2 = [(2,) + FACE, (2,) + FACE, (3,) + FACE, (3,) + FACE]
    chain = [(4,) + FACE, (4,) + FACE, (5,) + FACE, (5,) + FACE]
    rc = pair(msg1)
    out = call(k1c, [(Z_HALO + Z_ROWS[d], NZ) for d in (1, 2, 3)] + [(Z_HALO, NZ), (2, 48, NZ)] + chain2, (msg1, rc))
    msgz, ownz, blkx, pstat = out[:3], out[3], out[4], out[5:]
    msgz, w1 = lax.optimization_barrier((msgz, w))
    rz = [ring_z(m, d) for d, m in enumerate(msgz, 1)]
    fy, by, g = call(k1b, [LINE, LINE, (3,) + FACE], (w1,))
    out = call(
        k2, [(X_HALO + HALO[d], NZ) for d in (1, 2, 3)] + [
            (X_HALO, NZ), FIELD, FIELD, FACE] + chain + chain2,
        (rc, ownz, *rz, blkx, e, h, v, fy, by, g), scratch=[(4, 64, NZ), FIELD, (8, NZ), (4, 48, NZ)])
    msgx, (ownx, hzp, dx, hz_low), xsup, xgrp = out[:3], out[3:7], out[7:11], out[11:]
    msgx, w2 = lax.optimization_barrier((msgx, w))
    rx = [ring_x(m, d) for d, m in enumerate(msgx, 1)]
    hyp, dz0, hxp, dy1, zf = call(k2a, [FIELD] * 4 + [(15,) + FIELD], (e, h, w2, v))
    out = call(
        k2c, [(Y_HALO + HALO[d], NZ) for d in (1, 2, 3)] + [(Y_HALO, NZ), (4, 80, NZ)] + chain, (ownx, *rx))
    msgy, owny, blk, zstat = out[:3], out[3], out[4], out[5:]
    msgy, zf1 = lax.optimization_barrier((msgy, zf))
    ry = [ring_y(m, d) for d, m in enumerate(msgy, 1)]
    hxpp0, dy20 = call(k2b, [FIELD, FIELD], (v, hxp, dy1, zf1), scratch=[FIELD])
    out = call(
        k3, [(80, NZ)] + chain + chain + [(2,) + FACE, FIELD, FIELD, FACE, FIELD, FIELD, FIELD, FIELD, FIELD],
        (owny, *ry, rx[0], rx[2], blk, zstat[0], zstat[1], v, hzp, dx, fy, fx, bx, hz_low,
         hyp, dz0, hxpp0, dy20, zf), scratch=[(4, 80, NZ)])
    msg3, sstat, gstat, tr = out[0], out[1:5], out[5:9], out[9]
    ex1, hz1, hz1m, inj, hxpp, hzpp, dz, dy2 = out[10:]
    rc3 = pair(msg3)
    msgz3 = call(k3b, [(48, NZ), (32, NZ), (32, NZ)], (msg3, rc3, *pstat, *xsup))
    got3 = (msg3, rc3, *[ring_z(m, d) for d, m in enumerate(msgz3, 1)], xsup[0], xsup[1], *xgrp)
    msg4, dz2, hypp, own2 = call(
        k4, [(GY, R4, NZ), FIELD, FIELD, (2,) + FACE],
        (*got3, v, dz, fx, fy, by, hyp, hxpp, inj, *zstat, *sstat, *gstat, tr), scratch=[(4,) + FACE])
    m4 = exchange(msg4, "gy")
    e_out, h_out = call(
        k4b, [(3,) + FIELD, (3,) + FIELD], (*got3, v, w, fx, ex1, hz1, hz1m, hypp, hzpp, dy2),
        scratch=[FIELD] * 5 + [(4,) + FACE, dma((4,))], hbm_out=(0, 1))
    e_out, h_out = call(
        k5, [(3,) + FIELD, (3,) + FIELD], (m4, own2, dz2, fy, hxpp, sstat[0], sstat[1], *gstat, e_out, h_out),
        scratch=[FIELD, FIELD, dma((2,))], hbm_in=(11, 12), hbm_out=(0, 1), alias={11: 0, 12: 1})
    return e_out.reshape(3, CX, CY, NZ), h_out.reshape(3, CX, CY, NZ)


def solution(mesh):
    in_specs = (
        P(None, "gx", "gy", None),
        P(None, "gx", "gy", None),
        P("gx", "gy", None),
        P(),
        P(),
        P(("gx", "gy")),
        P(("gx", "gy"), None),
        P(("gx", "gy")),
        P(("gx", "gy")),
    )
    out_specs = (P(None, "gx", "gy", None), P(None, "gx", "gy", None))
    return jax.shard_map(body, mesh=mesh, in_specs=in_specs, out_specs=out_specs, check_vma=False)
```
